32 devices in a mesh: dp: 4 (over y, x), seq: 8 (over z, core).
Axes of the slice: x: 2, y: 2, z: 4, core: 2. Of those that a mesh axis runs over, the one named last changes fastest.
Arguments:
- residual_in: bfloat16 [4, 1024, 2048], P('dp', 'seq'), may hold values from -6 to 6
- attn_gain: bfloat16 [2048], P(('dp', 'seq')), may hold values from 0.099609375 to 1.8984375
- attn_shift: bfloat16 [2048], P(('dp', 'seq')), may hold values from -3 to 3
- qkv_weight: bfloat16 [2048, 6144], P(('dp', 'seq')), may hold values from -0.125 to 0.125
- qkv_bias: bfloat16 [6144], P(('dp', 'seq')), may hold values from -3 to 3
- out_weight: bfloat16 [2048, 2048], P(('dp', 'seq')), may hold values from -1 to 1
- ffn_gain: bfloat16 [2048], P(('dp', 'seq')), may hold values from 0.099609375 to 1.8984375
- ffn_shift: bfloat16 [2048], P(('dp', 'seq')), may hold values from -3 to 3
- gate_weight: bfloat16 [2048, 5632], P(('dp', 'seq')), may hold values from -0.125 to 0.125
- up_weight: bfloat16 [2048, 5632], P(('dp', 'seq')), may hold values from -0.125 to 0.125
- down_weight: bfloat16 [2048, 5632], P(('dp', 'seq')), may hold values from -0.078125 to 0.078125
- positions: int32 [4, 1024], P('dp', 'seq'), may hold values from 0 to 511, as said below
- cotangent: bfloat16 [4, 1024, 2048], P('dp', 'seq'), may hold values from -6 to 6
Outputs:
- residual_out: bfloat16 [4, 1024, 2048], P('dp', 'seq')
- grad_residual_in: float32 [4, 1024, 2048], P('dp', 'seq')
- grad_attn_gain: float32 [2048], P(('dp', 'seq'))
- grad_attn_shift: float32 [2048], P(('dp', 'seq'))
- grad_qkv_weight: float32 [2048, 6144], P(('dp', 'seq'))
- grad_qkv_bias: float32 [6144], P(('dp', 'seq'))
- grad_out_weight: float32 [2048, 2048], P(('dp', 'seq'))
- grad_ffn_gain: float32 [2048], P(('dp', 'seq'))
- grad_ffn_shift: float32 [2048], P(('dp', 'seq'))
- grad_gate_weight: float32 [2048, 5632], P(('dp', 'seq'))
- grad_up_weight: float32 [2048, 5632], P(('dp', 'seq'))
- grad_down_weight: float32 [2048, 5632], P(('dp', 'seq'))
The draws below stay inside these ranges and needn't reach their ends.
Inputs may be any that keep to these rules, and one draw needn't show every extreme that they name: `positions`: positions count from the start of each token's document and restart at 0 where a document begins; the first token of a sequence has position 0; a sequence holds at most four documents, one of exactly 512 tokens.
All inputs are finite; a program needn't handle non-finite values.
Results may differ from the reference program's by a relative error of at most 0.015.
Values may be sent and summed in bfloat16 or wider, within the bound.
No kernel may reach another device: no remote copies, remote signals or barrier semaphores. Data moves between devices by JAX's collectives and lax.ppermute only.
A program may use at most 192 MiB of HBM per device.

```python
import jax
import jax.numpy as jnp
from jax import lax

D = 2048
HEADS = 32
HD = 64
FF = 5632
ROT = 16
SEQ_LEN = 1024
BATCH = 4


def draw_positions(key, part):
    half = SEQ_LEN // 2

    def one_sequence(stream_key):
        first, second = jax.random.split(stream_key, 2)
        cuts = jax.random.randint(first, (2,), 1, half)
        low = jnp.min(cuts)
        high = jnp.max(cuts)
        others = jnp.stack([low, high - low, half - high]).astype(jnp.int32)
        longest = jax.random.randint(second, (), 0, 4)
        slots = jnp.arange(4, dtype=jnp.int32)
        order = jnp.clip(slots - (slots > longest).astype(jnp.int32), 0, 2)
        lengths = jnp.where(slots == longest, half, others[order]).astype(jnp.int32)
        begins = jnp.cumsum(lengths) - lengths
        tokens = jnp.arange(SEQ_LEN, dtype=jnp.int32)
        start_of = jnp.max(jnp.where(begins[None, :] <= tokens[:, None], begins[None, :], 0), axis=1)
        return (tokens - start_of).astype(jnp.int32)
    sequence_keys = jax.random.split(jax.random.fold_in(key, 11), BATCH)
    return jax.vmap(one_sequence)(sequence_keys)


def block_levels(own_key, shape, pieces, least, high):
    factor_of = 1.0
    for axis_at, parts in pieces:
        draws = jax.random.uniform(jax.random.fold_in(jax.random.fold_in(own_key, 6), axis_at), (parts,), jnp.float32, least / len(pieces), high / len(pieces))
        factor_of = factor_of * jnp.repeat(jnp.exp(draws), shape[axis_at] // parts).reshape((-1,) + (1,) * (len(shape) - 1 - axis_at))
    return factor_of


def bell_draw(rng, shape, width, most, cuts=(), held_as=jnp.bfloat16):
    result = width * jax.random.normal(rng, shape, jnp.float32)
    if cuts:
        result = result * block_levels(rng, shape, cuts, -0.22, 0.18)
    return jnp.clip(result, -most, most).astype(held_as)


def setup_inputs(seed: int = 0) -> dict:
    seeds = jax.random.split(jax.random.key(seed), 14)
    residual_in = bell_draw(seeds[0], (BATCH, SEQ_LEN, D), 1.0, 6.0, ((0, 4), (1, 8)))
    attn_gain = jnp.clip(1.0 + 0.18 * jax.random.normal(seeds[1], (D,), jnp.float32), 0.099609375, 1.8984375).astype(jnp.bfloat16)
    attn_shift = bell_draw(seeds[2], (D,), 0.5, 3.0, ((0, 32),))
    qkv_weight = bell_draw(seeds[3], (D, 3 * D), D ** -0.5, 0.125, ((0, 32),))
    qkv_bias = bell_draw(seeds[4], (3 * D,), 0.5, 3.0, ((0, 32),))
    out_weight = bell_draw(seeds[5], (D, D), (D // 64) ** -0.5, 1.0, ((0, 32),))
    ffn_gain = jnp.clip(1.0 + 0.18 * jax.random.normal(seeds[6], (D,), jnp.float32), 0.099609375, 1.8984375).astype(jnp.bfloat16)
    ffn_shift = bell_draw(seeds[7], (D,), 0.5, 3.0, ((0, 32),))
    gate_weight = bell_draw(seeds[8], (D, FF), D ** -0.5, 0.125, ((0, 32),))
    up_weight = bell_draw(seeds[9], (D, FF), D ** -0.5, 0.125, ((0, 32),))
    down_weight = bell_draw(seeds[10], (D, FF), FF ** -0.5, 0.078125, ((0, 32),))
    positions = draw_positions(jax.random.fold_in(seeds[13], 71), 0)
    cotangent = bell_draw(seeds[12], (BATCH, SEQ_LEN, D), 1.0, 6.0, ((0, 4), (1, 8)))
    return dict(residual_in=residual_in, attn_gain=attn_gain, attn_shift=attn_shift, qkv_weight=qkv_weight, qkv_bias=qkv_bias, out_weight=out_weight, ffn_gain=ffn_gain, ffn_shift=ffn_shift, gate_weight=gate_weight, up_weight=up_weight, down_weight=down_weight, positions=positions, cotangent=cotangent)


EPSILON = 1e-05
ROPE_BASE = 10000.0
MASKED = -1e+30

def rotary_tables(position):
    half = ROT // 2
    exponent = jnp.arange(half, dtype=jnp.float32) * (2.0 / ROT)
    angles = position.astype(jnp.float32)[:, None] * (ROPE_BASE ** (-exponent))[None, :]
    return (jnp.cos(angles)[:, None, :], jnp.sin(angles)[:, None, :])

def rotate(field, cosine, sine):
    half = ROT // 2
    first = field[..., :half]
    second = field[..., half:ROT]
    return jnp.concatenate([first * cosine - second * sine, second * cosine + first * sine, field[..., ROT:]], axis=-1)

def unrotate(field, cosine, sine):
    half = ROT // 2
    first = field[..., :half]
    second = field[..., half:ROT]
    return jnp.concatenate([first * cosine + second * sine, second * cosine - first * sine, field[..., ROT:]], axis=-1)

def normalize(values, gain, shift):
    center = values - lax.optimization_barrier(jnp.mean(values, axis=-1, keepdims=True))
    factor = lax.rsqrt(lax.optimization_barrier(jnp.mean(center * center, axis=-1, keepdims=True)) + EPSILON)
    unit = center * factor
    return (unit * gain.astype(jnp.float32) + shift.astype(jnp.float32), unit, factor)

def norm_back(upstream, unit, factor, gain):
    scaled = upstream * gain.astype(jnp.float32)
    return factor * (scaled - lax.optimization_barrier(jnp.mean(scaled, axis=-1, keepdims=True)) - unit * lax.optimization_barrier(jnp.mean(scaled * unit, axis=-1, keepdims=True)))

def product(left, right):
    return jnp.dot(left, right, preferred_element_type=jnp.float32)

def sequence_pass(params, inputs, position, upstream):
    attn_gain, attn_shift, qkv_weight, qkv_bias, out_weight, ffn_gain, ffn_shift, gate_weight, up_weight, down_weight = params
    qblock = min(512, SEQ_LEN)
    count = SEQ_LEN // qblock
    starts = jnp.arange(count, dtype=jnp.int32) * qblock
    columns = jnp.arange(SEQ_LEN, dtype=jnp.int32)
    lowest_all = columns - position.astype(jnp.int32)
    flat = inputs.astype(jnp.float32)
    normed_one, unit_one, factor_one = normalize(flat, attn_gain, attn_shift)
    normed_one = normed_one.astype(jnp.bfloat16)
    projected = product(normed_one, qkv_weight) + qkv_bias.astype(jnp.float32)
    cosine, sine = rotary_tables(position)
    query = rotate(projected[:, :D].reshape(SEQ_LEN, HEADS, HD), cosine, sine).astype(jnp.bfloat16)
    key = rotate(projected[:, D:2 * D].reshape(SEQ_LEN, HEADS, HD), cosine, sine).astype(jnp.bfloat16)
    value = projected[:, 2 * D:].reshape(SEQ_LEN, HEADS, HD).astype(jnp.bfloat16)
    key_float = key.astype(jnp.float32)
    value_float = value.astype(jnp.float32)

    def scores_of(start):
        rows = start + jnp.arange(qblock, dtype=jnp.int32)
        lowest = lax.dynamic_slice_in_dim(lowest_all, start, qblock, 0)
        piece = lax.dynamic_slice_in_dim(query, start, qblock, 0).astype(jnp.float32)
        scores = jnp.einsum('qhd,khd->hqk', piece, key_float) * 0.125
        visible = ((columns[None, :] <= rows[:, None]) & (columns[None, :] >= lowest[:, None]))[None]
        return (jnp.where(visible, scores, MASKED), visible, piece)

    def forward_block(start):
        masked, visible, piece = scores_of(start)
        top = lax.optimization_barrier(jnp.max(masked, axis=-1, keepdims=True))
        total = lax.optimization_barrier(jnp.sum(jnp.where(visible, jnp.exp(masked - top), 0.0), axis=-1))
        log_total = top[..., 0] + jnp.log(total)
        attend = jnp.where(visible, jnp.exp(masked - log_total[..., None]), 0.0).astype(jnp.bfloat16)
        context = jnp.einsum('hqk,khd->qhd', attend.astype(jnp.float32), value_float).astype(jnp.bfloat16)
        return (context, log_total)
    contexts, logs = lax.map(forward_block, starts)
    context = contexts.reshape(SEQ_LEN, D)
    middle = flat + product(context, out_weight.T)
    normed_two, unit_two, factor_two = normalize(middle, ffn_gain, ffn_shift)
    normed_two = normed_two.astype(jnp.bfloat16)
    gate = product(normed_two, gate_weight)
    upward = product(normed_two, up_weight)
    sigmoid_gate = jax.nn.sigmoid(gate)
    silu_gate = gate * sigmoid_gate
    hidden = (silu_gate * upward).astype(jnp.bfloat16)
    output = (middle + product(hidden, down_weight.T)).astype(jnp.bfloat16)
    grad_down = product(upstream.T, hidden)
    grad_hidden = product(upstream, down_weight)
    grad_gate = (grad_hidden * upward * sigmoid_gate * (1.0 + gate * (1.0 - sigmoid_gate))).astype(jnp.bfloat16)
    grad_up = (grad_hidden * silu_gate).astype(jnp.bfloat16)
    grad_gate_weight = product(normed_two.T, grad_gate)
    grad_up_weight = product(normed_two.T, grad_up)
    grad_normed_two = product(grad_gate, gate_weight.T) + product(grad_up, up_weight.T)
    grad_ffn_gain = lax.optimization_barrier(jnp.sum(grad_normed_two * unit_two, axis=0))
    grad_ffn_shift = lax.optimization_barrier(jnp.sum(grad_normed_two, axis=0))
    grad_middle = upstream.astype(jnp.float32) + norm_back(grad_normed_two, unit_two, factor_two, ffn_gain)
    grad_mixed = grad_middle.astype(jnp.bfloat16)
    grad_out_weight = product(grad_mixed.T, context)
    grad_context = product(grad_mixed, out_weight).astype(jnp.bfloat16).reshape(SEQ_LEN, HEADS, HD)
    grad_context_float = grad_context.astype(jnp.float32)
    delta = lax.optimization_barrier(jnp.sum(grad_context_float * context.reshape(SEQ_LEN, HEADS, HD).astype(jnp.float32), axis=-1))

    def backward_block(carry, items):
        grad_keys, grad_values = carry
        start, log_total = items
        masked, visible, piece = scores_of(start)
        attend = jnp.where(visible, jnp.exp(masked - log_total[..., None]), 0.0)
        attend_half = attend.astype(jnp.bfloat16).astype(jnp.float32)
        grad_piece = lax.dynamic_slice_in_dim(grad_context_float, start, qblock, 0)
        delta_piece = lax.dynamic_slice_in_dim(delta, start, qblock, 0).T
        grad_values = grad_values + jnp.einsum('hqk,qhd->khd', attend_half, grad_piece)
        grad_prob = jnp.einsum('qhd,khd->hqk', grad_piece, value_float)
        grad_score = (attend * (grad_prob - delta_piece[..., None]) * 0.125).astype(jnp.bfloat16).astype(jnp.float32)
        grad_keys = grad_keys + jnp.einsum('hqk,qhd->khd', grad_score, piece)
        grad_query = jnp.einsum('hqk,khd->qhd', grad_score, key_float)
        return ((grad_keys, grad_values), grad_query)
    empty = jnp.zeros((SEQ_LEN, HEADS, HD), jnp.float32)
    (grad_keys, grad_values), grad_queries = lax.scan(backward_block, (empty, empty), (starts, logs))
    grad_queries = grad_queries.reshape(SEQ_LEN, HEADS, HD)
    grad_projected = jnp.concatenate([unrotate(grad_queries, cosine, sine).reshape(SEQ_LEN, D), unrotate(grad_keys, cosine, sine).reshape(SEQ_LEN, D), grad_values.reshape(SEQ_LEN, D)], axis=1)
    grad_qkv_bias = lax.optimization_barrier(jnp.sum(grad_projected, axis=0))
    grad_projected_half = grad_projected.astype(jnp.bfloat16)
    grad_qkv_weight = product(normed_one.T, grad_projected_half)
    grad_normed_one = product(grad_projected_half, qkv_weight.T)
    grad_attn_gain = lax.optimization_barrier(jnp.sum(grad_normed_one * unit_one, axis=0))
    grad_attn_shift = lax.optimization_barrier(jnp.sum(grad_normed_one, axis=0))
    grad_input = grad_middle + norm_back(grad_normed_one, unit_one, factor_one, attn_gain)
    grads = (grad_attn_gain, grad_attn_shift, grad_qkv_weight, grad_qkv_bias, grad_out_weight, grad_ffn_gain, grad_ffn_shift, grad_gate_weight, grad_up_weight, grad_down)
    return (output, grad_input, grads)

def reference(residual_in, attn_gain, attn_shift, qkv_weight, qkv_bias, out_weight, ffn_gain, ffn_shift, gate_weight, up_weight, down_weight, positions, cotangent):
    params = (attn_gain, attn_shift, qkv_weight, qkv_bias, out_weight, ffn_gain, ffn_shift, gate_weight, up_weight, down_weight)
    init = tuple((jnp.zeros(param.shape, jnp.float32) for param in params))

    def one_sequence(carry, items):
        inputs, position, upstream = items
        output, grad_input, grads = sequence_pass(params, inputs, position, upstream)
        return (tuple((total + grad for total, grad in zip(carry, grads))), (output, grad_input))
    sums, (outputs, grad_inputs) = lax.scan(one_sequence, init, (residual_in, positions, cotangent))
    return (outputs, grad_inputs, sums[0], sums[1], sums[2], sums[3], sums[4], sums[5], sums[6], sums[7], sums[8], sums[9])
```

```python
import functools

import jax
import jax.numpy as jnp
from jax import lax
from jax.experimental import pallas as pl
from jax.experimental.pallas import tpu as pltpu
from jax.sharding import PartitionSpec as P

HEADS = 32
HD = 64
ROT = 16
LANES = 128
EPSILON = 1e-05
ROPE_BASE = 10000.0
MASKED = -1e30
BF = jnp.bfloat16
F32 = jnp.float32


def rotary_rows(position):
    lane = jnp.arange(LANES, dtype=jnp.int32) % HD
    half = ROT // 2
    power = ROPE_BASE ** (-(lane % half).astype(F32) * (2.0 / ROT))
    freq = jnp.where(lane < ROT, power, 0.0)
    angle = position.astype(F32)[:, None] * freq[None, :]
    cosine = jnp.cos(angle); sine = jnp.sin(angle)
    first = jnp.where(lane < half, -sine, 0.0)
    second = jnp.where((lane >= half) & (lane < ROT), sine, 0.0)
    return cosine, first, second

def turn(x, cosine, first, second):
    return x * cosine + pltpu.roll(x, LANES - ROT // 2, 1) * first + pltpu.roll(x, ROT // 2, 1) * second

def head_mask(x, h):
    lane = lax.broadcasted_iota(jnp.int32, x.shape, 1)
    return jnp.where((lane >= h * HD) & (lane < (h + 1) * HD), x, jnp.zeros_like(x))

def nt(a, b):
    return lax.dot_general(a, b, (((1,), (1,)), ((), ())), preferred_element_type=F32)

def nn(a, b):
    return lax.dot_general(a, b, (((1,), (0,)), ((), ())), preferred_element_type=F32)

def block_bias(i, j, bq, low_row):
    key = j * bq + lax.broadcasted_iota(jnp.int32, (bq, bq), 0)
    query = i * bq + lax.broadcasted_iota(jnp.int32, (bq, bq), 1)
    return jnp.where((key <= query) & (key >= low_row), 0.0, MASKED)

def fwd_kernel(heads, bq, first_ref, low_ref, cos_ref, s1_ref, s2_ref, proj_ref,
               qkv_ref, ctx_ref, lse_ref, k_s, vt_s, st_s):
    i = pl.program_id(0)
    hc = heads * HD
    c, s1, s2 = cos_ref[...], s1_ref[...], s2_ref[...]
    parts = []
    for base in (0, hc):
        for t in range(hc // LANES):
            x = proj_ref[:, base + t * LANES: base + (t + 1) * LANES]
            parts.append(turn(x, c, s1, s2).astype(BF))
    n = hc // LANES
    q = jnp.concatenate(parts[:n], axis=1) if n > 1 else parts[0]
    k = jnp.concatenate(parts[n:], axis=1) if n > 1 else parts[n]
    v32 = proj_ref[:, 2 * hc:]
    v = v32.astype(BF)
    qkv_ref[:, :hc] = q
    qkv_ref[:, hc:2 * hc] = k
    qkv_ref[:, 2 * hc:] = v
    rows = pl.ds(pl.multiple_of(i * bq, bq), bq)
    k_s[rows, :] = k
    vt_s[:, rows] = v32.T.astype(BF)
    low = low_ref[0:1, :]
    qm = [head_mask(q, h) for h in range(heads)]
    first = first_ref[i]

    def score_step(j, tops):
        kj = k_s[pl.ds(pl.multiple_of(j * bq, bq), bq), :]
        bias = block_bias(i, j, bq, low)
        out = []
        for h in range(heads):
            s = nt(kj, qm[h]) * 0.125 + bias
            st_s[h, pl.ds(pl.multiple_of(j * bq, bq), bq), :] = s
            out.append(jnp.maximum(tops[h], jnp.max(s.reshape(bq // 8, 8, bq), axis=0)))
        return tuple(out)

    tops = lax.fori_loop(first, i + 1, score_step,
                         tuple(jnp.full((8, bq), MASKED, F32) for _ in range(heads)))
    tops = [jnp.max(t, axis=0, keepdims=True) for t in tops]

    def value_step(j, state):
        new = []
        vt = vt_s[:, pl.ds(pl.multiple_of(j * bq, bq), bq)]
        for h in range(heads):
            tot, acc = state[h]
            p = jnp.exp(st_s[h, pl.ds(pl.multiple_of(j * bq, bq), bq), :] - tops[h])
            tot = tot + jnp.sum(p.reshape(bq // 8, 8, bq), axis=0)
            acc = acc + nn(vt[h * HD:(h + 1) * HD, :], p.astype(BF))
            new.append((tot, acc))
        return tuple(new)

    state = lax.fori_loop(first, i + 1, value_step,
                          tuple((jnp.zeros((8, bq), F32), jnp.zeros((HD, bq), F32)) for _ in range(heads)))
    outs = []
    lses = []
    for h in range(heads):
        tot, acc = state[h]
        tot = jnp.sum(tot, axis=0, keepdims=True)
        outs.append(acc / tot)
        lses.append(tops[h] + jnp.log(tot))
    ctx_ref[...] = jnp.concatenate(outs, axis=0).T.astype(BF)
    pad = [jnp.zeros((8 - heads, bq), F32)] if heads < 8 else []
    lse_ref[...] = jnp.concatenate(lses + pad, axis=0)

def attend_fwd(proj, tables, low8, first, heads, bq):
    T = proj.shape[0]; hc = heads * HD
    row = lambda w: pl.BlockSpec((bq, w), lambda i, f: (i, 0))
    return pl.pallas_call(
        functools.partial(fwd_kernel, heads, bq),
        grid_spec=pltpu.PrefetchScalarGridSpec(
            num_scalar_prefetch=1, grid=(T // bq,),
            in_specs=[pl.BlockSpec((8, bq), lambda i, f: (0, i)), row(LANES), row(LANES), row(LANES), row(3 * hc)],
            out_specs=[row(3 * hc), row(hc), pl.BlockSpec((8, bq), lambda i, f: (0, i))],
            scratch_shapes=[pltpu.VMEM((T, hc), BF), pltpu.VMEM((hc, T), BF), pltpu.VMEM((heads, T, bq), F32)]),
        out_shape=[jax.ShapeDtypeStruct((T, 3 * hc), BF), jax.ShapeDtypeStruct((T, hc), BF), jax.ShapeDtypeStruct((8, T), F32)],
        compiler_params=pltpu.CompilerParams(dimension_semantics=("arbitrary",)),
        cost_estimate=pl.CostEstimate(flops=2 * T * T * hc * 2, bytes_accessed=T * hc * 24, transcendentals=T * T * heads // 2),
        name="attend_fwd",
    )(first, low8, *tables, proj)

def bwd_kernel(heads, bq, count, first_ref, low_ref, cos_ref, s1_ref, s2_ref, qkv_ref, ctx_ref, lse_ref, gc_ref,
               gp_ref, bias_ref, dk_s, dv_s, dq_s):
    step = pl.program_id(0)
    i = count - 1 - step
    hc = heads * HD
    rows = pl.ds(pl.multiple_of(i * bq, bq), bq)

    @pl.when(step == 0)
    def _():
        dk_s[...] = jnp.zeros_like(dk_s)
        dv_s[...] = jnp.zeros_like(dv_s)
        bias_ref[...] = jnp.zeros_like(bias_ref)

    low = low_ref[0:1, rows]
    q = qkv_ref[rows, :hc]
    g = gc_ref[rows, :]
    prod = (g.astype(F32) * ctx_ref[rows, :].astype(F32)).T
    deltas = [jnp.sum(prod[h * HD:(h + 1) * HD, :], axis=0, keepdims=True) for h in range(heads)]
    lses = [lse_ref[h:h + 1, rows] for h in range(heads)]
    qm = [head_mask(q, h) for h in range(heads)]
    gm = [head_mask(g, h) for h in range(heads)]
    dq_s[...] = jnp.zeros_like(dq_s)

    @pl.loop(first_ref[i], i + 1)
    def _(j):
        cols = pl.ds(pl.multiple_of(j * bq, bq), bq)
        kj = qkv_ref[cols, hc:2 * hc]
        vj = qkv_ref[cols, 2 * hc:]
        kt = kj.T
        bias = block_bias(i, j, bq, low)
        dk = dk_s[cols, :]
        dv = dv_s[cols, :]
        for h in range(heads):
            s = nt(kj, qm[h]) * 0.125 + bias
            p = jnp.exp(s - lses[h])
            dp = nt(vj, gm[h])
            ds = (p * (dp - deltas[h]) * 0.125).astype(BF)
            dv = dv + nn(p.astype(BF), gm[h])
            dk = dk + nn(ds, qm[h])
            dq_s[h * HD:(h + 1) * HD, :] += nn(kt[h * HD:(h + 1) * HD, :], ds)
        dk_s[cols, :] = dk
        dv_s[cols, :] = dv

    c, s1, s2 = cos_ref[rows, :], s1_ref[rows, :], s2_ref[rows, :]
    dq = dq_s[...].T
    dk = dk_s[rows, :]
    dv = dv_s[rows, :]
    def emit(x, base):
        gp_ref[:, base: base + x.shape[1]] = x.astype(BF)
        bias_ref[:, base: base + x.shape[1]] += jnp.sum(x.reshape(bq // 8, 8, x.shape[1]), axis=0)
    for src, base in ((dq, 0), (dk, hc)):
        for t in range(hc // LANES):
            emit(turn(src[:, t * LANES:(t + 1) * LANES], c, -s1, -s2), base + t * LANES)
    emit(dv, 2 * hc)

def attend_bwd(qkv, ctx, lse, gc, tables, low8, first, heads, bq):
    T = qkv.shape[0]; hc = heads * HD; count = T // bq
    full = lambda r, w: pl.BlockSpec((r, w), lambda i, f: (0, 0))
    return pl.pallas_call(
        functools.partial(bwd_kernel, heads, bq, count),
        grid_spec=pltpu.PrefetchScalarGridSpec(
            num_scalar_prefetch=1, grid=(count,),
            in_specs=[full(8, T), full(T, LANES), full(T, LANES), full(T, LANES), full(T, 3 * hc), full(T, hc), full(8, T), full(T, hc)],
            out_specs=[pl.BlockSpec((bq, 3 * hc), lambda i, f: (count - 1 - i, 0)), full(8, 3 * hc)],
            scratch_shapes=[pltpu.VMEM((T, hc), F32), pltpu.VMEM((T, hc), F32), pltpu.VMEM((hc, bq), F32)]),
        out_shape=[jax.ShapeDtypeStruct((T, 3 * hc), BF), jax.ShapeDtypeStruct((8, 3 * hc), F32)],
        compiler_params=pltpu.CompilerParams(dimension_semantics=("arbitrary",)),
        cost_estimate=pl.CostEstimate(flops=5 * T * T * hc * 2, bytes_accessed=T * hc * 24, transcendentals=T * T * heads // 2),
        name="attend_bwd",
    )(first, low8, *tables, qkv, ctx, lse, gc)


def relate(values, mine, count, axis):
    size = values.shape[axis] // count
    bit = 1
    while bit < count:
        order = [m ^ bit for m in range(count)]
        swapped = jnp.concatenate(
            [lax.slice_in_dim(values, m * size, (m + 1) * size, axis=axis) for m in order], axis=axis
        )
        values = jnp.where((mine & bit) != 0, swapped, values)
        bit *= 2
    return values


def swap_dp(values, bit):
    return lax.ppermute(values, "dp", [(d, d ^ bit) for d in range(lax.axis_size("dp"))])


def dp_bits():
    count = lax.axis_size("dp")
    return [1 << n for n in range(count.bit_length() - 1)]


def spread_half(own, bits):
    pieces = {0: own}
    for bit in bits:
        pieces.update({rel ^ bit: swap_dp(piece, bit) for rel, piece in list(pieces.items())})
    return pieces


def collect_half(pieces, bits):
    for bit in reversed(bits):
        kept = {rel: piece for rel, piece in pieces.items() if not rel & bit}
        for rel, piece in kept.items():
            moved = swap_dp(pieces[rel | bit], bit)
            kept[rel] = (piece.astype(F32) + moved.astype(F32)).astype(BF)
        pieces = kept
    return pieces[0]


def fetch(view):
    groups, rows, cols = view.shape
    mine = lax.all_to_all(view, "seq", split_axis=0, concat_axis=0, tiled=True)
    mine = mine.reshape(groups * rows, cols)
    half = groups * rows // 2
    bits = dp_bits()
    low = spread_half(mine[:half], bits)
    high = spread_half(mine[half:], bits[::-1])
    return jnp.concatenate([p for rel in range(len(low)) for p in (low[rel], high[rel])], axis=0)


def give_back(grad, groups):
    count = lax.axis_size("dp")
    size = grad.shape[0] // count
    half = size // 2
    bits = dp_bits()
    low = collect_half({m: grad[m * size : m * size + half] for m in range(count)}, bits)
    high = collect_half({m: grad[m * size + half : (m + 1) * size] for m in range(count)}, bits[::-1])
    summed = jnp.concatenate([low, high], axis=0).reshape(groups, size // groups, grad.shape[1])
    back = lax.all_to_all(summed, "seq", split_axis=0, concat_axis=0, tiled=True)
    return back.transpose(1, 0, 2)


def unit_of(values):
    center = values - jnp.mean(values, axis=-1, keepdims=True)
    factor = lax.rsqrt(jnp.mean(center * center, axis=-1, keepdims=True) + EPSILON)
    return center * factor, factor


def norm_back(upstream, unit, factor, gain):
    scaled = upstream * gain
    return factor * (
        scaled
        - jnp.mean(scaled, axis=-1, keepdims=True)
        - unit * jnp.mean(scaled * unit, axis=-1, keepdims=True)
    )


def dot(left, right, dims):
    return lax.dot_general(left, right, (dims, ((), ())), preferred_element_type=F32)


NN = ((1,), (0,))
NT = ((1,), (1,))
TN = ((0,), (0,))


def own_rows(partial):
    return lax.psum_scatter(partial.astype(BF), "seq", scatter_dimension=0, tiled=True).astype(F32)


def every(values):
    return lax.all_gather(values, "seq", axis=0, tiled=True)


def layer(
    inputs,
    position,
    upstream,
    attn_gain,
    attn_shift,
    qkv_weight,
    qkv_bias,
    out_weight,
    ffn_gain,
    ffn_shift,
    gate_weight,
    up_weight,
    down_weight,
):
    tokens, width = inputs.shape
    groups = lax.axis_size("seq")
    copies = lax.axis_size("dp")
    me = lax.axis_index("seq")
    mine = lax.axis_index("dp")
    length = tokens * groups
    heads = HEADS // groups
    hc = heads * HD
    rows = qkv_weight.shape[0]
    nbias = qkv_bias.shape[0]
    bq = 256

    own = relate(inputs, mine, copies, 1)
    own_up = relate(upstream, mine, copies, 1)
    x_all = every(own)

    def by_group(weight, parts=1):
        cols = weight.shape[1] // (parts * groups)
        view = weight.reshape(rows, parts, groups, cols).transpose(2, 0, 1, 3)
        return view.reshape(groups, rows, parts * cols)

    weight_qkv = fetch(by_group(qkv_weight, 3))

    small = jnp.concatenate(
        [
            attn_gain,
            attn_shift,
            ffn_gain,
            ffn_shift,
            qkv_bias,
            (position // 256).astype(BF),
            (position % 256).astype(BF),
        ]
    )
    count = small.shape[0]
    table = every(jnp.pad(small, (0, -count % 1024)).reshape(1, -1))[:, :count]
    spot = table[:, 4 * rows + nbias :]
    positions = (
        spot[:, :tokens].astype(jnp.int32) * 256 + spot[:, tokens:].astype(jnp.int32)
    ).reshape(length)
    vectors = table[:, : 4 * rows + nbias]
    everyone = [vectors] + [
        lax.ppermute(vectors, "dp", [(d, d ^ m) for d in range(copies)]) for m in range(1, copies)
    ]
    everyone = jnp.stack(everyone).astype(F32)
    gain_one, shift_one, gain_two, shift_two = [
        everyone[:, :, n * rows : (n + 1) * rows].reshape(1, width) for n in range(4)
    ]
    bias_full = relate(everyone[:, :, 4 * rows :].reshape(-1), mine, copies, 0)
    chosen = (jnp.arange(groups, dtype=jnp.int32) == me).astype(F32)
    bias_mine = jnp.sum(bias_full.reshape(3, groups, hc) * chosen[None, :, None], axis=1).reshape(1, -1)

    tables = rotary_rows(positions)
    lowest = jnp.arange(length, dtype=jnp.int32) - positions
    low8 = jnp.broadcast_to(lowest[None], (8, length))
    first = (jnp.min(lowest.reshape(length // bq, bq), axis=1) // bq).astype(jnp.int32)

    unit_all, unused = unit_of(x_all.astype(F32))
    normed_one = (unit_all * gain_one + shift_one).astype(BF)
    projected = dot(normed_one, weight_qkv, NN) + bias_mine
    qkv, context, lse = attend_fwd(projected, tables, low8, first, heads, bq)
    weight_out = fetch(by_group(out_weight))
    up_all = every(own_up)
    flat = own.astype(F32)
    middle = flat + own_rows(dot(context, weight_out, NT))
    unit_two, factor_two = unit_of(middle)
    normed_two = every((unit_two * gain_two + shift_two).astype(BF))
    weight_gate = fetch(by_group(gate_weight))
    weight_up = fetch(by_group(up_weight))
    weight_down = fetch(by_group(down_weight))
    gate = dot(normed_two, weight_gate, NN)
    upward = dot(normed_two, weight_up, NN)
    sig = jax.nn.sigmoid(gate)
    silu = gate * sig
    hidden = (silu * upward).astype(BF)
    grad_hidden = dot(up_all, weight_down, NN)
    grad_gate = (grad_hidden * upward * sig * (1.0 + gate * (1.0 - sig))).astype(BF)
    grad_up = (grad_hidden * silu).astype(BF)
    grad_normed_two = own_rows(dot(grad_gate, weight_gate, NT) + dot(grad_up, weight_up, NT))
    output = (middle + own_rows(dot(hidden, weight_down, NT))).astype(BF)
    grad_gate_weight = dot(normed_two, grad_gate, TN).astype(BF)
    grad_up_weight = dot(normed_two, grad_up, TN).astype(BF)
    grad_down_weight = dot(up_all, hidden, TN).astype(BF)
    sum_gate = give_back(grad_gate_weight, groups)
    sum_up = give_back(grad_up_weight, groups)
    sum_down = give_back(grad_down_weight, groups)

    grad_middle = own_up.astype(F32) + norm_back(grad_normed_two, unit_two, factor_two, gain_two)
    grad_mixed = every(grad_middle.astype(BF))
    grad_context = dot(grad_mixed, weight_out, NN).astype(BF)
    grad_out_weight = dot(grad_mixed, context, TN).astype(BF)
    sum_out = give_back(grad_out_weight, groups)
    grad_projected, bias_part = attend_bwd(qkv, context, lse, grad_context, tables, low8, first, heads, bq)
    grad_normed_one = own_rows(dot(grad_projected, weight_qkv, NT))
    grad_qkv_weight = dot(normed_one, grad_projected, TN).astype(BF)
    sum_qkv = give_back(grad_qkv_weight, groups)
    unit_one, factor_one = unit_of(flat)
    grad_input = grad_middle + norm_back(grad_normed_one, unit_one, factor_one, gain_one)

    bias_part = jnp.sum(bias_part, axis=0).reshape(3, 1, hc) * chosen[None, :, None]
    bias_part = relate(bias_part.reshape(-1), mine, copies, 0).reshape(copies, groups, nbias)
    parts = [
        jnp.sum(grad_normed_one * unit_one, axis=0),
        jnp.sum(grad_normed_one, axis=0),
        jnp.sum(grad_normed_two * unit_two, axis=0),
        jnp.sum(grad_normed_two, axis=0),
    ]
    parts = jnp.concatenate([p.reshape(copies, groups, rows) for p in parts] + [bias_part], axis=2)
    moved = lax.all_to_all(parts.transpose(1, 0, 2), "seq", split_axis=0, concat_axis=0, tiled=True)
    mixed = jnp.sum(moved, axis=0)
    total = mixed[0]
    for m in range(1, copies):
        total = total + lax.ppermute(mixed[m], "dp", [(d, d ^ m) for d in range(copies)])
    sums = [total[n * rows : (n + 1) * rows] for n in range(4)] + [total[4 * rows :]]

    def wide(value):
        return value.astype(F32).reshape(rows, -1)

    wide_qkv = sum_qkv.reshape(rows, groups, 3, hc).transpose(0, 2, 1, 3)
    return (
        relate(output, mine, copies, 1)[None],
        relate(grad_input, mine, copies, 1)[None],
        sums[0],
        sums[1],
        wide(wide_qkv),
        sums[4],
        wide(sum_out),
        sums[2],
        sums[3],
        wide(sum_gate),
        wide(sum_up),
        wide(sum_down),
    )


def local(
    residual_in,
    attn_gain,
    attn_shift,
    qkv_weight,
    qkv_bias,
    out_weight,
    ffn_gain,
    ffn_shift,
    gate_weight,
    up_weight,
    down_weight,
    positions,
    cotangent,
):
    return layer(
        residual_in[0],
        positions[0],
        cotangent[0],
        attn_gain,
        attn_shift,
        qkv_weight,
        qkv_bias,
        out_weight,
        ffn_gain,
        ffn_shift,
        gate_weight,
        up_weight,
        down_weight,
    )


def solution(mesh):
    both = ("dp", "seq")
    in_specs = (
        P("dp", "seq", None),
        P(both),
        P(both),
        P(both, None),
        P(both),
        P(both, None),
        P(both),
        P(both),
        P(both, None),
        P(both, None),
        P(both, None),
        P("dp", "seq"),
        P("dp", "seq", None),
    )
    out_specs = (
        P("dp", "seq", None),
        P("dp", "seq", None),
        P(both),
        P(both),
        P(both, None),
        P(both),
        P(both, None),
        P(both),
        P(both),
        P(both, None),
        P(both, None),
        P(both, None),
    )
    return jax.shard_map(local, mesh=mesh, in_specs=in_specs, out_specs=out_specs, check_vma=False)
```

```python
import functools

import jax
import jax.numpy as jnp
from jax import lax
from jax.experimental import pallas as pl
from jax.experimental.pallas import tpu as pltpu
from jax.sharding import PartitionSpec as P


HEADS = 32
HD = 64
ROT = 16
LANES = 128
EPSILON = 1e-05
ROPE_BASE = 10000.0
MASKED = -1e30
BF = jnp.bfloat16
F32 = jnp.float32


def rotary_rows(position):
    lane = jnp.arange(LANES, dtype=jnp.int32) % HD
    half = ROT // 2
    power = ROPE_BASE ** (-(lane % half).astype(F32) * (2.0 / ROT))
    freq = jnp.where(lane < ROT, power, 0.0)
    angle = position.astype(F32)[:, None] * freq[None, :]
    cosine = jnp.cos(angle); sine = jnp.sin(angle)
    first = jnp.where(lane < half, -sine, 0.0)
    second = jnp.where((lane >= half) & (lane < ROT), sine, 0.0)
    return cosine, first, second


def turn(x, cosine, first, second):
    return x * cosine + pltpu.roll(x, LANES - ROT // 2, 1) * first + pltpu.roll(x, ROT // 2, 1) * second


def head_mask(x, h):
    lane = lax.broadcasted_iota(jnp.int32, x.shape, 1)
    return jnp.where((lane >= h * HD) & (lane < (h + 1) * HD), x, jnp.zeros_like(x))


def nt(a, b):
    return lax.dot_general(a, b, (((1,), (1,)), ((), ())), preferred_element_type=F32)


def nn(a, b):
    return lax.dot_general(a, b, (((1,), (0,)), ((), ())), preferred_element_type=F32)


def block_bias(i, j, bq, low_row):
    key = j * bq + lax.broadcasted_iota(jnp.int32, (bq, bq), 0)
    query = i * bq + lax.broadcasted_iota(jnp.int32, (bq, bq), 1)
    return jnp.where((key <= query) & (key >= low_row), 0.0, MASKED)


def fwd_kernel(heads, bq, first_ref, low_ref, cos_ref, s1_ref, s2_ref, proj_ref,
               qkv_ref, ctx_ref, lse_ref, k_s, vt_s, st_s):
    i = pl.program_id(0)
    hc = heads * HD
    c, s1, s2 = cos_ref[...], s1_ref[...], s2_ref[...]
    parts = []
    for base in (0, hc):
        for t in range(hc // LANES):
            x = proj_ref[:, base + t * LANES: base + (t + 1) * LANES]
            parts.append(turn(x, c, s1, s2).astype(BF))
    n = hc // LANES
    q = jnp.concatenate(parts[:n], axis=1) if n > 1 else parts[0]
    k = jnp.concatenate(parts[n:], axis=1) if n > 1 else parts[n]
    v32 = proj_ref[:, 2 * hc:]
    v = v32.astype(BF)
    qkv_ref[:, :hc] = q
    qkv_ref[:, hc:2 * hc] = k
    qkv_ref[:, 2 * hc:] = v
    rows = pl.ds(pl.multiple_of(i * bq, bq), bq)
    k_s[rows, :] = k
    vt_s[:, rows] = v32.T.astype(BF)
    low = low_ref[0:1, :]
    qm = [head_mask(q, h) for h in range(heads)]
    first = first_ref[i]

    def score_step(j, tops):
        kj = k_s[pl.ds(pl.multiple_of(j * bq, bq), bq), :]
        bias = block_bias(i, j, bq, low)
        out = []
        for h in range(heads):
            s = nt(kj, qm[h]) * 0.125 + bias
            st_s[h, pl.ds(pl.multiple_of(j * bq, bq), bq), :] = s
            out.append(jnp.maximum(tops[h], jnp.max(s.reshape(bq // 8, 8, bq), axis=0)))
        return tuple(out)

    tops = lax.fori_loop(first, i + 1, score_step,
                         tuple(jnp.full((8, bq), MASKED, F32) for _ in range(heads)))
    tops = [jnp.max(t, axis=0, keepdims=True) for t in tops]

    def value_step(j, state):
        new = []
        vt = vt_s[:, pl.ds(pl.multiple_of(j * bq, bq), bq)]
        for h in range(heads):
            tot, acc = state[h]
            p = jnp.exp(st_s[h, pl.ds(pl.multiple_of(j * bq, bq), bq), :] - tops[h])
            tot = tot + jnp.sum(p.reshape(bq // 8, 8, bq), axis=0)
            acc = acc + nn(vt[h * HD:(h + 1) * HD, :], p.astype(BF))
            new.append((tot, acc))
        return tuple(new)

    state = lax.fori_loop(first, i + 1, value_step,
                          tuple((jnp.zeros((8, bq), F32), jnp.zeros((HD, bq), F32)) for _ in range(heads)))
    outs = []
    lses = []
    for h in range(heads):
        tot, acc = state[h]
        tot = jnp.sum(tot, axis=0, keepdims=True)
        outs.append(acc / tot)
        lses.append(tops[h] + jnp.log(tot))
    ctx_ref[...] = jnp.concatenate(outs, axis=0).T.astype(BF)
    pad = [jnp.zeros((8 - heads, bq), F32)] if heads < 8 else []
    lse_ref[...] = jnp.concatenate(lses + pad, axis=0)


def attend_fwd(proj, tables, low8, first, heads, bq):
    T = proj.shape[0]; hc = heads * HD
    row = lambda w: pl.BlockSpec((bq, w), lambda i, f: (i, 0))
    return pl.pallas_call(
        functools.partial(fwd_kernel, heads, bq),
        grid_spec=pltpu.PrefetchScalarGridSpec(
            num_scalar_prefetch=1, grid=(T // bq,),
            in_specs=[pl.BlockSpec((8, bq), lambda i, f: (0, i)), row(LANES), row(LANES), row(LANES), row(3 * hc)],
            out_specs=[row(3 * hc), row(hc), pl.BlockSpec((8, bq), lambda i, f: (0, i))],
            scratch_shapes=[pltpu.VMEM((T, hc), BF), pltpu.VMEM((hc, T), BF), pltpu.VMEM((heads, T, bq), F32)]),
        out_shape=[jax.ShapeDtypeStruct((T, 3 * hc), BF), jax.ShapeDtypeStruct((T, hc), BF), jax.ShapeDtypeStruct((8, T), F32)],
        compiler_params=pltpu.CompilerParams(dimension_semantics=("arbitrary",)),
        cost_estimate=pl.CostEstimate(flops=2 * T * T * hc * 2, bytes_accessed=T * hc * 24, transcendentals=T * T * heads // 2),
        name="attend_fwd",
    )(first, low8, *tables, proj)


def bwd_kernel(heads, bq, count, first_ref, low_ref, cos_ref, s1_ref, s2_ref, qkv_ref, ctx_ref, lse_ref, gc_ref,
               gp_ref, bias_ref, dk_s, dv_s, dq_s):
    step = pl.program_id(0)
    i = count - 1 - step
    hc = heads * HD
    rows = pl.ds(pl.multiple_of(i * bq, bq), bq)

    @pl.when(step == 0)
    def _():
        dk_s[...] = jnp.zeros_like(dk_s)
        dv_s[...] = jnp.zeros_like(dv_s)
        bias_ref[...] = jnp.zeros_like(bias_ref)

    low = low_ref[0:1, rows]
    q = qkv_ref[rows, :hc]
    g = gc_ref[rows, :]
    prod = (g.astype(F32) * ctx_ref[rows, :].astype(F32)).T
    deltas = [jnp.sum(prod[h * HD:(h + 1) * HD, :], axis=0, keepdims=True) for h in range(heads)]
    lses = [lse_ref[h:h + 1, rows] for h in range(heads)]
    qm = [head_mask(q, h) for h in range(heads)]
    gm = [head_mask(g, h) for h in range(heads)]
    dq_s[...] = jnp.zeros_like(dq_s)

    @pl.loop(first_ref[i], i + 1)
    def _(j):
        cols = pl.ds(pl.multiple_of(j * bq, bq), bq)
        kj = qkv_ref[cols, hc:2 * hc]
        vj = qkv_ref[cols, 2 * hc:]
        kt = kj.T
        bias = block_bias(i, j, bq, low)
        dk = dk_s[cols, :]
        dv = dv_s[cols, :]
        for h in range(heads):
            s = nt(kj, qm[h]) * 0.125 + bias
            p = jnp.exp(s - lses[h])
            dp = nt(vj, gm[h])
            ds = (p * (dp - deltas[h]) * 0.125).astype(BF)
            dv = dv + nn(p.astype(BF), gm[h])
            dk = dk + nn(ds, qm[h])
            dq_s[h * HD:(h + 1) * HD, :] += nn(kt[h * HD:(h + 1) * HD, :], ds)
        dk_s[cols, :] = dk
        dv_s[cols, :] = dv

    c, s1, s2 = cos_ref[rows, :], s1_ref[rows, :], s2_ref[rows, :]
    dq = dq_s[...].T
    dk = dk_s[rows, :]
    dv = dv_s[rows, :]

    def emit(x, base):
        gp_ref[:, base: base + x.shape[1]] = x.astype(BF)
        bias_ref[:, base: base + x.shape[1]] += jnp.sum(x.reshape(bq // 8, 8, x.shape[1]), axis=0)

    for src, base in ((dq, 0), (dk, hc)):
        for t in range(hc // LANES):
            emit(turn(src[:, t * LANES:(t + 1) * LANES], c, -s1, -s2), base + t * LANES)
    emit(dv, 2 * hc)


def attend_bwd(qkv, ctx, lse, gc, tables, low8, first, heads, bq):
    T = qkv.shape[0]; hc = heads * HD; count = T // bq
    full = lambda r, w: pl.BlockSpec((r, w), lambda i, f: (0, 0))
    return pl.pallas_call(
        functools.partial(bwd_kernel, heads, bq, count),
        grid_spec=pltpu.PrefetchScalarGridSpec(
            num_scalar_prefetch=1, grid=(count,),
            in_specs=[full(8, T), full(T, LANES), full(T, LANES), full(T, LANES), full(T, 3 * hc), full(T, hc), full(8, T), full(T, hc)],
            out_specs=[pl.BlockSpec((bq, 3 * hc), lambda i, f: (count - 1 - i, 0)), full(8, 3 * hc)],
            scratch_shapes=[pltpu.VMEM((T, hc), F32), pltpu.VMEM((T, hc), F32), pltpu.VMEM((hc, bq), F32)]),
        out_shape=[jax.ShapeDtypeStruct((T, 3 * hc), BF), jax.ShapeDtypeStruct((8, 3 * hc), F32)],
        compiler_params=pltpu.CompilerParams(dimension_semantics=("arbitrary",)),
        cost_estimate=pl.CostEstimate(flops=5 * T * T * hc * 2, bytes_accessed=T * hc * 24, transcendentals=T * T * heads // 2),
        name="attend_bwd",
    )(first, low8, *tables, qkv, ctx, lse, gc)


def relate(values, mine, count, axis):
    size = values.shape[axis] // count
    bit = 1
    while bit < count:
        order = [m ^ bit for m in range(count)]
        swapped = jnp.concatenate(
            [lax.slice_in_dim(values, m * size, (m + 1) * size, axis=axis) for m in order], axis=axis
        )
        values = jnp.where((mine & bit) != 0, swapped, values)
        bit *= 2
    return values


def swap_dp(values, rel):
    return lax.ppermute(values, "dp", [(d, d ^ rel) for d in range(lax.axis_size("dp"))])


def fetch(view):
    mine = lax.all_to_all(view, "seq", split_axis=0, concat_axis=0, tiled=True)
    return [mine] + [swap_dp(mine, rel) for rel in range(1, lax.axis_size("dp"))]


def stack_rows(pieces, start, size):
    cols = pieces[0].shape[2]
    return jnp.concatenate([p[:, start : start + size] for p in pieces], axis=0).reshape(-1, cols)


def reduce_dp(parts):
    total = parts[0].astype(F32)
    moved = [swap_dp(parts[rel], rel) for rel in range(1, parts.shape[0])]
    for piece in moved:
        total = total + piece.astype(F32)
    return total.astype(BF)


def send_back(summed):
    return lax.all_to_all(summed, "seq", split_axis=0, concat_axis=0, tiled=True)


def unit_of(values):
    center = values - jnp.mean(values, axis=-1, keepdims=True)
    factor = lax.rsqrt(jnp.mean(center * center, axis=-1, keepdims=True) + EPSILON)
    return center * factor, factor


def norm_back(upstream, unit, factor, gain):
    scaled = upstream * gain
    return factor * (
        scaled
        - jnp.mean(scaled, axis=-1, keepdims=True)
        - unit * jnp.mean(scaled * unit, axis=-1, keepdims=True)
    )


def dot(left, right, dims):
    return lax.dot_general(left, right, (dims, ((), ())), preferred_element_type=F32)


NN = ((1,), (0,))
NT = ((1,), (1,))
TN = ((0,), (0,))


def own_rows(partial):
    return lax.psum_scatter(partial.astype(BF), "seq", scatter_dimension=0, tiled=True).astype(F32)


def every(values):
    return lax.all_gather(values, "seq", axis=0, tiled=True)


def chip_shift(values, k, groups):
    return lax.ppermute(values, "seq", [(s, (s + 2 * k) % groups) for s in range(groups)])


def core_swap(values, groups):
    return lax.ppermute(values, "seq", [(s, s ^ 1) for s in range(groups)])


def own_rows_beside(partial, me, groups):
    chips = groups // 2
    tokens = partial.shape[0] // groups
    blocks = partial.reshape(chips, 2, tokens, partial.shape[1])
    core = me % 2
    theirs = lax.dynamic_index_in_dim(blocks, 1 - core, 1, keepdims=False)
    ours = lax.dynamic_index_in_dim(blocks, core, 1, keepdims=False)
    moved = core_swap(theirs, groups)
    pair = (ours.astype(F32) + moved.astype(F32)).astype(BF)
    chip = me // 2
    total = lax.dynamic_index_in_dim(pair, chip, 0, keepdims=False).astype(F32)
    for k in range(1, chips):
        part = lax.dynamic_index_in_dim(pair, (chip + k) % chips, 0, keepdims=False)
        total = total + chip_shift(part, k, groups).astype(F32)
    return total


def layer(
    inputs,
    position,
    upstream,
    attn_gain,
    attn_shift,
    qkv_weight,
    qkv_bias,
    out_weight,
    ffn_gain,
    ffn_shift,
    gate_weight,
    up_weight,
    down_weight,
):
    tokens, width = inputs.shape
    groups = lax.axis_size("seq")
    copies = lax.axis_size("dp")
    me = lax.axis_index("seq")
    mine = lax.axis_index("dp")
    length = tokens * groups
    heads = HEADS // groups
    hc = heads * HD
    rows = qkv_weight.shape[0]
    nbias = qkv_bias.shape[0]
    bq = 256

    own = relate(inputs, mine, copies, 1)
    own_up = relate(upstream, mine, copies, 1)
    x_all = every(own)

    def by_group(weight, parts=1):
        cols = weight.shape[1] // (parts * groups)
        view = weight.reshape(rows, parts, groups, cols).transpose(2, 0, 1, 3)
        return view.reshape(groups, rows, parts * cols)

    small = jnp.concatenate(
        [
            attn_gain,
            attn_shift,
            ffn_gain,
            ffn_shift,
            qkv_bias,
            (position // 256).astype(BF),
            (position % 256).astype(BF),
        ]
    )
    extra = jnp.zeros((8, 3 * hc), BF).at[0, : small.shape[0]].set(small)
    view_qkv = jnp.concatenate(
        [by_group(qkv_weight, 3), jnp.broadcast_to(extra[None], (groups, 8, 3 * hc))], axis=1
    )
    pieces_qkv = fetch(view_qkv)
    weight_qkv = stack_rows(pieces_qkv, 0, rows)
    weight_out = stack_rows(fetch(by_group(out_weight)), 0, rows)
    spot = pieces_qkv[0][:, rows, 4 * rows + nbias : 4 * rows + nbias + 2 * tokens]
    positions = (
        spot[:, :tokens].astype(jnp.int32) * 256 + spot[:, tokens:].astype(jnp.int32)
    ).reshape(length)
    everyone = jnp.stack([p[:, rows, : 4 * rows + nbias] for p in pieces_qkv]).astype(F32)
    gain_one, shift_one, gain_two, shift_two = [
        everyone[:, :, n * rows : (n + 1) * rows].reshape(1, width) for n in range(4)
    ]
    bias_full = relate(everyone[:, :, 4 * rows :].reshape(-1), mine, copies, 0)
    chosen = (jnp.arange(groups, dtype=jnp.int32) == me).astype(F32)
    bias_mine = jnp.sum(bias_full.reshape(3, groups, hc) * chosen[None, :, None], axis=1).reshape(1, -1)

    tables = rotary_rows(positions)
    lowest = jnp.arange(length, dtype=jnp.int32) - positions
    low8 = jnp.broadcast_to(lowest[None], (8, length))
    first = (jnp.min(lowest.reshape(length // bq, bq), axis=1) // bq).astype(jnp.int32)

    view_gu = jnp.concatenate([by_group(gate_weight), by_group(up_weight)], axis=1)
    view_gu, view_down, own_up, x_all = lax.optimization_barrier(
        (view_gu, by_group(down_weight), own_up, x_all)
    )
    up_all = every(own_up)
    pieces_gu = fetch(view_gu)
    weight_gate = stack_rows(pieces_gu, 0, rows)
    weight_up = stack_rows(pieces_gu, rows, rows)
    weight_down = stack_rows(fetch(view_down), 0, rows)

    unit_all, _ = unit_of(x_all.astype(F32))
    normed_one = (unit_all * gain_one + shift_one).astype(BF)
    projected = dot(normed_one, weight_qkv, NN) + bias_mine
    qkv, context, lse = attend_fwd(projected, tables, low8, first, heads, bq)
    flat = own.astype(F32)
    middle = flat + own_rows(dot(context, weight_out, NT))
    unit_two, factor_two = unit_of(middle)
    normed_two = (unit_two * gain_two + shift_two).astype(BF)
    normed_two = every(normed_two)
    gate = dot(normed_two, weight_gate, NN)
    upward = dot(normed_two, weight_up, NN)
    sig = jax.nn.sigmoid(gate)
    silu = gate * sig
    hidden = (silu * upward).astype(BF)
    grad_hidden = dot(up_all, weight_down, NN)
    grad_gate = (grad_hidden * upward * sig * (1.0 + gate * (1.0 - sig))).astype(BF)
    grad_up = (grad_hidden * silu).astype(BF)
    grad_normed_two = own_rows(dot(grad_gate, weight_gate, NT) + dot(grad_up, weight_up, NT))
    down_part = dot(hidden, weight_down, NT).astype(BF)
    grad_gate_weight = dot(normed_two, grad_gate, TN).astype(BF)
    grad_up_weight = dot(normed_two, grad_up, TN).astype(BF)
    grad_down_weight = dot(up_all, hidden, TN).astype(BF)

    def by_owner(grad):
        return grad.reshape(copies, groups, rows, grad.shape[1])

    sum_ffn = jnp.concatenate(
        [
            reduce_dp(by_owner(grad_gate_weight)),
            reduce_dp(by_owner(grad_up_weight)),
            reduce_dp(by_owner(grad_down_weight)),
        ],
        axis=1,
    )
    sum_ffn = send_back(sum_ffn).transpose(1, 0, 2)

    grad_middle = own_up.astype(F32) + norm_back(grad_normed_two, unit_two, factor_two, gain_two)
    grad_mixed, down_part = lax.optimization_barrier((grad_middle.astype(BF), down_part))
    output = (middle + own_rows_beside(down_part, me, groups)).astype(BF)
    grad_mixed = every(grad_mixed)
    grad_context = dot(grad_mixed, weight_out, NN).astype(BF)
    grad_projected, bias_part = attend_bwd(qkv, context, lse, grad_context, tables, low8, first, heads, bq)
    dqkv = dot(grad_projected, weight_qkv, NT).astype(BF)
    grad_normed_one = own_rows(dqkv)

    bias_part = jnp.sum(bias_part, axis=0).reshape(3, 1, hc) * chosen[None, :, None]
    bias_part = relate(bias_part.reshape(-1), mine, copies, 0).reshape(copies, groups, nbias)
    parts = [
        jnp.sum(dqkv.astype(F32) * unit_all, axis=0),
        jnp.sum(dqkv.astype(F32), axis=0),
        jnp.sum(grad_normed_two * unit_two, axis=0),
        jnp.sum(grad_normed_two, axis=0),
    ]
    parts = [p.reshape(copies, groups, 1, rows) for p in parts] + [bias_part[:, :, None]]
    parts = jnp.concatenate(parts, axis=3)
    parts = jnp.pad(parts, ((0, 0), (0, 0), (0, 7), (0, 3 * hc - parts.shape[3]))).astype(BF)

    grad_out_weight = dot(grad_mixed, context, TN).astype(BF)
    sum_out = reduce_dp(by_owner(grad_out_weight))
    grad_qkv_weight = dot(normed_one, grad_projected, TN).astype(BF)
    sum_qkv = reduce_dp(jnp.concatenate([by_owner(grad_qkv_weight), parts], axis=2))
    sum_attn = jnp.concatenate([sum_qkv, jnp.pad(sum_out, ((0, 0), (0, 8), (0, 0)))], axis=2)
    sum_attn = send_back(sum_attn)
    total = jnp.sum(sum_attn[:, rows].astype(F32), axis=0)
    sums = [total[n * rows : (n + 1) * rows] for n in range(4)] + [total[4 * rows : 4 * rows + nbias]]
    sum_attn = sum_attn[:, :rows].transpose(1, 0, 2)
    sum_qkv = sum_attn[:, :, : 3 * hc]
    sum_out = sum_attn[:, :, 3 * hc :]
    unit_one, factor_one = unit_of(flat)
    grad_input = grad_middle + norm_back(grad_normed_one, unit_one, factor_one, gain_one)

    def wide(value):
        return value.astype(F32).reshape(rows, -1)

    wide_qkv = sum_qkv.reshape(rows, groups, 3, hc).transpose(0, 2, 1, 3)
    return (
        relate(output, mine, copies, 1)[None],
        relate(grad_input, mine, copies, 1)[None],
        sums[0],
        sums[1],
        wide(wide_qkv),
        sums[4],
        wide(sum_out),
        sums[2],
        sums[3],
        wide(sum_ffn[:rows]),
        wide(sum_ffn[rows : 2 * rows]),
        wide(sum_ffn[2 * rows :]),
    )


def local(
    residual_in,
    attn_gain,
    attn_shift,
    qkv_weight,
    qkv_bias,
    out_weight,
    ffn_gain,
    ffn_shift,
    gate_weight,
    up_weight,
    down_weight,
    positions,
    cotangent,
):
    return layer(
        residual_in[0],
        positions[0],
        cotangent[0],
        attn_gain,
        attn_shift,
        qkv_weight,
        qkv_bias,
        out_weight,
        ffn_gain,
        ffn_shift,
        gate_weight,
        up_weight,
        down_weight,
    )


def solution(mesh):
    both = ("dp", "seq")
    in_specs = (
        P("dp", "seq", None),
        P(both),
        P(both),
        P(both, None),
        P(both),
        P(both, None),
        P(both),
        P(both),
        P(both, None),
        P(both, None),
        P(both, None),
        P("dp", "seq"),
        P("dp", "seq", None),
    )
    out_specs = (
        P("dp", "seq", None),
        P("dp", "seq", None),
        P(both),
        P(both),
        P(both, None),
        P(both),
        P(both, None),
        P(both),
        P(both),
        P(both, None),
        P(both, None),
        P(both, None),
    )
    return jax.shard_map(local, mesh=mesh, in_specs=in_specs, out_specs=out_specs, check_vma=False)
```

```python
import functools

import jax
import jax.numpy as jnp
from jax import lax
from jax.experimental import pallas as pl
from jax.experimental.pallas import tpu as pltpu
from jax.sharding import PartitionSpec as P


HEADS = 32
HD = 64
ROT = 16
LANES = 128
EPSILON = 1e-05
ROPE_BASE = 10000.0
MASKED = -1e30
BF = jnp.bfloat16
F32 = jnp.float32


def rotary_rows(position):
    lane = jnp.arange(LANES, dtype=jnp.int32) % HD
    half = ROT // 2
    power = ROPE_BASE ** (-(lane % half).astype(F32) * (2.0 / ROT))
    freq = jnp.where(lane < ROT, power, 0.0)
    angle = position.astype(F32)[:, None] * freq[None, :]
    cosine = jnp.cos(angle); sine = jnp.sin(angle)
    first = jnp.where(lane < half, -sine, 0.0)
    second = jnp.where((lane >= half) & (lane < ROT), sine, 0.0)
    return cosine, first, second


def turn(x, cosine, first, second):
    return x * cosine + pltpu.roll(x, LANES - ROT // 2, 1) * first + pltpu.roll(x, ROT // 2, 1) * second


def head_mask(x, h):
    lane = lax.broadcasted_iota(jnp.int32, x.shape, 1)
    return jnp.where((lane >= h * HD) & (lane < (h + 1) * HD), x, jnp.zeros_like(x))


def nt(a, b):
    return lax.dot_general(a, b, (((1,), (1,)), ((), ())), preferred_element_type=F32)


def nn(a, b):
    return lax.dot_general(a, b, (((1,), (0,)), ((), ())), preferred_element_type=F32)


def block_bias(i, j, bq, low_row):
    key = j * bq + lax.broadcasted_iota(jnp.int32, (bq, bq), 0)
    query = i * bq + lax.broadcasted_iota(jnp.int32, (bq, bq), 1)
    return jnp.where((key <= query) & (key >= low_row), 0.0, MASKED)


def fwd_kernel(heads, bq, first_ref, low_ref, cos_ref, s1_ref, s2_ref, proj_ref,
               qkv_ref, ctx_ref, lse_ref, k_s, vt_s, st_s):
    i = pl.program_id(0)
    hc = heads * HD
    c, s1, s2 = cos_ref[...], s1_ref[...], s2_ref[...]
    parts = []
    for base in (0, hc):
        for t in range(hc // LANES):
            x = proj_ref[:, base + t * LANES: base + (t + 1) * LANES]
            parts.append(turn(x, c, s1, s2).astype(BF))
    n = hc // LANES
    q = jnp.concatenate(parts[:n], axis=1) if n > 1 else parts[0]
    k = jnp.concatenate(parts[n:], axis=1) if n > 1 else parts[n]
    v32 = proj_ref[:, 2 * hc:]
    v = v32.astype(BF)
    qkv_ref[:, :hc] = q
    qkv_ref[:, hc:2 * hc] = k
    qkv_ref[:, 2 * hc:] = v
    rows = pl.ds(pl.multiple_of(i * bq, bq), bq)
    k_s[rows, :] = k
    vt_s[:, rows] = v32.T.astype(BF)
    low = low_ref[0:1, :]
    qm = [head_mask(q, h) for h in range(heads)]
    first = first_ref[i]

    def score_step(j, tops):
        kj = k_s[pl.ds(pl.multiple_of(j * bq, bq), bq), :]
        bias = block_bias(i, j, bq, low)
        out = []
        for h in range(heads):
            s = nt(kj, qm[h]) * 0.125 + bias
            st_s[h, pl.ds(pl.multiple_of(j * bq, bq), bq), :] = s
            out.append(jnp.maximum(tops[h], jnp.max(s.reshape(bq // 8, 8, bq), axis=0)))
        return tuple(out)

    tops = lax.fori_loop(first, i + 1, score_step,
                         tuple(jnp.full((8, bq), MASKED, F32) for _ in range(heads)))
    tops = [jnp.max(t, axis=0, keepdims=True) for t in tops]

    def value_step(j, state):
        new = []
        vt = vt_s[:, pl.ds(pl.multiple_of(j * bq, bq), bq)]
        for h in range(heads):
            tot, acc = state[h]
            p = jnp.exp(st_s[h, pl.ds(pl.multiple_of(j * bq, bq), bq), :] - tops[h])
            tot = tot + jnp.sum(p.reshape(bq // 8, 8, bq), axis=0)
            acc = acc + nn(vt[h * HD:(h + 1) * HD, :], p.astype(BF))
            new.append((tot, acc))
        return tuple(new)

    state = lax.fori_loop(first, i + 1, value_step,
                          tuple((jnp.zeros((8, bq), F32), jnp.zeros((HD, bq), F32)) for _ in range(heads)))
    outs = []
    lses = []
    for h in range(heads):
        tot, acc = state[h]
        tot = jnp.sum(tot, axis=0, keepdims=True)
        outs.append(acc / tot)
        lses.append(tops[h] + jnp.log(tot))
    ctx_ref[...] = jnp.concatenate(outs, axis=0).T.astype(BF)
    pad = [jnp.zeros((8 - heads, bq), F32)] if heads < 8 else []
    lse_ref[...] = jnp.concatenate(lses + pad, axis=0)


def attend_fwd(proj, tables, low8, first, heads, bq):
    T = proj.shape[0]; hc = heads * HD
    row = lambda w: pl.BlockSpec((bq, w), lambda i, f: (i, 0))
    return pl.pallas_call(
        functools.partial(fwd_kernel, heads, bq),
        grid_spec=pltpu.PrefetchScalarGridSpec(
            num_scalar_prefetch=1, grid=(T // bq,),
            in_specs=[pl.BlockSpec((8, bq), lambda i, f: (0, i)), row(LANES), row(LANES), row(LANES), row(3 * hc)],
            out_specs=[row(3 * hc), row(hc), pl.BlockSpec((8, bq), lambda i, f: (0, i))],
            scratch_shapes=[pltpu.VMEM((T, hc), BF), pltpu.VMEM((hc, T), BF), pltpu.VMEM((heads, T, bq), F32)]),
        out_shape=[jax.ShapeDtypeStruct((T, 3 * hc), BF), jax.ShapeDtypeStruct((T, hc), BF), jax.ShapeDtypeStruct((8, T), F32)],
        compiler_params=pltpu.CompilerParams(dimension_semantics=("arbitrary",)),
        cost_estimate=pl.CostEstimate(flops=2 * T * T * hc * 2, bytes_accessed=T * hc * 24, transcendentals=T * T * heads // 2),
        name="attend_fwd",
    )(first, low8, *tables, proj)


def bwd_kernel(heads, bq, count, first_ref, low_ref, cos_ref, s1_ref, s2_ref, qkv_ref, ctx_ref, lse_ref, gc_ref,
               gp_ref, bias_ref, dk_s, dv_s, dq_s):
    step = pl.program_id(0)
    i = count - 1 - step
    hc = heads * HD
    rows = pl.ds(pl.multiple_of(i * bq, bq), bq)

    @pl.when(step == 0)
    def _():
        dk_s[...] = jnp.zeros_like(dk_s)
        dv_s[...] = jnp.zeros_like(dv_s)
        bias_ref[...] = jnp.zeros_like(bias_ref)

    low = low_ref[0:1, rows]
    q = qkv_ref[rows, :hc]
    g = gc_ref[rows, :]
    prod = (g.astype(F32) * ctx_ref[rows, :].astype(F32)).T
    deltas = [jnp.sum(prod[h * HD:(h + 1) * HD, :], axis=0, keepdims=True) for h in range(heads)]
    lses = [lse_ref[h:h + 1, rows] for h in range(heads)]
    qm = [head_mask(q, h) for h in range(heads)]
    gm = [head_mask(g, h) for h in range(heads)]
    dq_s[...] = jnp.zeros_like(dq_s)

    @pl.loop(first_ref[i], i + 1)
    def _(j):
        cols = pl.ds(pl.multiple_of(j * bq, bq), bq)
        kj = qkv_ref[cols, hc:2 * hc]
        vj = qkv_ref[cols, 2 * hc:]
        kt = kj.T
        bias = block_bias(i, j, bq, low)
        dk = dk_s[cols, :]
        dv = dv_s[cols, :]
        for h in range(heads):
            s = nt(kj, qm[h]) * 0.125 + bias
            p = jnp.exp(s - lses[h])
            dp = nt(vj, gm[h])
            ds = (p * (dp - deltas[h]) * 0.125).astype(BF)
            dv = dv + nn(p.astype(BF), gm[h])
            dk = dk + nn(ds, qm[h])
            dq_s[h * HD:(h + 1) * HD, :] += nn(kt[h * HD:(h + 1) * HD, :], ds)
        dk_s[cols, :] = dk
        dv_s[cols, :] = dv

    c, s1, s2 = cos_ref[rows, :], s1_ref[rows, :], s2_ref[rows, :]
    dq = dq_s[...].T
    dk = dk_s[rows, :]
    dv = dv_s[rows, :]

    def emit(x, base):
        gp_ref[:, base: base + x.shape[1]] = x.astype(BF)
        bias_ref[:, base: base + x.shape[1]] += jnp.sum(x.reshape(bq // 8, 8, x.shape[1]), axis=0)

    for src, base in ((dq, 0), (dk, hc)):
        for t in range(hc // LANES):
            emit(turn(src[:, t * LANES:(t + 1) * LANES], c, -s1, -s2), base + t * LANES)
    emit(dv, 2 * hc)


def attend_bwd(qkv, ctx, lse, gc, tables, low8, first, heads, bq):
    T = qkv.shape[0]; hc = heads * HD; count = T // bq
    full = lambda r, w: pl.BlockSpec((r, w), lambda i, f: (0, 0))
    return pl.pallas_call(
        functools.partial(bwd_kernel, heads, bq, count),
        grid_spec=pltpu.PrefetchScalarGridSpec(
            num_scalar_prefetch=1, grid=(count,),
            in_specs=[full(8, T), full(T, LANES), full(T, LANES), full(T, LANES), full(T, 3 * hc), full(T, hc), full(8, T), full(T, hc)],
            out_specs=[pl.BlockSpec((bq, 3 * hc), lambda i, f: (count - 1 - i, 0)), full(8, 3 * hc)],
            scratch_shapes=[pltpu.VMEM((T, hc), F32), pltpu.VMEM((T, hc), F32), pltpu.VMEM((hc, bq), F32)]),
        out_shape=[jax.ShapeDtypeStruct((T, 3 * hc), BF), jax.ShapeDtypeStruct((8, 3 * hc), F32)],
        compiler_params=pltpu.CompilerParams(dimension_semantics=("arbitrary",)),
        cost_estimate=pl.CostEstimate(flops=5 * T * T * hc * 2, bytes_accessed=T * hc * 24, transcendentals=T * T * heads // 2),
        name="attend_bwd",
    )(first, low8, *tables, qkv, ctx, lse, gc)


def relate(values, mine, count, axis):
    size = values.shape[axis] // count
    bit = 1
    while bit < count:
        order = [m ^ bit for m in range(count)]
        swapped = jnp.concatenate(
            [lax.slice_in_dim(values, m * size, (m + 1) * size, axis=axis) for m in order], axis=axis
        )
        values = jnp.where((mine & bit) != 0, swapped, values)
        bit *= 2
    return values


def swap_dp(values, rel):
    return lax.ppermute(values, "dp", [(d, d ^ rel) for d in range(lax.axis_size("dp"))])


def take(view):
    return lax.all_to_all(view, "seq", split_axis=0, concat_axis=0, tiled=True)


def spread(mine):
    return [mine] + [swap_dp(mine, rel) for rel in range(1, lax.axis_size("dp"))]


def stack_rows(pieces, start, size):
    cols = pieces[0].shape[2]
    return jnp.concatenate([p[:, start : start + size] for p in pieces], axis=0).reshape(-1, cols)


def reduce_dp(parts):
    total = parts[0].astype(F32)
    moved = [swap_dp(parts[rel], rel) for rel in range(1, len(parts))]
    for piece in moved:
        total = total + piece.astype(F32)
    return total.astype(BF)


def send_back(summed):
    return lax.all_to_all(summed, "seq", split_axis=0, concat_axis=0, tiled=True)


def unit_of(values):
    center = values - jnp.mean(values, axis=-1, keepdims=True)
    factor = lax.rsqrt(jnp.mean(center * center, axis=-1, keepdims=True) + EPSILON)
    return center * factor, factor


def norm_back(upstream, unit, factor, gain):
    scaled = upstream * gain
    return factor * (
        scaled
        - jnp.mean(scaled, axis=-1, keepdims=True)
        - unit * jnp.mean(scaled * unit, axis=-1, keepdims=True)
    )


def dot(left, right, dims):
    return lax.dot_general(left, right, (dims, ((), ())), preferred_element_type=F32)


NN = ((1,), (0,))
NT = ((1,), (1,))
TN = ((0,), (0,))


def own_rows(partial):
    return lax.psum_scatter(partial.astype(BF), "seq", scatter_dimension=0, tiled=True).astype(F32)


def every(values):
    return lax.all_gather(values, "seq", axis=0, tiled=True)


def chip_shift(values, k, groups):
    return lax.ppermute(values, "seq", [(s, (s + 2 * k) % groups) for s in range(groups)])


def core_swap(values, groups):
    return lax.ppermute(values, "seq", [(s, s ^ 1) for s in range(groups)])


def own_rows_beside(partial, me, groups):
    chips = groups // 2
    tokens = partial.shape[0] // groups
    blocks = partial.reshape(chips, 2, tokens, partial.shape[1])
    core = me % 2
    theirs = lax.dynamic_index_in_dim(blocks, 1 - core, 1, keepdims=False)
    ours = lax.dynamic_index_in_dim(blocks, core, 1, keepdims=False)
    moved = core_swap(theirs, groups)
    pair = (ours.astype(F32) + moved.astype(F32)).astype(BF)
    chip = me // 2
    moved = [
        chip_shift(lax.dynamic_index_in_dim(pair, (chip + k) % chips, 0, keepdims=False), k, groups)
        for k in range(1, chips)
    ]
    return [lax.dynamic_index_in_dim(pair, chip, 0, keepdims=False)] + moved


def layer(
    inputs,
    position,
    upstream,
    attn_gain,
    attn_shift,
    qkv_weight,
    qkv_bias,
    out_weight,
    ffn_gain,
    ffn_shift,
    gate_weight,
    up_weight,
    down_weight,
):
    tokens, width = inputs.shape
    groups = lax.axis_size("seq")
    copies = lax.axis_size("dp")
    me = lax.axis_index("seq")
    mine = lax.axis_index("dp")
    length = tokens * groups
    heads = HEADS // groups
    hc = heads * HD
    rows = qkv_weight.shape[0]
    nbias = qkv_bias.shape[0]
    bq = 256

    own = relate(inputs, mine, copies, 1)
    own_up = relate(upstream, mine, copies, 1)

    def by_group(weight, parts=1):
        cols = weight.shape[1] // (parts * groups)
        view = weight.reshape(rows, parts, groups, cols).transpose(2, 0, 1, 3)
        return view.reshape(groups, rows, parts * cols)

    small = jnp.concatenate(
        [
            attn_gain,
            attn_shift,
            ffn_gain,
            ffn_shift,
            qkv_bias,
            (position // 256).astype(BF),
            (position % 256).astype(BF),
        ]
    )
    extra = jnp.zeros((8, 3 * hc), BF).at[0, : small.shape[0]].set(small)
    view_qkv = jnp.concatenate(
        [by_group(qkv_weight, 3), jnp.broadcast_to(extra[None], (groups, 8, 3 * hc))], axis=1
    )
    taken, own = lax.optimization_barrier((take(view_qkv), own))
    x_all = every(own)
    pieces_qkv = spread(taken)
    weight_qkv = stack_rows(pieces_qkv, 0, rows)
    taken, own_up = lax.optimization_barrier((take(by_group(out_weight)), own_up))
    up_all = every(own_up)
    weight_out = stack_rows(spread(taken), 0, rows)
    spot = pieces_qkv[0][:, rows, 4 * rows + nbias : 4 * rows + nbias + 2 * tokens]
    positions = (
        spot[:, :tokens].astype(jnp.int32) * 256 + spot[:, tokens:].astype(jnp.int32)
    ).reshape(length)
    everyone = jnp.stack([p[:, rows, : 4 * rows + nbias] for p in pieces_qkv]).astype(F32)
    gain_one, shift_one, gain_two, shift_two = [
        everyone[:, :, n * rows : (n + 1) * rows].reshape(1, width) for n in range(4)
    ]
    bias_full = relate(everyone[:, :, 4 * rows :].reshape(-1), mine, copies, 0)
    chosen = (jnp.arange(groups, dtype=jnp.int32) == me).astype(F32)
    bias_mine = jnp.sum(bias_full.reshape(3, groups, hc) * chosen[None, :, None], axis=1).reshape(1, -1)

    tables = rotary_rows(positions)
    lowest = jnp.arange(length, dtype=jnp.int32) - positions
    low8 = jnp.broadcast_to(lowest[None], (8, length))
    first = (jnp.min(lowest.reshape(length // bq, bq), axis=1) // bq).astype(jnp.int32)

    view_gu = jnp.concatenate([by_group(gate_weight), by_group(up_weight)], axis=1)
    view_gu, view_down, x_all = lax.optimization_barrier((view_gu, by_group(down_weight), x_all))
    pieces_gu = spread(take(view_gu))
    weight_gate = stack_rows(pieces_gu, 0, rows)
    weight_up = stack_rows(pieces_gu, rows, rows)
    weight_down = stack_rows(spread(take(view_down)), 0, rows)

    unit_all, unused = unit_of(x_all.astype(F32))
    normed_one = (unit_all * gain_one + shift_one).astype(BF)
    projected = dot(normed_one, weight_qkv, NN) + bias_mine
    qkv, context, lse = attend_fwd(projected, tables, low8, first, heads, bq)
    flat = own.astype(F32)
    middle = flat + own_rows(dot(context, weight_out, NT))
    unit_two, factor_two = unit_of(middle)
    normed_two = (unit_two * gain_two + shift_two).astype(BF)
    normed_two = every(normed_two)
    gate = dot(normed_two, weight_gate, NN)
    upward = dot(normed_two, weight_up, NN)
    sig = jax.nn.sigmoid(gate)
    silu = gate * sig
    hidden = (silu * upward).astype(BF)
    grad_hidden = dot(up_all, weight_down, NN)
    grad_gate = (grad_hidden * upward * sig * (1.0 + gate * (1.0 - sig))).astype(BF)
    grad_up = (grad_hidden * silu).astype(BF)
    grad_normed_two = own_rows(dot(grad_gate, weight_gate, NT) + dot(grad_up, weight_up, NT))
    down_part = dot(hidden, weight_down, NT).astype(BF)
    block = width // copies

    def by_owner(left, right):
        return [
            dot(left[:, m * block : (m + 1) * block], right, TN).astype(BF).reshape(groups, rows, -1)
            for m in range(copies)
        ]

    grad_gate_weight = by_owner(normed_two, grad_gate)
    grad_up_weight = by_owner(normed_two, grad_up)
    grad_down_weight = by_owner(up_all, hidden)
    sum_ffn = jnp.concatenate(
        [reduce_dp(grad_gate_weight), reduce_dp(grad_up_weight), reduce_dp(grad_down_weight)],
        axis=1,
    )
    sum_ffn = send_back(sum_ffn).transpose(1, 0, 2)

    grad_middle = own_up.astype(F32) + norm_back(grad_normed_two, unit_two, factor_two, gain_two)
    grad_mixed = grad_middle.astype(BF)
    down_sum = own_rows_beside(down_part, me, groups)
    grad_mixed = every(grad_mixed)
    grad_context = dot(grad_mixed, weight_out, NN).astype(BF)
    grad_projected, bias_part = attend_bwd(qkv, context, lse, grad_context, tables, low8, first, heads, bq)
    dqkv = dot(grad_projected, weight_qkv, NT).astype(BF)
    grad_normed_one = own_rows(dqkv)

    late, unused = lax.optimization_barrier((down_sum[0], bias_part))
    total = late.astype(F32)
    for piece in down_sum[1:]:
        total = total + piece.astype(F32)
    output = (middle + total).astype(BF)

    bias_part = jnp.sum(bias_part, axis=0).reshape(3, 1, hc) * chosen[None, :, None]
    bias_part = relate(bias_part.reshape(-1), mine, copies, 0).reshape(copies, groups, nbias)
    parts = [
        jnp.sum(dqkv.astype(F32) * unit_all, axis=0),
        jnp.sum(dqkv.astype(F32), axis=0),
        jnp.sum(grad_normed_two * unit_two, axis=0),
        jnp.sum(grad_normed_two, axis=0),
    ]
    parts = [p.reshape(copies, groups, 1, rows) for p in parts] + [bias_part[:, :, None]]
    parts = jnp.concatenate(parts, axis=3)
    parts = jnp.pad(parts, ((0, 0), (0, 0), (0, 7), (0, 3 * hc - parts.shape[3]))).astype(BF)

    sum_out = reduce_dp(by_owner(grad_mixed, context))
    grad_qkv_weight = by_owner(normed_one, grad_projected)
    sum_qkv = reduce_dp([jnp.concatenate([grad_qkv_weight[m], parts[m]], axis=1) for m in range(copies)])
    sum_attn = jnp.concatenate([sum_qkv, jnp.pad(sum_out, ((0, 0), (0, 8), (0, 0)))], axis=2)
    sum_attn = send_back(sum_attn)
    total = jnp.sum(sum_attn[:, rows].astype(F32), axis=0)
    sums = [total[n * rows : (n + 1) * rows] for n in range(4)] + [total[4 * rows : 4 * rows + nbias]]
    sum_attn = sum_attn[:, :rows].transpose(1, 0, 2)
    sum_qkv = sum_attn[:, :, : 3 * hc]
    sum_out = sum_attn[:, :, 3 * hc :]
    unit_one, factor_one = unit_of(flat)
    grad_input = grad_middle + norm_back(grad_normed_one, unit_one, factor_one, gain_one)

    def wide(value):
        return value.astype(F32).reshape(rows, -1)

    wide_qkv = sum_qkv.reshape(rows, groups, 3, hc).transpose(0, 2, 1, 3)
    return (
        relate(output, mine, copies, 1)[None],
        relate(grad_input, mine, copies, 1)[None],
        sums[0],
        sums[1],
        wide(wide_qkv),
        sums[4],
        wide(sum_out),
        sums[2],
        sums[3],
        wide(sum_ffn[:rows]),
        wide(sum_ffn[rows : 2 * rows]),
        wide(sum_ffn[2 * rows :]),
    )


def local(
    residual_in,
    attn_gain,
    attn_shift,
    qkv_weight,
    qkv_bias,
    out_weight,
    ffn_gain,
    ffn_shift,
    gate_weight,
    up_weight,
    down_weight,
    positions,
    cotangent,
):
    return layer(
        residual_in[0],
        positions[0],
        cotangent[0],
        attn_gain,
        attn_shift,
        qkv_weight,
        qkv_bias,
        out_weight,
        ffn_gain,
        ffn_shift,
        gate_weight,
        up_weight,
        down_weight,
    )


def solution(mesh):
    both = ("dp", "seq")
    in_specs = (
        P("dp", "seq", None),
        P(both),
        P(both),
        P(both, None),
        P(both),
        P(both, None),
        P(both),
        P(both),
        P(both, None),
        P(both, None),
        P(both, None),
        P("dp", "seq"),
        P("dp", "seq", None),
    )
    out_specs = (
        P("dp", "seq", None),
        P("dp", "seq", None),
        P(both),
        P(both),
        P(both, None),
        P(both),
        P(both, None),
        P(both),
        P(both),
        P(both, None),
        P(both, None),
        P(both, None),
    )
    return jax.shard_map(local, mesh=mesh, in_specs=in_specs, out_specs=out_specs, check_vma=False)
```

```python
import functools

import jax
import jax.numpy as jnp
from jax import lax
from jax.experimental import pallas as pl
from jax.experimental.pallas import tpu as pltpu
from jax.sharding import PartitionSpec as P


HEADS = 32
HD = 64
ROT = 16
LANES = 128
EPSILON = 1e-05
ROPE_BASE = 10000.0
MASKED = -1e30
BF = jnp.bfloat16
F32 = jnp.float32

DP = "dp"
SEQ = "seq"


def rotary_rows(position):
    lane = jnp.arange(LANES, dtype=jnp.int32) % HD
    half = ROT // 2
    power = ROPE_BASE ** (-(lane % half).astype(F32) * (2.0 / ROT))
    freq = jnp.where(lane < ROT, power, 0.0)
    angle = position.astype(F32)[:, None] * freq[None, :]
    cosine = jnp.cos(angle); sine = jnp.sin(angle)
    first = jnp.where(lane < half, -sine, 0.0)
    second = jnp.where((lane >= half) & (lane < ROT), sine, 0.0)
    return cosine, first, second


def turn(x, cosine, first, second):
    return x * cosine + pltpu.roll(x, LANES - ROT // 2, 1) * first + pltpu.roll(x, ROT // 2, 1) * second


def head_mask(x, h):
    lane = lax.broadcasted_iota(jnp.int32, x.shape, 1)
    return jnp.where((lane >= h * HD) & (lane < (h + 1) * HD), x, jnp.zeros_like(x))


def nt(a, b):
    return lax.dot_general(a, b, (((1,), (1,)), ((), ())), preferred_element_type=F32)


def nn(a, b):
    return lax.dot_general(a, b, (((1,), (0,)), ((), ())), preferred_element_type=F32)


def block_bias(i, j, bq, low_row):
    key = j * bq + lax.broadcasted_iota(jnp.int32, (bq, bq), 0)
    query = i * bq + lax.broadcasted_iota(jnp.int32, (bq, bq), 1)
    return jnp.where((key <= query) & (key >= low_row), 0.0, MASKED)


def fwd_kernel(heads, bq, first_ref, low_ref, cos_ref, s1_ref, s2_ref, proj_ref,
               qkv_ref, ctx_ref, lse_ref, k_s, vt_s, st_s):
    i = pl.program_id(0)
    hc = heads * HD
    c, s1, s2 = cos_ref[...], s1_ref[...], s2_ref[...]
    parts = []
    for base in (0, hc):
        for t in range(hc // LANES):
            x = proj_ref[:, base + t * LANES: base + (t + 1) * LANES]
            parts.append(turn(x, c, s1, s2).astype(BF))
    n = hc // LANES
    q = jnp.concatenate(parts[:n], axis=1) if n > 1 else parts[0]
    k = jnp.concatenate(parts[n:], axis=1) if n > 1 else parts[n]
    v32 = proj_ref[:, 2 * hc:]
    v = v32.astype(BF)
    qkv_ref[:, :hc] = q
    qkv_ref[:, hc:2 * hc] = k
    qkv_ref[:, 2 * hc:] = v
    rows = pl.ds(pl.multiple_of(i * bq, bq), bq)
    k_s[rows, :] = k
    vt_s[:, rows] = v32.T.astype(BF)
    low = low_ref[0:1, :]
    qm = [head_mask(q, h) for h in range(heads)]
    first = first_ref[i]

    def score_step(j, tops):
        kj = k_s[pl.ds(pl.multiple_of(j * bq, bq), bq), :]
        bias = block_bias(i, j, bq, low)
        out = []
        for h in range(heads):
            s = nt(kj, qm[h]) * 0.125 + bias
            st_s[h, pl.ds(pl.multiple_of(j * bq, bq), bq), :] = s
            out.append(jnp.maximum(tops[h], jnp.max(s.reshape(bq // 8, 8, bq), axis=0)))
        return tuple(out)

    tops = lax.fori_loop(first, i + 1, score_step,
                         tuple(jnp.full((8, bq), MASKED, F32) for _ in range(heads)))
    tops = [jnp.max(t, axis=0, keepdims=True) for t in tops]

    def value_step(j, state):
        new = []
        vt = vt_s[:, pl.ds(pl.multiple_of(j * bq, bq), bq)]
        for h in range(heads):
            tot, acc = state[h]
            p = jnp.exp(st_s[h, pl.ds(pl.multiple_of(j * bq, bq), bq), :] - tops[h])
            tot = tot + jnp.sum(p.reshape(bq // 8, 8, bq), axis=0)
            acc = acc + nn(vt[h * HD:(h + 1) * HD, :], p.astype(BF))
            new.append((tot, acc))
        return tuple(new)

    state = lax.fori_loop(first, i + 1, value_step,
                          tuple((jnp.zeros((8, bq), F32), jnp.zeros((HD, bq), F32)) for _ in range(heads)))
    outs = []
    lses = []
    for h in range(heads):
        tot, acc = state[h]
        tot = jnp.sum(tot, axis=0, keepdims=True)
        outs.append(acc / tot)
        lses.append(tops[h] + jnp.log(tot))
    ctx_ref[...] = jnp.concatenate(outs, axis=0).T.astype(BF)
    pad = [jnp.zeros((8 - heads, bq), F32)] if heads < 8 else []
    lse_ref[...] = jnp.concatenate(lses + pad, axis=0)


def attend_fwd(proj, tables, low8, first, heads, bq):
    T = proj.shape[0]; hc = heads * HD
    row = lambda w: pl.BlockSpec((bq, w), lambda i, f: (i, 0))
    return pl.pallas_call(
        functools.partial(fwd_kernel, heads, bq),
        grid_spec=pltpu.PrefetchScalarGridSpec(
            num_scalar_prefetch=1, grid=(T // bq,),
            in_specs=[pl.BlockSpec((8, bq), lambda i, f: (0, i)), row(LANES), row(LANES), row(LANES), row(3 * hc)],
            out_specs=[row(3 * hc), row(hc), pl.BlockSpec((8, bq), lambda i, f: (0, i))],
            scratch_shapes=[pltpu.VMEM((T, hc), BF), pltpu.VMEM((hc, T), BF), pltpu.VMEM((heads, T, bq), F32)]),
        out_shape=[jax.ShapeDtypeStruct((T, 3 * hc), BF), jax.ShapeDtypeStruct((T, hc), BF), jax.ShapeDtypeStruct((8, T), F32)],
        cost_estimate=pl.CostEstimate(flops=2 * T * T * hc * 2, bytes_accessed=T * hc * 24, transcendentals=T * T * heads // 2),
        name="af",
    )(first, low8, *tables, proj)


def bwd_kernel(heads, bq, count, first_ref, low_ref, cos_ref, s1_ref, s2_ref, qkv_ref, ctx_ref, lse_ref, gc_ref,
               gp_ref, bias_ref, dk_s, dv_s, dq_s):
    step = pl.program_id(0)
    i = count - 1 - step
    hc = heads * HD
    rows = pl.ds(pl.multiple_of(i * bq, bq), bq)

    @pl.when(step == 0)
    def _():
        dk_s[...] = jnp.zeros_like(dk_s)
        dv_s[...] = jnp.zeros_like(dv_s)
        bias_ref[...] = jnp.zeros_like(bias_ref)

    low = low_ref[0:1, rows]
    q = qkv_ref[rows, :hc]
    g = gc_ref[rows, :]
    prod = (g.astype(F32) * ctx_ref[rows, :].astype(F32)).T
    deltas = [jnp.sum(prod[h * HD:(h + 1) * HD, :], axis=0, keepdims=True) for h in range(heads)]
    lses = [lse_ref[h:h + 1, rows] for h in range(heads)]
    qm = [head_mask(q, h) for h in range(heads)]
    gm = [head_mask(g, h) for h in range(heads)]
    dq_s[...] = jnp.zeros_like(dq_s)

    @pl.loop(first_ref[i], i + 1)
    def _(j):
        cols = pl.ds(pl.multiple_of(j * bq, bq), bq)
        kj = qkv_ref[cols, hc:2 * hc]
        vj = qkv_ref[cols, 2 * hc:]
        kt = kj.T
        bias = block_bias(i, j, bq, low)
        dk = dk_s[cols, :]
        dv = dv_s[cols, :]
        for h in range(heads):
            s = nt(kj, qm[h]) * 0.125 + bias
            p = jnp.exp(s - lses[h])
            dp = nt(vj, gm[h])
            ds = (p * (dp - deltas[h]) * 0.125).astype(BF)
            dv = dv + nn(p.astype(BF), gm[h])
            dk = dk + nn(ds, qm[h])
            dq_s[h * HD:(h + 1) * HD, :] += nn(kt[h * HD:(h + 1) * HD, :], ds)
        dk_s[cols, :] = dk
        dv_s[cols, :] = dv

    c, s1, s2 = cos_ref[rows, :], s1_ref[rows, :], s2_ref[rows, :]
    dq = dq_s[...].T
    dk = dk_s[rows, :]
    dv = dv_s[rows, :]

    def emit(x, base):
        gp_ref[:, base: base + x.shape[1]] = x.astype(BF)
        bias_ref[:, base: base + x.shape[1]] += jnp.sum(x.reshape(bq // 8, 8, x.shape[1]), axis=0)

    for src, base in ((dq, 0), (dk, hc)):
        for t in range(hc // LANES):
            emit(turn(src[:, t * LANES:(t + 1) * LANES], c, -s1, -s2), base + t * LANES)
    emit(dv, 2 * hc)


def attend_bwd(qkv, ctx, lse, gc, tables, low8, first, heads, bq):
    T = qkv.shape[0]; hc = heads * HD; count = T // bq
    full = lambda r, w: pl.BlockSpec((r, w), lambda i, f: (0, 0))
    return pl.pallas_call(
        functools.partial(bwd_kernel, heads, bq, count),
        grid_spec=pltpu.PrefetchScalarGridSpec(
            num_scalar_prefetch=1, grid=(count,),
            in_specs=[full(8, T), full(T, LANES), full(T, LANES), full(T, LANES), full(T, 3 * hc), full(T, hc), full(8, T), full(T, hc)],
            out_specs=[pl.BlockSpec((bq, 3 * hc), lambda i, f: (count - 1 - i, 0)), full(8, 3 * hc)],
            scratch_shapes=[pltpu.VMEM((T, hc), F32), pltpu.VMEM((T, hc), F32), pltpu.VMEM((hc, bq), F32)]),
        out_shape=[jax.ShapeDtypeStruct((T, 3 * hc), BF), jax.ShapeDtypeStruct((8, 3 * hc), F32)],
        cost_estimate=pl.CostEstimate(flops=5 * T * T * hc * 2, bytes_accessed=T * hc * 24, transcendentals=T * T * heads // 2),
        name="ab",
    )(first, low8, *tables, qkv, ctx, lse, gc)


def relate(values, mine, count, axis):
    size = values.shape[axis] // count
    bit = 1
    while bit < count:
        order = [m ^ bit for m in range(count)]
        swapped = jnp.concatenate(
            [lax.slice_in_dim(values, m * size, (m + 1) * size, axis=axis) for m in order], axis=axis
        )
        values = jnp.where((mine & bit) != 0, swapped, values)
        bit *= 2
    return values


def swap_dp(values, rel):
    return lax.ppermute(values, DP, [(d, d ^ rel) for d in range(lax.axis_size(DP))])


def take(view):
    return lax.all_to_all(view, SEQ, split_axis=0, concat_axis=0, tiled=True)


def spread(mine):
    return [mine] + [swap_dp(mine, rel) for rel in range(1, lax.axis_size(DP))]


def stack_rows(pieces, start, size):
    cols = pieces[0].shape[2]
    return jnp.concatenate([p[:, start : start + size] for p in pieces], axis=0).reshape(-1, cols)


def reduce_dp(parts):
    total = parts[0].astype(F32)
    moved = [swap_dp(parts[rel], rel) for rel in range(1, len(parts))]
    for piece in moved:
        total = total + piece.astype(F32)
    return total.astype(BF)


def send_back(summed):
    return lax.all_to_all(summed, SEQ, split_axis=0, concat_axis=0, tiled=True)


def ffn_kernel(copies, rows, n_ref, u_ref, *refs):
    pair, down, (act_ref, dx_ref) = refs[:copies], refs[copies : 2 * copies], refs[2 * copies :]
    block = n_ref.shape[1] // copies
    cols = pair[0].shape[2]

    def gate_rows(m):
        return pair[m][:, :rows, :].reshape(block, cols)

    def up_rows(m):
        return pair[m][:, rows:, :].reshape(block, cols)

    gate = upward = grad = 0.0
    for m in range(copies):
        span = slice(m * block, (m + 1) * block)
        gate = gate + nn(n_ref[:, span], gate_rows(m))
        upward = upward + nn(n_ref[:, span], up_rows(m))
        grad = grad + nn(u_ref[:, span], down[m][...].reshape(block, cols))
    sig = jax.nn.sigmoid(gate)
    silu = gate * sig
    grad_gate = (grad * upward * sig * (1.0 + gate * (1.0 - sig))).astype(BF)
    grad_up = (grad * silu).astype(BF)
    act_ref[0] = grad_gate
    act_ref[1] = grad_up
    act_ref[2] = (silu * upward).astype(BF)
    for m in range(copies):
        part = nt(grad_gate, gate_rows(m)) + nt(grad_up, up_rows(m))
        dx_ref[:, m * block : (m + 1) * block] = part.astype(BF)


def whole(array):
    zero = (0,) * array.ndim
    return pl.BlockSpec(array.shape, lambda *i: zero, pipeline_mode=pl.Buffered(1))


def ffn_both(normed, upstream, pair, down, rows, bq):
    length, width = normed.shape
    cols = down[0].shape[2]
    row = pl.BlockSpec((bq, width), lambda i: (i, 0))
    return pl.pallas_call(
        functools.partial(ffn_kernel, len(pair), rows),
        grid=(length // bq,),
        in_specs=[row, row] + [whole(w) for w in pair + down],
        out_specs=[pl.BlockSpec((3, bq, cols), lambda i: (0, i, 0)), row],
        out_shape=[
            jax.ShapeDtypeStruct((3, length, cols), BF),
            jax.ShapeDtypeStruct((length, width), BF),
        ],
        cost_estimate=pl.CostEstimate(
            flops=10 * length * width * cols,
            bytes_accessed=6 * length * width + 6 * width * cols,
            transcendentals=length * cols,
        ),
        name="ffn",
    )(normed, upstream, *pair, *down)


def down_kernel(copies, h_ref, *refs):
    out_ref = refs[-1]
    block = out_ref.shape[1] // copies
    for m in range(copies):
        weight = refs[m][...].reshape(block, h_ref.shape[2])
        out_ref[:, m * block : (m + 1) * block] = nt(h_ref[0], weight).astype(BF)


def down_rows(act, down, width, bq):
    _, length, cols = act.shape
    return pl.pallas_call(
        functools.partial(down_kernel, len(down)),
        grid=(length // bq,),
        in_specs=[pl.BlockSpec((1, bq, cols), lambda i: (2, i, 0))] + [whole(w) for w in down],
        out_specs=pl.BlockSpec((bq, width), lambda i: (i, 0)),
        out_shape=jax.ShapeDtypeStruct((length, width), BF),
        cost_estimate=pl.CostEstimate(
            flops=2 * length * width * cols,
            bytes_accessed=2 * length * width + 2 * width * cols,
            transcendentals=0,
        ),
        name="down",
    )(act, *down)


def grad_kernel(n_ref, u_ref, act_ref, out_ref):
    kind = pl.program_id(0)
    groups, _, rows, cols = out_ref.shape

    def emit(left):
        out_ref[...] = nn(left[...].T, act_ref[0]).astype(BF).reshape(groups, 1, rows, cols)

    @pl.when(kind < 2)
    def _():
        emit(n_ref)

    @pl.when(kind == 2)
    def _():
        emit(u_ref)


def ffn_grads(normed, upstream, act, m, copies, groups):
    length, width = normed.shape
    block = width // copies
    rows = block // groups
    cols = act.shape[2]
    side = pl.BlockSpec((length, block), lambda k: (0, m), pipeline_mode=pl.Buffered(1))
    return pl.pallas_call(
        grad_kernel,
        grid=(3,),
        in_specs=[side, side, pl.BlockSpec((1, length, cols), lambda k: (k, 0, 0))],
        out_specs=pl.BlockSpec((groups, 1, rows, cols), lambda k: (0, k, 0, 0)),
        out_shape=jax.ShapeDtypeStruct((groups, 3, rows, cols), BF),
        cost_estimate=pl.CostEstimate(
            flops=6 * length * block * cols,
            bytes_accessed=4 * length * block + 6 * length * cols + 6 * block * cols,
            transcendentals=0,
        ),
        name="gw",
    )(normed, upstream, act)


def unit_of(values):
    center = values - jnp.mean(values, axis=-1, keepdims=True)
    factor = lax.rsqrt(jnp.mean(center * center, axis=-1, keepdims=True) + EPSILON)
    return center * factor, factor


def norm_back(upstream, unit, factor, gain):
    scaled = upstream * gain
    return factor * (
        scaled
        - jnp.mean(scaled, axis=-1, keepdims=True)
        - unit * jnp.mean(scaled * unit, axis=-1, keepdims=True)
    )


def dot(left, right, dims):
    return lax.dot_general(left, right, (dims, ((), ())), preferred_element_type=F32)


NN = ((1,), (0,))
NT = ((1,), (1,))
TN = ((0,), (0,))


def own_rows(partial):
    return lax.psum_scatter(partial.astype(BF), SEQ, scatter_dimension=0, tiled=True).astype(F32)


def every(values):
    return lax.all_gather(values, SEQ, axis=0, tiled=True)


def chip_shift(values, k, groups):
    return lax.ppermute(values, SEQ, [(s, (s + 2 * k) % groups) for s in range(groups)])


def core_swap(values, groups):
    return lax.ppermute(values, SEQ, [(s, s ^ 1) for s in range(groups)])


def own_rows_beside(partial, me, groups):
    chips = groups // 2
    tokens = partial.shape[0] // groups
    blocks = partial.reshape(chips, 2, tokens, partial.shape[1])
    core = me % 2
    theirs = lax.dynamic_index_in_dim(blocks, 1 - core, 1, keepdims=False)
    ours = lax.dynamic_index_in_dim(blocks, core, 1, keepdims=False)
    moved = core_swap(theirs, groups)
    pair = (ours.astype(F32) + moved.astype(F32)).astype(BF)
    chip = me // 2
    moved = [
        chip_shift(lax.dynamic_index_in_dim(pair, (chip + k) % chips, 0, keepdims=False), k, groups)
        for k in range(1, chips)
    ]
    return [lax.dynamic_index_in_dim(pair, chip, 0, keepdims=False)] + moved


def layer(
    inputs,
    position,
    upstream,
    attn_gain,
    attn_shift,
    qkv_weight,
    qkv_bias,
    out_weight,
    ffn_gain,
    ffn_shift,
    gate_weight,
    up_weight,
    down_weight,
):
    tokens, width = inputs.shape
    groups = lax.axis_size(SEQ)
    copies = lax.axis_size(DP)
    me = lax.axis_index(SEQ)
    mine = lax.axis_index(DP)
    length = tokens * groups
    heads = HEADS // groups
    hc = heads * HD
    rows = qkv_weight.shape[0]
    nbias = qkv_bias.shape[0]
    bq = 256

    own = relate(inputs, mine, copies, 1)
    own_up = relate(upstream, mine, copies, 1)
    up_all = every(own_up)

    def by_group(weight, parts=1):
        cols = weight.shape[1] // (parts * groups)
        view = weight.reshape(rows, parts, groups, cols).transpose(2, 0, 1, 3)
        return view.reshape(groups, rows, parts * cols)

    small = jnp.concatenate(
        [
            attn_gain,
            attn_shift,
            ffn_gain,
            ffn_shift,
            qkv_bias,
            (position // 256).astype(BF),
            (position % 256).astype(BF),
        ]
    )
    extra = jnp.zeros((8, 3 * hc), BF).at[0, : small.shape[0]].set(small)
    view_qkv = jnp.concatenate(
        [by_group(qkv_weight, 3), jnp.broadcast_to(extra[None], (groups, 8, 3 * hc))], axis=1
    )
    taken, own = lax.optimization_barrier((take(view_qkv), own))
    x_all = every(own)
    pieces_qkv = spread(taken)
    weight_qkv = stack_rows(pieces_qkv, 0, rows)
    weight_out = stack_rows(spread(take(by_group(out_weight))), 0, rows)
    spot = pieces_qkv[0][:, rows, 4 * rows + nbias : 4 * rows + nbias + 2 * tokens]
    positions = (
        spot[:, :tokens].astype(jnp.int32) * 256 + spot[:, tokens:].astype(jnp.int32)
    ).reshape(length)
    everyone = jnp.stack([p[:, rows, : 4 * rows + nbias] for p in pieces_qkv]).astype(F32)
    gain_one, shift_one, gain_two, shift_two = [
        everyone[:, :, n * rows : (n + 1) * rows].reshape(1, width) for n in range(4)
    ]
    bias_full = relate(everyone[:, :, 4 * rows :].reshape(-1), mine, copies, 0)
    chosen = (jnp.arange(groups, dtype=jnp.int32) == me).astype(F32)
    bias_mine = jnp.sum(bias_full.reshape(3, groups, hc) * chosen[None, :, None], axis=1).reshape(1, -1)

    tables = rotary_rows(positions)
    lowest = jnp.arange(length, dtype=jnp.int32) - positions
    low8 = jnp.broadcast_to(lowest[None], (8, length))
    first = (jnp.min(lowest.reshape(length // bq, bq), axis=1) // bq).astype(jnp.int32)

    view_gu = jnp.concatenate([by_group(gate_weight), by_group(up_weight)], axis=1)
    view_gu, view_down, x_all = lax.optimization_barrier((view_gu, by_group(down_weight), x_all))
    pieces_gu = spread(take(view_gu))
    pieces_down = spread(take(view_down))

    unit_all, unused = unit_of(x_all.astype(F32))
    normed_one = (unit_all * gain_one + shift_one).astype(BF)
    projected = dot(normed_one, weight_qkv, NN) + bias_mine
    qkv, context, lse = attend_fwd(projected, tables, low8, first, heads, bq)
    flat = own.astype(F32)
    middle = flat + own_rows(dot(context, weight_out, NT))
    unit_two, factor_two = unit_of(middle)
    normed_two = (unit_two * gain_two + shift_two).astype(BF)
    normed_two = every(normed_two)
    act, dx = ffn_both(normed_two, up_all, pieces_gu, pieces_down, rows, bq)
    grad_normed_two = own_rows(dx)
    down_part = down_rows(act, pieces_down, width, bq)
    block = width // copies

    def by_owner(left, right):
        return [
            dot(left[:, m * block : (m + 1) * block], right, TN).astype(BF).reshape(groups, rows, -1)
            for m in range(copies)
        ]

    grads = [None] * copies
    for m in [*range(1, copies), 0]:
        grads[m] = ffn_grads(normed_two, up_all, act, m, copies, groups)
    sum_ffn = reduce_dp(grads).reshape(groups, 3 * rows, -1)
    sum_ffn = send_back(sum_ffn).transpose(1, 0, 2)

    grad_middle = own_up.astype(F32) + norm_back(grad_normed_two, unit_two, factor_two, gain_two)
    grad_mixed = grad_middle.astype(BF)
    down_sum = own_rows_beside(down_part, me, groups)
    grad_mixed = every(grad_mixed)
    grad_context = dot(grad_mixed, weight_out, NN).astype(BF)
    grad_projected, bias_part = attend_bwd(qkv, context, lse, grad_context, tables, low8, first, heads, bq)
    dqkv = dot(grad_projected, weight_qkv, NT).astype(BF)
    grad_normed_one = own_rows(dqkv)

    late, unused = lax.optimization_barrier((down_sum[0], bias_part))
    total = late.astype(F32)
    for piece in down_sum[1:]:
        total = total + piece.astype(F32)
    output = (middle + total).astype(BF)

    bias_part = jnp.sum(bias_part, axis=0).reshape(3, 1, hc) * chosen[None, :, None]
    bias_part = relate(bias_part.reshape(-1), mine, copies, 0).reshape(copies, groups, nbias)
    parts = [
        jnp.sum(dqkv.astype(F32) * unit_all, axis=0),
        jnp.sum(dqkv.astype(F32), axis=0),
        jnp.sum(grad_normed_two * unit_two, axis=0),
        jnp.sum(grad_normed_two, axis=0),
    ]
    parts = [p.reshape(copies, groups, 1, rows) for p in parts] + [bias_part[:, :, None]]
    parts = jnp.concatenate(parts, axis=3)
    parts = jnp.pad(parts, ((0, 0), (0, 0), (0, 7), (0, 3 * hc - parts.shape[3]))).astype(BF)

    sum_out = reduce_dp(by_owner(grad_mixed, context))
    grad_qkv_weight = by_owner(normed_one, grad_projected)
    sum_qkv = reduce_dp([jnp.concatenate([grad_qkv_weight[m], parts[m]], axis=1) for m in range(copies)])
    sum_attn = jnp.concatenate([sum_qkv, jnp.pad(sum_out, ((0, 0), (0, 8), (0, 0)))], axis=2)
    sum_attn = send_back(sum_attn)
    total = jnp.sum(sum_attn[:, rows].astype(F32), axis=0)
    sums = [total[n * rows : (n + 1) * rows] for n in range(4)] + [total[4 * rows : 4 * rows + nbias]]
    sum_attn = sum_attn[:, :rows].transpose(1, 0, 2)
    sum_qkv = sum_attn[:, :, : 3 * hc]
    sum_out = sum_attn[:, :, 3 * hc :]
    unit_one, factor_one = unit_of(flat)
    grad_input = grad_middle + norm_back(grad_normed_one, unit_one, factor_one, gain_one)

    def wide(value):
        return value.astype(F32).reshape(rows, -1)

    wide_qkv = sum_qkv.reshape(rows, groups, 3, hc).transpose(0, 2, 1, 3)
    return (
        relate(output, mine, copies, 1)[None],
        relate(grad_input, mine, copies, 1)[None],
        sums[0],
        sums[1],
        wide(wide_qkv),
        sums[4],
        wide(sum_out),
        sums[2],
        sums[3],
        wide(sum_ffn[:rows]),
        wide(sum_ffn[rows : 2 * rows]),
        wide(sum_ffn[2 * rows :]),
    )


def local(
    residual_in,
    attn_gain,
    attn_shift,
    qkv_weight,
    qkv_bias,
    out_weight,
    ffn_gain,
    ffn_shift,
    gate_weight,
    up_weight,
    down_weight,
    positions,
    cotangent,
):
    return layer(
        residual_in[0],
        positions[0],
        cotangent[0],
        attn_gain,
        attn_shift,
        qkv_weight,
        qkv_bias,
        out_weight,
        ffn_gain,
        ffn_shift,
        gate_weight,
        up_weight,
        down_weight,
    )


def solution(mesh):
    both = (DP, SEQ)
    in_specs = (
        P(DP, SEQ, None),
        P(both),
        P(both),
        P(both, None),
        P(both),
        P(both, None),
        P(both),
        P(both),
        P(both, None),
        P(both, None),
        P(both, None),
        P(DP, SEQ),
        P(DP, SEQ, None),
    )
    out_specs = (
        P(DP, SEQ, None),
        P(DP, SEQ, None),
        P(both),
        P(both),
        P(both, None),
        P(both),
        P(both, None),
        P(both),
        P(both),
        P(both, None),
        P(both, None),
        P(both, None),
    )
    return jax.shard_map(local, mesh=mesh, in_specs=in_specs, out_specs=out_specs, check_vma=False)
```

```python
import functools

import jax
import jax.numpy as jnp
from jax import lax
from jax.experimental import pallas as pl
from jax.experimental.pallas import tpu as pltpu
from jax.sharding import PartitionSpec as P


HEADS = 32
HD = 64
ROT = 16
LANES = 128
EPSILON = 1e-05
ROPE_BASE = 10000.0
MASKED = -1e30
BF = jnp.bfloat16
F32 = jnp.float32

DP = "dp"
SEQ = "seq"


def rotary_rows(position):
    lane = jnp.arange(LANES, dtype=jnp.int32) % HD
    half = ROT // 2
    power = ROPE_BASE ** (-(lane % half).astype(F32) * (2.0 / ROT))
    freq = jnp.where(lane < ROT, power, 0.0)
    angle = position.astype(F32)[:, None] * freq[None, :]
    cosine = jnp.cos(angle); sine = jnp.sin(angle)
    first = jnp.where(lane < half, -sine, 0.0)
    second = jnp.where((lane >= half) & (lane < ROT), sine, 0.0)
    return cosine, first, second


def turn(x, cosine, first, second):
    return x * cosine + pltpu.roll(x, LANES - ROT // 2, 1) * first + pltpu.roll(x, ROT // 2, 1) * second


def head_mask(x, h):
    lane = lax.broadcasted_iota(jnp.int32, x.shape, 1)
    return jnp.where((lane >= h * HD) & (lane < (h + 1) * HD), x, jnp.zeros_like(x))


def nt(a, b):
    return lax.dot_general(a, b, (((1,), (1,)), ((), ())), preferred_element_type=F32)


def nn(a, b):
    return lax.dot_general(a, b, (((1,), (0,)), ((), ())), preferred_element_type=F32)


def block_bias(i, j, bq, low_row):
    key = j * bq + lax.broadcasted_iota(jnp.int32, (bq, bq), 0)
    query = i * bq + lax.broadcasted_iota(jnp.int32, (bq, bq), 1)
    return jnp.where((key <= query) & (key >= low_row), 0.0, MASKED)


def fwd_kernel(heads, bq, rows, first_ref, low_ref, cos_ref, s1_ref, s2_ref, x_ref, gain_ref, shift_ref, add_ref, *refs):
    weights = refs[:-7]
    norm_ref, qkv_ref, ctx_ref, lse_ref, k_s, vt_s, st_s = refs[-7:]
    i = pl.program_id(0)
    hc = heads * HD
    x = x_ref[...].astype(F32)
    center = x - jnp.mean(x, axis=-1, keepdims=True)
    factor = lax.rsqrt(jnp.mean(center * center, axis=-1, keepdims=True) + EPSILON)
    normed = (center * factor * gain_ref[...] + shift_ref[...]).astype(BF)
    norm_ref[...] = normed
    proj = add_ref[...]
    size = x_ref.shape[1] // len(weights)
    for n, weight in enumerate(weights):
        part = weight[:, :rows, :].reshape(size, 3 * hc)
        proj = proj + nn(normed[:, n * size:(n + 1) * size], part)
    c, s1, s2 = cos_ref[...], s1_ref[...], s2_ref[...]
    parts = []
    for base in (0, hc):
        for t in range(hc // LANES):
            x = proj[:, base + t * LANES: base + (t + 1) * LANES]
            parts.append(turn(x, c, s1, s2).astype(BF))
    n = hc // LANES
    q = jnp.concatenate(parts[:n], axis=1) if n > 1 else parts[0]
    k = jnp.concatenate(parts[n:], axis=1) if n > 1 else parts[n]
    v32 = proj[:, 2 * hc:]
    v = v32.astype(BF)
    qkv_ref[:, :hc] = q
    qkv_ref[:, hc:2 * hc] = k
    qkv_ref[:, 2 * hc:] = v
    rows = pl.ds(pl.multiple_of(i * bq, bq), bq)
    k_s[rows, :] = k
    vt_s[:, rows] = v32.T.astype(BF)
    low = low_ref[0:1, :]
    qm = [head_mask(q, h) for h in range(heads)]
    first = first_ref[i]

    def score_step(j, tops):
        kj = k_s[pl.ds(pl.multiple_of(j * bq, bq), bq), :]
        bias = block_bias(i, j, bq, low)
        out = []
        for h in range(heads):
            s = nt(kj, qm[h]) * 0.125 + bias
            st_s[h, pl.ds(pl.multiple_of(j * bq, bq), bq), :] = s
            out.append(jnp.maximum(tops[h], jnp.max(s.reshape(bq // 8, 8, bq), axis=0)))
        return tuple(out)

    tops = lax.fori_loop(first, i + 1, score_step,
                         tuple(jnp.full((8, bq), MASKED, F32) for _ in range(heads)))
    tops = [jnp.max(t, axis=0, keepdims=True) for t in tops]

    def value_step(j, state):
        new = []
        vt = vt_s[:, pl.ds(pl.multiple_of(j * bq, bq), bq)]
        for h in range(heads):
            tot, acc = state[h]
            p = jnp.exp(st_s[h, pl.ds(pl.multiple_of(j * bq, bq), bq), :] - tops[h])
            tot = tot + jnp.sum(p.reshape(bq // 8, 8, bq), axis=0)
            acc = acc + nn(vt[h * HD:(h + 1) * HD, :], p.astype(BF))
            new.append((tot, acc))
        return tuple(new)

    state = lax.fori_loop(first, i + 1, value_step,
                          tuple((jnp.zeros((8, bq), F32), jnp.zeros((HD, bq), F32)) for _ in range(heads)))
    outs = []
    lses = []
    for h in range(heads):
        tot, acc = state[h]
        tot = jnp.sum(tot, axis=0, keepdims=True)
        outs.append(acc / tot)
        lses.append(tops[h] + jnp.log(tot))
    ctx_ref[...] = jnp.concatenate(outs, axis=0).T.astype(BF)
    pad = [jnp.zeros((8 - heads, bq), F32)] if heads < 8 else []
    lse_ref[...] = jnp.concatenate(lses + pad, axis=0)


def attend_fwd(x, gain, shift, add, weights, rows, tables, low8, first, heads, bq):
    T, width = x.shape; hc = heads * HD
    row = lambda w: pl.BlockSpec((bq, w), lambda i, f: (i, 0))
    return pl.pallas_call(
        functools.partial(fwd_kernel, heads, bq, rows),
        grid_spec=pltpu.PrefetchScalarGridSpec(
            num_scalar_prefetch=1, grid=(T // bq,),
            in_specs=[pl.BlockSpec((8, bq), lambda i, f: (0, i)), row(LANES), row(LANES), row(LANES), row(width)]
            + [whole(w) for w in (gain, shift, add, *weights)],
            out_specs=[row(width), row(3 * hc), row(hc), pl.BlockSpec((8, bq), lambda i, f: (0, i))],
            scratch_shapes=[pltpu.VMEM((T, hc), BF), pltpu.VMEM((hc, T), BF), pltpu.VMEM((heads, T, bq), F32)]),
        out_shape=[jax.ShapeDtypeStruct((T, width), BF), jax.ShapeDtypeStruct((T, 3 * hc), BF),
                   jax.ShapeDtypeStruct((T, hc), BF), jax.ShapeDtypeStruct((8, T), F32)],
        cost_estimate=pl.CostEstimate(flops=4 * T * T * hc + 6 * T * width * hc, bytes_accessed=T * hc * 24 + 4 * T * width,
                                      transcendentals=T * T * heads // 2),
        name="af",
    )(first, low8, *tables, x, gain, shift, add, *weights)


def bwd_kernel(heads, bq, count, first_ref, low_ref, cos_ref, s1_ref, s2_ref, qkv_ref, ctx_ref, lse_ref, gc_ref,
               gp_ref, bias_ref, dk_s, dv_s, dq_s):
    step = pl.program_id(0)
    i = count - 1 - step
    hc = heads * HD
    rows = pl.ds(pl.multiple_of(i * bq, bq), bq)

    @pl.when(step == 0)
    def _():
        dk_s[...] = jnp.zeros_like(dk_s)
        dv_s[...] = jnp.zeros_like(dv_s)
        bias_ref[...] = jnp.zeros_like(bias_ref)

    low = low_ref[0:1, rows]
    q = qkv_ref[rows, :hc]
    g = gc_ref[rows, :]
    prod = (g.astype(F32) * ctx_ref[rows, :].astype(F32)).T
    deltas = [jnp.sum(prod[h * HD:(h + 1) * HD, :], axis=0, keepdims=True) for h in range(heads)]
    lses = [lse_ref[h:h + 1, rows] for h in range(heads)]
    qm = [head_mask(q, h) for h in range(heads)]
    gm = [head_mask(g, h) for h in range(heads)]
    dq_s[...] = jnp.zeros_like(dq_s)

    @pl.loop(first_ref[i], i + 1)
    def _(j):
        cols = pl.ds(pl.multiple_of(j * bq, bq), bq)
        kj = qkv_ref[cols, hc:2 * hc]
        vj = qkv_ref[cols, 2 * hc:]
        kt = kj.T
        bias = block_bias(i, j, bq, low)
        dk = dk_s[cols, :]
        dv = dv_s[cols, :]
        for h in range(heads):
            s = nt(kj, qm[h]) * 0.125 + bias
            p = jnp.exp(s - lses[h])
            dp = nt(vj, gm[h])
            ds = (p * (dp - deltas[h]) * 0.125).astype(BF)
            dv = dv + nn(p.astype(BF), gm[h])
            dk = dk + nn(ds, qm[h])
            dq_s[h * HD:(h + 1) * HD, :] += nn(kt[h * HD:(h + 1) * HD, :], ds)
        dk_s[cols, :] = dk
        dv_s[cols, :] = dv

    c, s1, s2 = cos_ref[rows, :], s1_ref[rows, :], s2_ref[rows, :]
    dq = dq_s[...].T
    dk = dk_s[rows, :]
    dv = dv_s[rows, :]

    def emit(x, base):
        gp_ref[:, base: base + x.shape[1]] = x.astype(BF)
        bias_ref[:, base: base + x.shape[1]] += jnp.sum(x.reshape(bq // 8, 8, x.shape[1]), axis=0)

    for src, base in ((dq, 0), (dk, hc)):
        for t in range(hc // LANES):
            emit(turn(src[:, t * LANES:(t + 1) * LANES], c, -s1, -s2), base + t * LANES)
    emit(dv, 2 * hc)


def attend_bwd(qkv, ctx, lse, gc, tables, low8, first, heads, bq):
    T = qkv.shape[0]; hc = heads * HD; count = T // bq
    full = lambda r, w: pl.BlockSpec((r, w), lambda i, f: (0, 0))
    return pl.pallas_call(
        functools.partial(bwd_kernel, heads, bq, count),
        grid_spec=pltpu.PrefetchScalarGridSpec(
            num_scalar_prefetch=1, grid=(count,),
            in_specs=[full(8, T), full(T, LANES), full(T, LANES), full(T, LANES), full(T, 3 * hc), full(T, hc), full(8, T), full(T, hc)],
            out_specs=[pl.BlockSpec((bq, 3 * hc), lambda i, f: (count - 1 - i, 0)), full(8, 3 * hc)],
            scratch_shapes=[pltpu.VMEM((T, hc), F32), pltpu.VMEM((T, hc), F32), pltpu.VMEM((hc, bq), F32)]),
        out_shape=[jax.ShapeDtypeStruct((T, 3 * hc), BF), jax.ShapeDtypeStruct((8, 3 * hc), F32)],
        cost_estimate=pl.CostEstimate(flops=5 * T * T * hc * 2, bytes_accessed=T * hc * 24, transcendentals=T * T * heads // 2),
        name="ab",
    )(first, low8, *tables, qkv, ctx, lse, gc)


def relate(values, mine, count, axis):
    size = values.shape[axis] // count
    bit = 1
    while bit < count:
        order = [m ^ bit for m in range(count)]
        swapped = jnp.concatenate(
            [lax.slice_in_dim(values, m * size, (m + 1) * size, axis=axis) for m in order], axis=axis
        )
        values = jnp.where((mine & bit) != 0, swapped, values)
        bit *= 2
    return values


def swap_dp(values, rel):
    return lax.ppermute(values, DP, [(d, d ^ rel) for d in range(lax.axis_size(DP))])


def take(view):
    return lax.all_to_all(view, SEQ, split_axis=0, concat_axis=0, tiled=True)


def spread(mine):
    return [mine] + [swap_dp(mine, rel) for rel in range(1, lax.axis_size(DP))]


def spread_halves(mine):
    half = mine.shape[0] // 2
    count = lax.axis_size(DP)
    bits = [1 << n for n in range(count.bit_length() - 1)]
    low, high = {0: mine[:half]}, {0: mine[half:]}
    for one, other in zip(bits, bits[::-1]):
        low.update({rel ^ one: swap_dp(piece, one) for rel, piece in list(low.items())})
        high.update({rel ^ other: swap_dp(piece, other) for rel, piece in list(high.items())})
    return [(low[rel], high[rel]) for rel in range(count)]


def stack_rows(pieces, start, size):
    cols = pieces[0].shape[2]
    return jnp.concatenate([p[:, start : start + size] for p in pieces], axis=0).reshape(-1, cols)


def reduce_dp(parts):
    total = parts[0].astype(F32)
    moved = [swap_dp(parts[rel], rel) for rel in range(1, len(parts))]
    for piece in moved:
        total = total + piece.astype(F32)
    return total.astype(BF)


def send_back(summed):
    return lax.all_to_all(summed, SEQ, split_axis=0, concat_axis=0, tiled=True)


def ffn_kernel(copies, rows, n_ref, u_ref, *refs):
    pair, down, (act_ref, dx_ref) = refs[:copies], refs[copies : 2 * copies], refs[2 * copies :]
    block = n_ref.shape[1] // copies
    cols = pair[0].shape[2]

    def gate_rows(m):
        return pair[m][:, :rows, :].reshape(block, cols)

    def up_rows(m):
        return pair[m][:, rows:, :].reshape(block, cols)

    gate = upward = grad = 0.0
    for m in range(copies):
        span = slice(m * block, (m + 1) * block)
        gate = gate + nn(n_ref[:, span], gate_rows(m))
        upward = upward + nn(n_ref[:, span], up_rows(m))
        grad = grad + nn(u_ref[:, span], down[m][...].reshape(block, cols))
    sig = jax.nn.sigmoid(gate)
    silu = gate * sig
    grad_gate = (grad * upward * sig * (1.0 + gate * (1.0 - sig))).astype(BF)
    grad_up = (grad * silu).astype(BF)
    act_ref[0] = grad_gate
    act_ref[1] = grad_up
    act_ref[2] = (silu * upward).astype(BF)
    for m in range(copies):
        part = nt(grad_gate, gate_rows(m)) + nt(grad_up, up_rows(m))
        dx_ref[:, m * block : (m + 1) * block] = part.astype(BF)


def whole(array):
    zero = (0,) * array.ndim
    return pl.BlockSpec(array.shape, lambda *i: zero, pipeline_mode=pl.Buffered(1))


def ffn_both(normed, upstream, pair, down, rows, bq):
    length, width = normed.shape
    cols = down[0].shape[2]
    row = pl.BlockSpec((bq, width), lambda i: (i, 0))
    return pl.pallas_call(
        functools.partial(ffn_kernel, len(pair), rows),
        grid=(length // bq,),
        in_specs=[row, row] + [whole(w) for w in pair + down],
        out_specs=[pl.BlockSpec((3, bq, cols), lambda i: (0, i, 0)), row],
        out_shape=[
            jax.ShapeDtypeStruct((3, length, cols), BF),
            jax.ShapeDtypeStruct((length, width), BF),
        ],
        cost_estimate=pl.CostEstimate(
            flops=10 * length * width * cols,
            bytes_accessed=6 * length * width + 6 * width * cols,
            transcendentals=length * cols,
        ),
        name="ffn",
    )(normed, upstream, *pair, *down)


def back_kernel(rows, x_ref, *refs):
    weights, out_ref = refs[:-1], refs[-1]
    cols = weights[0].shape[2]
    size = out_ref.shape[1] // len(weights)
    x = x_ref[...].reshape(out_ref.shape[0], cols)
    for n, weight in enumerate(weights):
        part = weight[:, :rows, :].reshape(size, cols)
        out_ref[:, n * size : (n + 1) * size] = nt(x, part).astype(BF)


def back_rows(x, kind, weights, rows, width, bq):
    _, length, cols = x.shape
    return pl.pallas_call(
        functools.partial(back_kernel, rows),
        grid=(length // bq,),
        in_specs=[pl.BlockSpec((1, bq, cols), lambda i: (kind, i, 0))] + [whole(w) for w in weights],
        out_specs=pl.BlockSpec((bq, width), lambda i: (i, 0)),
        out_shape=jax.ShapeDtypeStruct((length, width), BF),
        cost_estimate=pl.CostEstimate(
            flops=2 * length * width * cols,
            bytes_accessed=2 * length * width + 2 * width * cols,
            transcendentals=0,
        ),
        name="back",
    )(x, *weights)


def grad_kernel(n_ref, u_ref, act_ref, out_ref):
    kind = pl.program_id(0)
    groups, _, rows, cols = out_ref.shape

    def emit(left):
        out_ref[...] = nn(left[...].T, act_ref[0]).astype(BF).reshape(groups, 1, rows, cols)

    @pl.when(kind < 2)
    def _():
        emit(n_ref)

    @pl.when(kind == 2)
    def _():
        emit(u_ref)


def ffn_grads(normed, upstream, act, m, copies, groups):
    length, width = normed.shape
    block = width // copies
    rows = block // groups
    cols = act.shape[2]
    side = pl.BlockSpec((length, block), lambda k: (0, m), pipeline_mode=pl.Buffered(1))
    return pl.pallas_call(
        grad_kernel,
        grid=(3,),
        in_specs=[side, side, pl.BlockSpec((1, length, cols), lambda k: (k, 0, 0))],
        out_specs=pl.BlockSpec((groups, 1, rows, cols), lambda k: (0, k, 0, 0)),
        out_shape=jax.ShapeDtypeStruct((groups, 3, rows, cols), BF),
        cost_estimate=pl.CostEstimate(
            flops=6 * length * block * cols,
            bytes_accessed=4 * length * block + 6 * length * cols + 6 * block * cols,
            transcendentals=0,
        ),
        name="gw",
    )(normed, upstream, act)


def wide_kernel(parts, back_ref, *outs):
    rows = outs[0].shape[0]
    groups = back_ref.shape[0]
    for out, pieces in zip(outs, parts):
        for start, at, cols, base, step in pieces:
            for s in range(groups):
                value = back_ref[s, start : start + rows, at : at + cols]
                out[:, base + s * step : base + s * step + cols] = value.astype(F32)


def widen(back, rows, parts):
    groups = back.shape[0]
    shapes = [jax.ShapeDtypeStruct((rows, groups * sum(p[2] for p in pieces)), F32) for pieces in parts]
    return pl.pallas_call(
        functools.partial(wide_kernel, parts),
        out_shape=shapes,
        cost_estimate=pl.CostEstimate(flops=0, bytes_accessed=3 * back.size * 2, transcendentals=0),
        name="wide",
    )(back)


def unit_of(values):
    center = values - jnp.mean(values, axis=-1, keepdims=True)
    factor = lax.rsqrt(jnp.mean(center * center, axis=-1, keepdims=True) + EPSILON)
    return center * factor, factor


def norm_back(upstream, unit, factor, gain):
    scaled = upstream * gain
    return factor * (
        scaled
        - jnp.mean(scaled, axis=-1, keepdims=True)
        - unit * jnp.mean(scaled * unit, axis=-1, keepdims=True)
    )


def dot(left, right, dims):
    return lax.dot_general(left, right, (dims, ((), ())), preferred_element_type=F32)


NN = ((1,), (0,))
NT = ((1,), (1,))
TN = ((0,), (0,))


def own_rows(partial):
    return lax.psum_scatter(partial.astype(BF), SEQ, scatter_dimension=0, tiled=True).astype(F32)


def every(values):
    return lax.all_gather(values, SEQ, axis=0, tiled=True)


def chip_shift(values, k, groups):
    return lax.ppermute(values, SEQ, [(s, (s + 2 * k) % groups) for s in range(groups)])


def core_swap(values, groups):
    return lax.ppermute(values, SEQ, [(s, s ^ 1) for s in range(groups)])


def own_rows_beside(partial, me, groups):
    chips = groups // 2
    tokens = partial.shape[0] // groups
    blocks = partial.reshape(chips, 2, tokens, partial.shape[1])
    core = me % 2
    theirs = lax.dynamic_index_in_dim(blocks, 1 - core, 1, keepdims=False)
    ours = lax.dynamic_index_in_dim(blocks, core, 1, keepdims=False)
    moved = core_swap(theirs, groups)
    pair = (ours.astype(F32) + moved.astype(F32)).astype(BF)
    chip = me // 2
    moved = [
        chip_shift(lax.dynamic_index_in_dim(pair, (chip + k) % chips, 0, keepdims=False), k, groups)
        for k in range(1, chips)
    ]
    return [lax.dynamic_index_in_dim(pair, chip, 0, keepdims=False)] + moved


def layer(
    inputs,
    position,
    upstream,
    attn_gain,
    attn_shift,
    qkv_weight,
    qkv_bias,
    out_weight,
    ffn_gain,
    ffn_shift,
    gate_weight,
    up_weight,
    down_weight,
):
    tokens, width = inputs.shape
    groups = lax.axis_size(SEQ)
    copies = lax.axis_size(DP)
    me = lax.axis_index(SEQ)
    mine = lax.axis_index(DP)
    length = tokens * groups
    heads = HEADS // groups
    hc = heads * HD
    rows = qkv_weight.shape[0]
    nbias = qkv_bias.shape[0]
    bq = 256

    own = relate(inputs, mine, copies, 1)
    own_up = relate(upstream, mine, copies, 1)

    def by_group(weight, parts=1):
        cols = weight.shape[1] // (parts * groups)
        view = weight.reshape(rows, parts, groups, cols).transpose(2, 0, 1, 3)
        return view.reshape(groups, rows, parts * cols)

    small = jnp.concatenate(
        [
            attn_gain,
            attn_shift,
            ffn_gain,
            ffn_shift,
            qkv_bias,
            (position // 256).astype(BF),
            (position % 256).astype(BF),
        ]
    )
    extra = jnp.zeros((8, 3 * hc), BF).at[0, : small.shape[0]].set(small)
    view_qkv = jnp.concatenate(
        [by_group(qkv_weight, 3), jnp.broadcast_to(extra[None], (groups, 8, 3 * hc))], axis=1
    )
    taken, own = lax.optimization_barrier((take(view_qkv), own))
    x_all = every(own)
    pieces_qkv = [piece for pair in spread_halves(taken) for piece in pair]
    own_up, unused = lax.optimization_barrier((own_up, taken))
    up_all = every(own_up)
    weight_out = stack_rows(spread(take(by_group(out_weight))), 0, rows)
    spot = taken[:, rows, 4 * rows + nbias : 4 * rows + nbias + 2 * tokens]
    positions = (
        spot[:, :tokens].astype(jnp.int32) * 256 + spot[:, tokens:].astype(jnp.int32)
    ).reshape(length)
    everyone = jnp.concatenate([p[:, rows, : 4 * rows + nbias] for p in pieces_qkv]).astype(F32)
    everyone = everyone.reshape(copies, groups, -1)
    gain_one, shift_one, gain_two, shift_two = [
        everyone[:, :, n * rows : (n + 1) * rows].reshape(1, width) for n in range(4)
    ]
    bias_full = relate(everyone[:, :, 4 * rows :].reshape(-1), mine, copies, 0)
    chosen = (jnp.arange(groups, dtype=jnp.int32) == me).astype(F32)
    bias_mine = jnp.sum(bias_full.reshape(3, groups, hc) * chosen[None, :, None], axis=1).reshape(1, -1)

    tables = rotary_rows(positions)
    lowest = jnp.arange(length, dtype=jnp.int32) - positions
    low8 = jnp.broadcast_to(lowest[None], (8, length))
    first = (jnp.min(lowest.reshape(length // bq, bq), axis=1) // bq).astype(jnp.int32)

    view_gu = jnp.concatenate([by_group(gate_weight), by_group(up_weight)], axis=1)
    view_gu, view_down, x_all = lax.optimization_barrier((view_gu, by_group(down_weight), x_all))
    pieces_gu = spread(take(view_gu))
    pieces_down = spread(take(view_down))

    normed_one, qkv, context, lse = attend_fwd(
        x_all, gain_one, shift_one, bias_mine, pieces_qkv, rows, tables, low8, first, heads, bq
    )
    flat = own.astype(F32)
    middle = flat + own_rows(dot(context, weight_out, NT))
    unit_two, factor_two = unit_of(middle)
    normed_two = (unit_two * gain_two + shift_two).astype(BF)
    normed_two = every(normed_two)
    act, dx = ffn_both(normed_two, up_all, pieces_gu, pieces_down, rows, bq)
    grad_normed_two = own_rows(dx)
    down_part = back_rows(act, 2, pieces_down, rows, width, bq)
    block = width // copies

    def by_owner(left, right):
        return [
            dot(left[:, m * block : (m + 1) * block], right, TN).astype(BF).reshape(groups, rows, -1)
            for m in range(copies)
        ]

    grads = [None] * copies
    for m in [*range(1, copies), 0]:
        grads[m] = ffn_grads(normed_two, up_all, act, m, copies, groups)
    sum_ffn = reduce_dp(grads).reshape(groups, 3 * rows, -1)
    sum_ffn = send_back(sum_ffn)

    grad_middle = own_up.astype(F32) + norm_back(grad_normed_two, unit_two, factor_two, gain_two)
    grad_mixed = grad_middle.astype(BF)
    down_sum = own_rows_beside(down_part, me, groups)
    grad_mixed = every(grad_mixed)
    grad_context = dot(grad_mixed, weight_out, NN).astype(BF)
    grad_projected, bias_part = attend_bwd(qkv, context, lse, grad_context, tables, low8, first, heads, bq)
    dqkv = back_rows(grad_projected[None], 0, pieces_qkv, rows, width, bq)
    grad_normed_one = own_rows(dqkv)

    late, unused = lax.optimization_barrier((down_sum[0], bias_part))
    total = late.astype(F32)
    for piece in down_sum[1:]:
        total = total + piece.astype(F32)
    output = (middle + total).astype(BF)

    grad_qkv_weight = by_owner(normed_one, grad_projected)
    x_late, unused = lax.optimization_barrier((x_all, grad_qkv_weight[0]))
    unit_all, unused = unit_of(x_late.astype(F32))
    bias_part = jnp.sum(bias_part, axis=0).reshape(3, 1, hc) * chosen[None, :, None]
    bias_part = relate(bias_part.reshape(-1), mine, copies, 0).reshape(copies, groups, nbias)
    parts = [
        jnp.sum(dqkv.astype(F32) * unit_all, axis=0),
        jnp.sum(dqkv.astype(F32), axis=0),
        jnp.sum(grad_normed_two * unit_two, axis=0),
        jnp.sum(grad_normed_two, axis=0),
    ]
    parts = [p.reshape(copies, groups, 1, rows) for p in parts] + [bias_part[:, :, None]]
    parts = jnp.concatenate(parts, axis=3)
    parts = jnp.pad(parts, ((0, 0), (0, 0), (0, 0), (0, 8 * hc - parts.shape[3]))).astype(BF)
    parts = parts.reshape(copies, groups, 8, hc)

    sum_qkv = reduce_dp(grad_qkv_weight)
    grad_out_weight = by_owner(grad_mixed, context)
    sum_out = reduce_dp([jnp.concatenate([grad_out_weight[m], parts[m]], axis=1) for m in range(copies)])
    sum_attn = jnp.concatenate([jnp.pad(sum_qkv, ((0, 0), (0, 8), (0, 0))), sum_out], axis=2)
    sum_attn = send_back(sum_attn)
    total = jnp.sum(sum_attn[:, rows:, 3 * hc :].astype(F32), axis=0).reshape(-1)
    sums = [total[n * rows : (n + 1) * rows] for n in range(4)] + [total[4 * rows : 4 * rows + nbias]]
    wide_qkv, wide_out = widen(
        sum_attn,
        rows,
        (tuple((0, n * hc, hc, n * width, hc) for n in range(3)), ((0, 3 * hc, hc, 0, hc),)),
    )
    unit_one, factor_one = unit_of(flat)
    grad_input = grad_middle + norm_back(grad_normed_one, unit_one, factor_one, gain_one)

    cols = sum_ffn.shape[2]
    wide_gate, wide_up, wide_down = widen(
        sum_ffn, rows, tuple(((n * rows, 0, cols, 0, cols),) for n in range(3))
    )
    return (
        relate(output, mine, copies, 1)[None],
        relate(grad_input, mine, copies, 1)[None],
        sums[0],
        sums[1],
        wide_qkv,
        sums[4],
        wide_out,
        sums[2],
        sums[3],
        wide_gate,
        wide_up,
        wide_down,
    )


def local(
    residual_in,
    attn_gain,
    attn_shift,
    qkv_weight,
    qkv_bias,
    out_weight,
    ffn_gain,
    ffn_shift,
    gate_weight,
    up_weight,
    down_weight,
    positions,
    cotangent,
):
    return layer(
        residual_in[0],
        positions[0],
        cotangent[0],
        attn_gain,
        attn_shift,
        qkv_weight,
        qkv_bias,
        out_weight,
        ffn_gain,
        ffn_shift,
        gate_weight,
        up_weight,
        down_weight,
    )


def solution(mesh):
    both = (DP, SEQ)
    in_specs = (
        P(DP, SEQ, None),
        P(both),
        P(both),
        P(both, None),
        P(both),
        P(both, None),
        P(both),
        P(both),
        P(both, None),
        P(both, None),
        P(both, None),
        P(DP, SEQ),
        P(DP, SEQ, None),
    )
    out_specs = (
        P(DP, SEQ, None),
        P(DP, SEQ, None),
        P(both),
        P(both),
        P(both, None),
        P(both),
        P(both, None),
        P(both),
        P(both),
        P(both, None),
        P(both, None),
        P(both, None),
    )
    return jax.shard_map(local, mesh=mesh, in_specs=in_specs, out_specs=out_specs, check_vma=False)
```

```python
import functools

import jax
import jax.numpy as jnp
from jax import lax
from jax.experimental import pallas as pl
from jax.experimental.pallas import tpu as pltpu
from jax.sharding import PartitionSpec as P


HEADS = 32
HD = 64
ROT = 16
LANES = 128
EPSILON = 1e-05
ROPE_BASE = 10000.0
MASKED = -1e30
BF = jnp.bfloat16
F32 = jnp.float32

DP = "dp"
SEQ = "seq"


def rotary_rows(position):
    lane = jnp.arange(LANES, dtype=jnp.int32) % HD
    half = ROT // 2
    power = ROPE_BASE ** (-(lane % half).astype(F32) * (2.0 / ROT))
    freq = jnp.where(lane < ROT, power, 0.0)
    angle = position.astype(F32)[:, None] * freq[None, :]
    cosine = jnp.cos(angle); sine = jnp.sin(angle)
    first = jnp.where(lane < half, -sine, 0.0)
    second = jnp.where((lane >= half) & (lane < ROT), sine, 0.0)
    return cosine, first, second


def turn(x, cosine, first, second):
    return x * cosine + pltpu.roll(x, LANES - ROT // 2, 1) * first + pltpu.roll(x, ROT // 2, 1) * second


def head_mask(x, h):
    lane = lax.broadcasted_iota(jnp.int32, x.shape, 1)
    return jnp.where((lane >= h * HD) & (lane < (h + 1) * HD), x, jnp.zeros_like(x))


def nt(a, b):
    return lax.dot_general(a, b, (((1,), (1,)), ((), ())), preferred_element_type=F32)


def nn(a, b):
    return lax.dot_general(a, b, (((1,), (0,)), ((), ())), preferred_element_type=F32)


def block_bias(i, j, bq, low_row):
    key = j * bq + lax.broadcasted_iota(jnp.int32, (bq, bq), 0)
    query = i * bq + lax.broadcasted_iota(jnp.int32, (bq, bq), 1)
    return jnp.where((key <= query) & (key >= low_row), 0.0, MASKED)


def fwd_kernel(heads, bq, rows, first_ref, low_ref, cos_ref, s1_ref, s2_ref, x_ref, gain_ref, shift_ref, add_ref, *refs):
    weights = refs[:-7]
    norm_ref, qkv_ref, ctx_ref, lse_ref, k_s, vt_s, st_s = refs[-7:]
    i = pl.program_id(0)
    hc = heads * HD
    x = x_ref[...].astype(F32)
    center = x - jnp.mean(x, axis=-1, keepdims=True)
    factor = lax.rsqrt(jnp.mean(center * center, axis=-1, keepdims=True) + EPSILON)
    normed = (center * factor * gain_ref[...] + shift_ref[...]).astype(BF)
    norm_ref[...] = normed
    proj = add_ref[...]
    size = x_ref.shape[1] // len(weights)
    for n, weight in enumerate(weights):
        part = weight[:, :rows, :].reshape(size, 3 * hc)
        proj = proj + nn(normed[:, n * size:(n + 1) * size], part)
    c, s1, s2 = cos_ref[...], s1_ref[...], s2_ref[...]
    parts = []
    for base in (0, hc):
        for t in range(hc // LANES):
            x = proj[:, base + t * LANES: base + (t + 1) * LANES]
            parts.append(turn(x, c, s1, s2).astype(BF))
    n = hc // LANES
    q = jnp.concatenate(parts[:n], axis=1) if n > 1 else parts[0]
    k = jnp.concatenate(parts[n:], axis=1) if n > 1 else parts[n]
    v32 = proj[:, 2 * hc:]
    v = v32.astype(BF)
    qkv_ref[:, :hc] = q
    qkv_ref[:, hc:2 * hc] = k
    qkv_ref[:, 2 * hc:] = v
    rows = pl.ds(pl.multiple_of(i * bq, bq), bq)
    k_s[rows, :] = k
    vt_s[:, rows] = v32.T.astype(BF)
    low = low_ref[0:1, :]
    qm = [head_mask(q, h) for h in range(heads)]
    first = first_ref[i]

    def score_step(j, tops):
        kj = k_s[pl.ds(pl.multiple_of(j * bq, bq), bq), :]
        bias = block_bias(i, j, bq, low)
        out = []
        for h in range(heads):
            s = nt(kj, qm[h]) * 0.125 + bias
            st_s[h, pl.ds(pl.multiple_of(j * bq, bq), bq), :] = s
            out.append(jnp.maximum(tops[h], jnp.max(s.reshape(bq // 8, 8, bq), axis=0)))
        return tuple(out)

    tops = lax.fori_loop(first, i + 1, score_step,
                         tuple(jnp.full((8, bq), MASKED, F32) for _ in range(heads)))
    tops = [jnp.max(t, axis=0, keepdims=True) for t in tops]

    def value_step(j, state):
        new = []
        vt = vt_s[:, pl.ds(pl.multiple_of(j * bq, bq), bq)]
        for h in range(heads):
            tot, acc = state[h]
            p = jnp.exp(st_s[h, pl.ds(pl.multiple_of(j * bq, bq), bq), :] - tops[h])
            tot = tot + jnp.sum(p.reshape(bq // 8, 8, bq), axis=0)
            acc = acc + nn(vt[h * HD:(h + 1) * HD, :], p.astype(BF))
            new.append((tot, acc))
        return tuple(new)

    state = lax.fori_loop(first, i + 1, value_step,
                          tuple((jnp.zeros((8, bq), F32), jnp.zeros((HD, bq), F32)) for _ in range(heads)))
    outs = []
    lses = []
    for h in range(heads):
        tot, acc = state[h]
        tot = jnp.sum(tot, axis=0, keepdims=True)
        outs.append(acc / tot)
        lses.append(tops[h] + jnp.log(tot))
    ctx_ref[...] = jnp.concatenate(outs, axis=0).T.astype(BF)
    pad = [jnp.zeros((8 - heads, bq), F32)] if heads < 8 else []
    lse_ref[...] = jnp.concatenate(lses + pad, axis=0)


def attend_fwd(x, gain, shift, add, weights, rows, tables, low8, first, heads, bq):
    T, width = x.shape; hc = heads * HD
    row = lambda w: pl.BlockSpec((bq, w), lambda i, f: (i, 0))
    return pl.pallas_call(
        functools.partial(fwd_kernel, heads, bq, rows),
        grid_spec=pltpu.PrefetchScalarGridSpec(
            num_scalar_prefetch=1, grid=(T // bq,),
            in_specs=[pl.BlockSpec((8, bq), lambda i, f: (0, i)), row(LANES), row(LANES), row(LANES), row(width)]
            + [whole(w) for w in (gain, shift, add, *weights)],
            out_specs=[row(width), row(3 * hc), row(hc), pl.BlockSpec((8, bq), lambda i, f: (0, i))],
            scratch_shapes=[pltpu.VMEM((T, hc), BF), pltpu.VMEM((hc, T), BF), pltpu.VMEM((heads, T, bq), F32)]),
        out_shape=[jax.ShapeDtypeStruct((T, width), BF), jax.ShapeDtypeStruct((T, 3 * hc), BF),
                   jax.ShapeDtypeStruct((T, hc), BF), jax.ShapeDtypeStruct((8, T), F32)],
        cost_estimate=pl.CostEstimate(flops=4 * T * T * hc + 6 * T * width * hc, bytes_accessed=T * hc * 24 + 4 * T * width,
                                      transcendentals=T * T * heads // 2),
        name="af",
    )(first, low8, *tables, x, gain, shift, add, *weights)


def bwd_kernel(heads, bq, count, first_ref, low_ref, cos_ref, s1_ref, s2_ref, qkv_ref, ctx_ref, lse_ref, gc_ref,
               gp_ref, bias_ref, dk_s, dv_s, dq_s):
    step = pl.program_id(0)
    i = count - 1 - step
    hc = heads * HD
    rows = pl.ds(pl.multiple_of(i * bq, bq), bq)

    @pl.when(step == 0)
    def _():
        dk_s[...] = jnp.zeros_like(dk_s)
        dv_s[...] = jnp.zeros_like(dv_s)
        bias_ref[...] = jnp.zeros_like(bias_ref)

    low = low_ref[0:1, rows]
    q = qkv_ref[rows, :hc]
    g = gc_ref[rows, :]
    prod = (g.astype(F32) * ctx_ref[rows, :].astype(F32)).T
    deltas = [jnp.sum(prod[h * HD:(h + 1) * HD, :], axis=0, keepdims=True) for h in range(heads)]
    lses = [lse_ref[h:h + 1, rows] for h in range(heads)]
    qm = [head_mask(q, h) for h in range(heads)]
    gm = [head_mask(g, h) for h in range(heads)]
    dq_s[...] = jnp.zeros_like(dq_s)

    @pl.loop(first_ref[i], i + 1)
    def _(j):
        cols = pl.ds(pl.multiple_of(j * bq, bq), bq)
        kj = qkv_ref[cols, hc:2 * hc]
        vj = qkv_ref[cols, 2 * hc:]
        kt = kj.T
        bias = block_bias(i, j, bq, low)
        dk = dk_s[cols, :]
        dv = dv_s[cols, :]
        for h in range(heads):
            s = nt(kj, qm[h]) * 0.125 + bias
            p = jnp.exp(s - lses[h])
            dp = nt(vj, gm[h])
            ds = (p * (dp - deltas[h]) * 0.125).astype(BF)
            dv = dv + nn(p.astype(BF), gm[h])
            dk = dk + nn(ds, qm[h])
            dq_s[h * HD:(h + 1) * HD, :] += nn(kt[h * HD:(h + 1) * HD, :], ds)
        dk_s[cols, :] = dk
        dv_s[cols, :] = dv

    c, s1, s2 = cos_ref[rows, :], s1_ref[rows, :], s2_ref[rows, :]
    dq = dq_s[...].T
    dk = dk_s[rows, :]
    dv = dv_s[rows, :]

    def emit(x, base):
        gp_ref[:, base: base + x.shape[1]] = x.astype(BF)
        bias_ref[:, base: base + x.shape[1]] += jnp.sum(x.reshape(bq // 8, 8, x.shape[1]), axis=0)

    for src, base in ((dq, 0), (dk, hc)):
        for t in range(hc // LANES):
            emit(turn(src[:, t * LANES:(t + 1) * LANES], c, -s1, -s2), base + t * LANES)
    emit(dv, 2 * hc)


def attend_bwd(qkv, ctx, lse, gc, tables, low8, first, heads, bq):
    T = qkv.shape[0]; hc = heads * HD; count = T // bq
    full = lambda r, w: pl.BlockSpec((r, w), lambda i, f: (0, 0))
    return pl.pallas_call(
        functools.partial(bwd_kernel, heads, bq, count),
        grid_spec=pltpu.PrefetchScalarGridSpec(
            num_scalar_prefetch=1, grid=(count,),
            in_specs=[full(8, T), full(T, LANES), full(T, LANES), full(T, LANES), full(T, 3 * hc), full(T, hc), full(8, T), full(T, hc)],
            out_specs=[pl.BlockSpec((bq, 3 * hc), lambda i, f: (count - 1 - i, 0)), full(8, 3 * hc)],
            scratch_shapes=[pltpu.VMEM((T, hc), F32), pltpu.VMEM((T, hc), F32), pltpu.VMEM((hc, bq), F32)]),
        out_shape=[jax.ShapeDtypeStruct((T, 3 * hc), BF), jax.ShapeDtypeStruct((8, 3 * hc), F32)],
        cost_estimate=pl.CostEstimate(flops=5 * T * T * hc * 2, bytes_accessed=T * hc * 24, transcendentals=T * T * heads // 2),
        name="ab",
    )(first, low8, *tables, qkv, ctx, lse, gc)


def relate(values, mine, count, axis):
    size = values.shape[axis] // count
    bit = 1
    while bit < count:
        order = [m ^ bit for m in range(count)]
        swapped = jnp.concatenate(
            [lax.slice_in_dim(values, m * size, (m + 1) * size, axis=axis) for m in order], axis=axis
        )
        values = jnp.where((mine & bit) != 0, swapped, values)
        bit *= 2
    return values


def swap_dp(values, rel):
    return lax.ppermute(values, DP, [(d, d ^ rel) for d in range(lax.axis_size(DP))])


def take(view):
    return lax.all_to_all(view, SEQ, split_axis=0, concat_axis=0, tiled=True)


def spread(mine):
    return [mine] + [swap_dp(mine, rel) for rel in range(1, lax.axis_size(DP))]


def spread_halves(mine):
    half = mine.shape[0] // 2
    count = lax.axis_size(DP)
    bits = [1 << n for n in range(count.bit_length() - 1)]
    low, high = {0: mine[:half]}, {0: mine[half:]}
    for one, other in zip(bits, bits[::-1]):
        low.update({rel ^ one: swap_dp(piece, one) for rel, piece in list(low.items())})
        high.update({rel ^ other: swap_dp(piece, other) for rel, piece in list(high.items())})
    return [(low[rel], high[rel]) for rel in range(count)]


def stack_rows(pieces, start, size):
    cols = pieces[0].shape[2]
    return jnp.concatenate([p[:, start : start + size] for p in pieces], axis=0).reshape(-1, cols)


def reduce_dp(parts):
    total = parts[0].astype(F32)
    moved = [swap_dp(parts[rel], rel) for rel in range(1, len(parts))]
    for piece in moved:
        total = total + piece.astype(F32)
    return total.astype(BF)


def send_back(summed):
    return lax.all_to_all(summed, SEQ, split_axis=0, concat_axis=0, tiled=True)


def ffn_kernel(copies, rows, n_ref, u_ref, *refs):
    pair, down, (act_ref, dx_ref) = refs[:copies], refs[copies : 2 * copies], refs[2 * copies :]
    block = n_ref.shape[1] // copies
    cols = pair[0].shape[2]

    def gate_rows(m):
        return pair[m][:, :rows, :].reshape(block, cols)

    def up_rows(m):
        return pair[m][:, rows:, :].reshape(block, cols)

    gate = upward = grad = 0.0
    for m in range(copies):
        span = slice(m * block, (m + 1) * block)
        gate = gate + nn(n_ref[:, span], gate_rows(m))
        upward = upward + nn(n_ref[:, span], up_rows(m))
        grad = grad + nn(u_ref[:, span], down[m][...].reshape(block, cols))
    sig = jax.nn.sigmoid(gate)
    silu = gate * sig
    grad_gate = (grad * upward * sig * (1.0 + gate * (1.0 - sig))).astype(BF)
    grad_up = (grad * silu).astype(BF)
    act_ref[0] = grad_gate
    act_ref[1] = grad_up
    act_ref[2] = (silu * upward).astype(BF)
    for m in range(copies):
        part = nt(grad_gate, gate_rows(m)) + nt(grad_up, up_rows(m))
        dx_ref[:, m * block : (m + 1) * block] = part.astype(BF)


def whole(array):
    zero = (0,) * array.ndim
    return pl.BlockSpec(array.shape, lambda *i: zero, pipeline_mode=pl.Buffered(1))


def ffn_both(normed, upstream, pair, down, rows, bq):
    length, width = normed.shape
    cols = down[0].shape[2]
    row = pl.BlockSpec((bq, width), lambda i: (i, 0))
    return pl.pallas_call(
        functools.partial(ffn_kernel, len(pair), rows),
        grid=(length // bq,),
        in_specs=[row, row] + [whole(w) for w in pair + down],
        out_specs=[pl.BlockSpec((3, bq, cols), lambda i: (0, i, 0)), row],
        out_shape=[
            jax.ShapeDtypeStruct((3, length, cols), BF),
            jax.ShapeDtypeStruct((length, width), BF),
        ],
        cost_estimate=pl.CostEstimate(
            flops=10 * length * width * cols,
            bytes_accessed=6 * length * width + 6 * width * cols,
            transcendentals=length * cols,
        ),
        name="ffn",
    )(normed, upstream, *pair, *down)


def back_kernel(rows, x_ref, *refs):
    weights, out_ref = refs[:-1], refs[-1]
    cols = weights[0].shape[2]
    size = out_ref.shape[1] // len(weights)
    x = x_ref[...].reshape(out_ref.shape[0], cols)
    for n, weight in enumerate(weights):
        part = weight[:, :rows, :].reshape(size, cols)
        out_ref[:, n * size : (n + 1) * size] = nt(x, part).astype(BF)


def back_rows(x, kind, weights, rows, width, bq):
    _, length, cols = x.shape
    return pl.pallas_call(
        functools.partial(back_kernel, rows),
        grid=(length // bq,),
        in_specs=[pl.BlockSpec((1, bq, cols), lambda i: (kind, i, 0))] + [whole(w) for w in weights],
        out_specs=pl.BlockSpec((bq, width), lambda i: (i, 0)),
        out_shape=jax.ShapeDtypeStruct((length, width), BF),
        cost_estimate=pl.CostEstimate(
            flops=2 * length * width * cols,
            bytes_accessed=2 * length * width + 2 * width * cols,
            transcendentals=0,
        ),
        name="back",
    )(x, *weights)


def grad_kernel(n_ref, u_ref, act_ref, out_ref):
    kind = pl.program_id(0)
    groups, _, rows, cols = out_ref.shape

    def emit(left):
        out_ref[...] = nn(left[...].T, act_ref[0]).astype(BF).reshape(groups, 1, rows, cols)

    @pl.when(kind < 2)
    def _():
        emit(n_ref)

    @pl.when(kind == 2)
    def _():
        emit(u_ref)


def ffn_grads(normed, upstream, act, m, copies, groups):
    length, width = normed.shape
    block = width // copies
    rows = block // groups
    cols = act.shape[2]
    side = pl.BlockSpec((length, block), lambda k: (0, m), pipeline_mode=pl.Buffered(1))
    return pl.pallas_call(
        grad_kernel,
        grid=(3,),
        in_specs=[side, side, pl.BlockSpec((1, length, cols), lambda k: (k, 0, 0))],
        out_specs=pl.BlockSpec((groups, 1, rows, cols), lambda k: (0, k, 0, 0)),
        out_shape=jax.ShapeDtypeStruct((groups, 3, rows, cols), BF),
        cost_estimate=pl.CostEstimate(
            flops=6 * length * block * cols,
            bytes_accessed=4 * length * block + 6 * length * cols + 6 * block * cols,
            transcendentals=0,
        ),
        name="gw",
    )(normed, upstream, act)


def wide_kernel(parts, back_ref, *outs):
    rows = outs[0].shape[0]
    groups = back_ref.shape[0]
    for out, pieces in zip(outs, parts):
        for start, at, cols, base, step in pieces:
            for s in range(groups):
                value = back_ref[s, start : start + rows, at : at + cols]
                out[:, base + s * step : base + s * step + cols] = value.astype(F32)


def widen(back, rows, parts):
    groups = back.shape[0]
    shapes = [jax.ShapeDtypeStruct((rows, groups * sum(p[2] for p in pieces)), F32) for pieces in parts]
    return pl.pallas_call(
        functools.partial(wide_kernel, parts),
        out_shape=shapes,
        cost_estimate=pl.CostEstimate(flops=0, bytes_accessed=3 * back.size * 2, transcendentals=0),
        name="wide",
    )(back)


def unit_of(values):
    center = values - jnp.mean(values, axis=-1, keepdims=True)
    factor = lax.rsqrt(jnp.mean(center * center, axis=-1, keepdims=True) + EPSILON)
    return center * factor, factor


def norm_back(upstream, unit, factor, gain):
    scaled = upstream * gain
    return factor * (
        scaled
        - jnp.mean(scaled, axis=-1, keepdims=True)
        - unit * jnp.mean(scaled * unit, axis=-1, keepdims=True)
    )


def dot(left, right, dims):
    return lax.dot_general(left, right, (dims, ((), ())), preferred_element_type=F32)


NN = ((1,), (0,))
NT = ((1,), (1,))
TN = ((0,), (0,))


def own_rows(partial):
    return lax.psum_scatter(partial.astype(BF), SEQ, scatter_dimension=0, tiled=True).astype(F32)


def every(values):
    return lax.all_gather(values, SEQ, axis=0, tiled=True)


def chip_shift(values, k, groups):
    return lax.ppermute(values, SEQ, [(s, (s + 2 * k) % groups) for s in range(groups)])


def core_swap(values, groups):
    return lax.ppermute(values, SEQ, [(s, s ^ 1) for s in range(groups)])


def place_kernel(spot_ref, *refs):
    out_ref = refs[-1]
    for n, piece in enumerate(refs[:-1]):

        @pl.when(pl.program_id(0) == n)
        def _():
            out_ref[...] = piece[...]


def every_beside(values, me, groups):
    chips = groups // 2
    tokens, width = values.shape
    held = [values] + [chip_shift(values, k, groups) for k in range(1, chips)]
    other = [core_swap(piece, groups) for piece in held]
    steps = jnp.arange(groups, dtype=jnp.int32)
    who = jnp.where(steps < chips, me, me + 1 - 2 * (me % 2))
    spots = (who - 2 * (steps % chips) + groups) % groups
    return pl.pallas_call(
        place_kernel,
        grid_spec=pltpu.PrefetchScalarGridSpec(
            num_scalar_prefetch=1,
            grid=(groups,),
            in_specs=[whole(values)] * groups,
            out_specs=pl.BlockSpec((tokens, width), lambda n, spot: (spot[n], 0)),
        ),
        out_shape=jax.ShapeDtypeStruct((groups * tokens, width), values.dtype),
        cost_estimate=pl.CostEstimate(flops=0, bytes_accessed=4 * groups * tokens * width, transcendentals=0),
        name="place",
    )(spots.astype(jnp.int32), *held, *other)


def own_rows_beside(partial, me, groups):
    chips = groups // 2
    tokens = partial.shape[0] // groups
    blocks = partial.reshape(chips, 2, tokens, partial.shape[1])
    core = me % 2
    theirs = lax.dynamic_index_in_dim(blocks, 1 - core, 1, keepdims=False)
    ours = lax.dynamic_index_in_dim(blocks, core, 1, keepdims=False)
    moved = core_swap(theirs, groups)
    pair = (ours.astype(F32) + moved.astype(F32)).astype(BF)
    chip = me // 2
    moved = [
        chip_shift(lax.dynamic_index_in_dim(pair, (chip + k) % chips, 0, keepdims=False), k, groups)
        for k in range(1, chips)
    ]
    return [lax.dynamic_index_in_dim(pair, chip, 0, keepdims=False)] + moved


def layer(
    inputs,
    position,
    upstream,
    attn_gain,
    attn_shift,
    qkv_weight,
    qkv_bias,
    out_weight,
    ffn_gain,
    ffn_shift,
    gate_weight,
    up_weight,
    down_weight,
):
    tokens, width = inputs.shape
    groups = lax.axis_size(SEQ)
    copies = lax.axis_size(DP)
    me = lax.axis_index(SEQ)
    mine = lax.axis_index(DP)
    length = tokens * groups
    heads = HEADS // groups
    hc = heads * HD
    rows = qkv_weight.shape[0]
    nbias = qkv_bias.shape[0]
    bq = 256

    own = relate(inputs, mine, copies, 1)
    own_up = relate(upstream, mine, copies, 1)

    def by_group(weight, parts=1):
        cols = weight.shape[1] // (parts * groups)
        view = weight.reshape(rows, parts, groups, cols).transpose(2, 0, 1, 3)
        return view.reshape(groups, rows, parts * cols)

    small = jnp.concatenate(
        [
            attn_gain,
            attn_shift,
            ffn_gain,
            ffn_shift,
            qkv_bias,
            (position // 256).astype(BF),
            (position % 256).astype(BF),
        ]
    )
    extra = jnp.zeros((8, 3 * hc), BF).at[0, : small.shape[0]].set(small)
    view_qkv = jnp.concatenate(
        [by_group(qkv_weight, 3), jnp.broadcast_to(extra[None], (groups, 8, 3 * hc))], axis=1
    )
    taken, own = lax.optimization_barrier((take(view_qkv), own))
    x_all = every(own)
    pieces_qkv = [piece for pair in spread_halves(taken) for piece in pair]
    weight_out = stack_rows(spread(take(by_group(out_weight))), 0, rows)
    spot = taken[:, rows, 4 * rows + nbias : 4 * rows + nbias + 2 * tokens]
    positions = (
        spot[:, :tokens].astype(jnp.int32) * 256 + spot[:, tokens:].astype(jnp.int32)
    ).reshape(length)
    everyone = jnp.concatenate([p[:, rows, : 4 * rows + nbias] for p in pieces_qkv]).astype(F32)
    everyone = everyone.reshape(copies, groups, -1)
    gain_one, shift_one, gain_two, shift_two = [
        everyone[:, :, n * rows : (n + 1) * rows].reshape(1, width) for n in range(4)
    ]
    bias_full = relate(everyone[:, :, 4 * rows :].reshape(-1), mine, copies, 0)
    chosen = (jnp.arange(groups, dtype=jnp.int32) == me).astype(F32)
    bias_mine = jnp.sum(bias_full.reshape(3, groups, hc) * chosen[None, :, None], axis=1).reshape(1, -1)

    tables = rotary_rows(positions)
    lowest = jnp.arange(length, dtype=jnp.int32) - positions
    low8 = jnp.broadcast_to(lowest[None], (8, length))
    first = (jnp.min(lowest.reshape(length // bq, bq), axis=1) // bq).astype(jnp.int32)

    view_gu = jnp.concatenate([by_group(gate_weight), by_group(up_weight)], axis=1)
    view_gu, view_down, own_up, x_all = lax.optimization_barrier(
        (view_gu, by_group(down_weight), own_up, x_all)
    )
    up_all = every_beside(own_up, me, groups)
    pieces_gu = spread(take(view_gu))
    pieces_down = spread(take(view_down))

    normed_one, qkv, context, lse = attend_fwd(
        x_all, gain_one, shift_one, bias_mine, pieces_qkv, rows, tables, low8, first, heads, bq
    )
    flat = own.astype(F32)
    middle = flat + own_rows(dot(context, weight_out, NT))
    unit_two, factor_two = unit_of(middle)
    normed_two = (unit_two * gain_two + shift_two).astype(BF)
    normed_two = every(normed_two)
    act, dx = ffn_both(normed_two, up_all, pieces_gu, pieces_down, rows, bq)
    grad_normed_two = own_rows(dx)
    down_part = back_rows(act, 2, pieces_down, rows, width, bq)
    block = width // copies

    def by_owner(left, right):
        return [
            dot(left[:, m * block : (m + 1) * block], right, TN).astype(BF).reshape(groups, rows, -1)
            for m in range(copies)
        ]

    grads = [None] * copies
    for m in [*range(1, copies), 0]:
        grads[m] = ffn_grads(normed_two, up_all, act, m, copies, groups)
    sum_ffn = reduce_dp(grads).reshape(groups, 3 * rows, -1)
    sum_ffn = send_back(sum_ffn)

    down_sum = own_rows_beside(down_part, me, groups)
    grad_middle = own_up.astype(F32) + norm_back(grad_normed_two, unit_two, factor_two, gain_two)
    grad_mixed = grad_middle.astype(BF)
    grad_mixed = every(grad_mixed)
    grad_context = dot(grad_mixed, weight_out, NN).astype(BF)
    grad_projected, bias_part = attend_bwd(qkv, context, lse, grad_context, tables, low8, first, heads, bq)
    dqkv = back_rows(grad_projected[None], 0, pieces_qkv, rows, width, bq)
    grad_normed_one = own_rows(dqkv)

    late, unused = lax.optimization_barrier((down_sum[0], bias_part))
    total = late.astype(F32)
    for piece in down_sum[1:]:
        total = total + piece.astype(F32)
    output = (middle + total).astype(BF)

    grad_qkv_weight = by_owner(normed_one, grad_projected)
    x_late, unused = lax.optimization_barrier((x_all, grad_qkv_weight[0]))
    unit_all, unused = unit_of(x_late.astype(F32))
    bias_part = jnp.sum(bias_part, axis=0).reshape(3, 1, hc) * chosen[None, :, None]
    bias_part = relate(bias_part.reshape(-1), mine, copies, 0).reshape(copies, groups, nbias)
    parts = [
        jnp.sum(dqkv.astype(F32) * unit_all, axis=0),
        jnp.sum(dqkv.astype(F32), axis=0),
        jnp.sum(grad_normed_two * unit_two, axis=0),
        jnp.sum(grad_normed_two, axis=0),
    ]
    parts = [p.reshape(copies, groups, 1, rows) for p in parts] + [bias_part[:, :, None]]
    parts = jnp.concatenate(parts, axis=3)
    parts = jnp.pad(parts, ((0, 0), (0, 0), (0, 0), (0, 8 * hc - parts.shape[3]))).astype(BF)
    parts = parts.reshape(copies, groups, 8, hc)

    sum_qkv = reduce_dp(grad_qkv_weight)
    grad_out_weight = by_owner(grad_mixed, context)
    sum_out = reduce_dp([jnp.concatenate([grad_out_weight[m], parts[m]], axis=1) for m in range(copies)])
    sum_attn = jnp.concatenate([jnp.pad(sum_qkv, ((0, 0), (0, 8), (0, 0))), sum_out], axis=2)
    sum_attn = send_back(sum_attn)
    total = jnp.sum(sum_attn[:, rows:, 3 * hc :].astype(F32), axis=0).reshape(-1)
    sums = [total[n * rows : (n + 1) * rows] for n in range(4)] + [total[4 * rows : 4 * rows + nbias]]
    wide_qkv, wide_out = widen(
        sum_attn,
        rows,
        (tuple((0, n * hc, hc, n * width, hc) for n in range(3)), ((0, 3 * hc, hc, 0, hc),)),
    )
    unit_one, factor_one = unit_of(flat)
    grad_input = grad_middle + norm_back(grad_normed_one, unit_one, factor_one, gain_one)

    cols = sum_ffn.shape[2]
    wide_gate, wide_up, wide_down = widen(
        sum_ffn, rows, tuple(((n * rows, 0, cols, 0, cols),) for n in range(3))
    )
    return (
        relate(output, mine, copies, 1)[None],
        relate(grad_input, mine, copies, 1)[None],
        sums[0],
        sums[1],
        wide_qkv,
        sums[4],
        wide_out,
        sums[2],
        sums[3],
        wide_gate,
        wide_up,
        wide_down,
    )


def local(
    residual_in,
    attn_gain,
    attn_shift,
    qkv_weight,
    qkv_bias,
    out_weight,
    ffn_gain,
    ffn_shift,
    gate_weight,
    up_weight,
    down_weight,
    positions,
    cotangent,
):
    return layer(
        residual_in[0],
        positions[0],
        cotangent[0],
        attn_gain,
        attn_shift,
        qkv_weight,
        qkv_bias,
        out_weight,
        ffn_gain,
        ffn_shift,
        gate_weight,
        up_weight,
        down_weight,
    )


def solution(mesh):
    both = (DP, SEQ)
    in_specs = (
        P(DP, SEQ, None),
        P(both),
        P(both),
        P(both, None),
        P(both),
        P(both, None),
        P(both),
        P(both),
        P(both, None),
        P(both, None),
        P(both, None),
        P(DP, SEQ),
        P(DP, SEQ, None),
    )
    out_specs = (
        P(DP, SEQ, None),
        P(DP, SEQ, None),
        P(both),
        P(both),
        P(both, None),
        P(both),
        P(both, None),
        P(both),
        P(both),
        P(both, None),
        P(both, None),
        P(both, None),
    )
    return jax.shard_map(local, mesh=mesh, in_specs=in_specs, out_specs=out_specs, check_vma=False)
```

```python
import functools

import jax
import jax.numpy as jnp
from jax import lax
from jax.experimental import pallas as pl
from jax.experimental.pallas import tpu as pltpu
from jax.sharding import PartitionSpec as P


HEADS = 32
HD = 64
ROT = 16
LANES = 128
EPSILON = 1e-05
ROPE_BASE = 10000.0
MASKED = -1e30
BF = jnp.bfloat16
F32 = jnp.float32

DP = "dp"
SEQ = "seq"


def rotary_rows(position):
    lane = jnp.arange(LANES, dtype=jnp.int32) % HD
    half = ROT // 2
    power = ROPE_BASE ** (-(lane % half).astype(F32) * (2.0 / ROT))
    freq = jnp.where(lane < ROT, power, 0.0)
    angle = position.astype(F32)[:, None] * freq[None, :]
    cosine = jnp.cos(angle); sine = jnp.sin(angle)
    first = jnp.where(lane < half, -sine, 0.0)
    second = jnp.where((lane >= half) & (lane < ROT), sine, 0.0)
    return cosine, first, second


def turn(x, cosine, first, second):
    return x * cosine + pltpu.roll(x, LANES - ROT // 2, 1) * first + pltpu.roll(x, ROT // 2, 1) * second


def head_mask(x, h):
    lane = lax.broadcasted_iota(jnp.int32, x.shape, 1)
    return jnp.where((lane >= h * HD) & (lane < (h + 1) * HD), x, jnp.zeros_like(x))


def nt(a, b):
    return lax.dot_general(a, b, (((1,), (1,)), ((), ())), preferred_element_type=F32)


def nn(a, b):
    return lax.dot_general(a, b, (((1,), (0,)), ((), ())), preferred_element_type=F32)


def block_bias(i, j, bq, low_row):
    key = j * bq + lax.broadcasted_iota(jnp.int32, (bq, bq), 0)
    query = i * bq + lax.broadcasted_iota(jnp.int32, (bq, bq), 1)
    return jnp.where((key <= query) & (key >= low_row), 0.0, MASKED)


def fwd_kernel(heads, bq, rows, first_ref, low_ref, cos_ref, s1_ref, s2_ref, x_ref, gain_ref, shift_ref, add_ref, *refs):
    weights = refs[:-7]
    norm_ref, qkv_ref, ctx_ref, lse_ref, k_s, vt_s, st_s = refs[-7:]
    i = pl.program_id(0)
    hc = heads * HD
    x = x_ref[...].astype(F32)
    center = x - jnp.mean(x, axis=-1, keepdims=True)
    factor = lax.rsqrt(jnp.mean(center * center, axis=-1, keepdims=True) + EPSILON)
    normed = (center * factor * gain_ref[...] + shift_ref[...]).astype(BF)
    norm_ref[...] = normed
    proj = add_ref[...]
    size = x_ref.shape[1] // len(weights)
    for n, weight in enumerate(weights):
        part = weight[:, :rows, :].reshape(size, 3 * hc)
        proj = proj + nn(normed[:, n * size:(n + 1) * size], part)
    c, s1, s2 = cos_ref[...], s1_ref[...], s2_ref[...]
    parts = []
    for base in (0, hc):
        for t in range(hc // LANES):
            x = proj[:, base + t * LANES: base + (t + 1) * LANES]
            parts.append(turn(x, c, s1, s2).astype(BF))
    n = hc // LANES
    q = jnp.concatenate(parts[:n], axis=1) if n > 1 else parts[0]
    k = jnp.concatenate(parts[n:], axis=1) if n > 1 else parts[n]
    v32 = proj[:, 2 * hc:]
    v = v32.astype(BF)
    qkv_ref[:, :hc] = q
    qkv_ref[:, hc:2 * hc] = k
    qkv_ref[:, 2 * hc:] = v
    rows = pl.ds(pl.multiple_of(i * bq, bq), bq)
    k_s[rows, :] = k
    vt_s[:, rows] = v32.T.astype(BF)
    low = low_ref[0:1, :]
    qm = [head_mask(q, h) for h in range(heads)]
    first = first_ref[i]

    def score_step(j, tops):
        kj = k_s[pl.ds(pl.multiple_of(j * bq, bq), bq), :]
        bias = block_bias(i, j, bq, low)
        out = []
        for h in range(heads):
            s = nt(kj, qm[h]) * 0.125 + bias
            st_s[h, pl.ds(pl.multiple_of(j * bq, bq), bq), :] = s
            out.append(jnp.maximum(tops[h], jnp.max(s.reshape(bq // 8, 8, bq), axis=0)))
        return tuple(out)

    tops = lax.fori_loop(first, i + 1, score_step,
                         tuple(jnp.full((8, bq), MASKED, F32) for _ in range(heads)))
    tops = [jnp.max(t, axis=0, keepdims=True) for t in tops]

    def value_step(j, state):
        new = []
        vt = vt_s[:, pl.ds(pl.multiple_of(j * bq, bq), bq)]
        for h in range(heads):
            tot, acc = state[h]
            p = jnp.exp(st_s[h, pl.ds(pl.multiple_of(j * bq, bq), bq), :] - tops[h])
            tot = tot + jnp.sum(p.reshape(bq // 8, 8, bq), axis=0)
            acc = acc + nn(vt[h * HD:(h + 1) * HD, :], p.astype(BF))
            new.append((tot, acc))
        return tuple(new)

    state = lax.fori_loop(first, i + 1, value_step,
                          tuple((jnp.zeros((8, bq), F32), jnp.zeros((HD, bq), F32)) for _ in range(heads)))
    outs = []
    lses = []
    for h in range(heads):
        tot, acc = state[h]
        tot = jnp.sum(tot, axis=0, keepdims=True)
        outs.append(acc / tot)
        lses.append(tops[h] + jnp.log(tot))
    ctx_ref[...] = jnp.concatenate(outs, axis=0).T.astype(BF)
    pad = [jnp.zeros((8 - heads, bq), F32)] if heads < 8 else []
    lse_ref[...] = jnp.concatenate(lses + pad, axis=0)


def attend_fwd(x, gain, shift, add, weights, rows, tables, low8, first, heads, bq):
    T, width = x.shape; hc = heads * HD
    row = lambda w: pl.BlockSpec((bq, w), lambda i, f: (i, 0))
    return pl.pallas_call(
        functools.partial(fwd_kernel, heads, bq, rows),
        grid_spec=pltpu.PrefetchScalarGridSpec(
            num_scalar_prefetch=1, grid=(T // bq,),
            in_specs=[pl.BlockSpec((8, bq), lambda i, f: (0, i)), row(LANES), row(LANES), row(LANES), row(width)]
            + [whole(w) for w in (gain, shift, add, *weights)],
            out_specs=[row(width), row(3 * hc), row(hc), pl.BlockSpec((8, bq), lambda i, f: (0, i))],
            scratch_shapes=[pltpu.VMEM((T, hc), BF), pltpu.VMEM((hc, T), BF), pltpu.VMEM((heads, T, bq), F32)]),
        out_shape=[jax.ShapeDtypeStruct((T, width), BF), jax.ShapeDtypeStruct((T, 3 * hc), BF),
                   jax.ShapeDtypeStruct((T, hc), BF), jax.ShapeDtypeStruct((8, T), F32)],
        cost_estimate=pl.CostEstimate(flops=4 * T * T * hc + 6 * T * width * hc, bytes_accessed=T * hc * 24 + 4 * T * width,
                                      transcendentals=T * T * heads // 2),
        name="af",
    )(first, low8, *tables, x, gain, shift, add, *weights)


def bwd_kernel(heads, bq, count, first_ref, low_ref, cos_ref, s1_ref, s2_ref, qkv_ref, ctx_ref, lse_ref, gc_ref,
               gp_ref, bias_ref, dk_s, dv_s, dq_s):
    step = pl.program_id(0)
    i = count - 1 - step
    hc = heads * HD
    rows = pl.ds(pl.multiple_of(i * bq, bq), bq)

    @pl.when(step == 0)
    def _():
        dk_s[...] = jnp.zeros_like(dk_s)
        dv_s[...] = jnp.zeros_like(dv_s)
        bias_ref[...] = jnp.zeros_like(bias_ref)

    low = low_ref[0:1, rows]
    q = qkv_ref[rows, :hc]
    g = gc_ref[rows, :]
    prod = (g.astype(F32) * ctx_ref[rows, :].astype(F32)).T
    deltas = [jnp.sum(prod[h * HD:(h + 1) * HD, :], axis=0, keepdims=True) for h in range(heads)]
    lses = [lse_ref[h:h + 1, rows] for h in range(heads)]
    qm = [head_mask(q, h) for h in range(heads)]
    gm = [head_mask(g, h) for h in range(heads)]
    dq_s[...] = jnp.zeros_like(dq_s)

    @pl.loop(first_ref[i], i + 1)
    def _(j):
        cols = pl.ds(pl.multiple_of(j * bq, bq), bq)
        kj = qkv_ref[cols, hc:2 * hc]
        vj = qkv_ref[cols, 2 * hc:]
        kt = kj.T
        bias = block_bias(i, j, bq, low)
        dk = dk_s[cols, :]
        dv = dv_s[cols, :]
        for h in range(heads):
            s = nt(kj, qm[h]) * 0.125 + bias
            p = jnp.exp(s - lses[h])
            dp = nt(vj, gm[h])
            ds = (p * (dp - deltas[h]) * 0.125).astype(BF)
            dv = dv + nn(p.astype(BF), gm[h])
            dk = dk + nn(ds, qm[h])
            dq_s[h * HD:(h + 1) * HD, :] += nn(kt[h * HD:(h + 1) * HD, :], ds)
        dk_s[cols, :] = dk
        dv_s[cols, :] = dv

    c, s1, s2 = cos_ref[rows, :], s1_ref[rows, :], s2_ref[rows, :]
    dq = dq_s[...].T
    dk = dk_s[rows, :]
    dv = dv_s[rows, :]

    def emit(x, base):
        gp_ref[:, base: base + x.shape[1]] = x.astype(BF)
        bias_ref[:, base: base + x.shape[1]] += jnp.sum(x.reshape(bq // 8, 8, x.shape[1]), axis=0)

    for src, base in ((dq, 0), (dk, hc)):
        for t in range(hc // LANES):
            emit(turn(src[:, t * LANES:(t + 1) * LANES], c, -s1, -s2), base + t * LANES)
    emit(dv, 2 * hc)


def attend_bwd(qkv, ctx, lse, gc, tables, low8, first, heads, bq):
    T = qkv.shape[0]; hc = heads * HD; count = T // bq
    full = lambda r, w: pl.BlockSpec((r, w), lambda i, f: (0, 0))
    return pl.pallas_call(
        functools.partial(bwd_kernel, heads, bq, count),
        grid_spec=pltpu.PrefetchScalarGridSpec(
            num_scalar_prefetch=1, grid=(count,),
            in_specs=[full(8, T), full(T, LANES), full(T, LANES), full(T, LANES), full(T, 3 * hc), full(T, hc), full(8, T), full(T, hc)],
            out_specs=[pl.BlockSpec((bq, 3 * hc), lambda i, f: (count - 1 - i, 0)), full(8, 3 * hc)],
            scratch_shapes=[pltpu.VMEM((T, hc), F32), pltpu.VMEM((T, hc), F32), pltpu.VMEM((hc, bq), F32)]),
        out_shape=[jax.ShapeDtypeStruct((T, 3 * hc), BF), jax.ShapeDtypeStruct((8, 3 * hc), F32)],
        cost_estimate=pl.CostEstimate(flops=5 * T * T * hc * 2, bytes_accessed=T * hc * 24, transcendentals=T * T * heads // 2),
        name="ab",
    )(first, low8, *tables, qkv, ctx, lse, gc)


def relate(values, mine, count, axis):
    size = values.shape[axis] // count
    bit = 1
    while bit < count:
        order = [m ^ bit for m in range(count)]
        swapped = jnp.concatenate(
            [lax.slice_in_dim(values, m * size, (m + 1) * size, axis=axis) for m in order], axis=axis
        )
        values = jnp.where((mine & bit) != 0, swapped, values)
        bit *= 2
    return values


def swap_dp(values, rel):
    return lax.ppermute(values, DP, [(d, d ^ rel) for d in range(lax.axis_size(DP))])


def take(view):
    return lax.all_to_all(view, SEQ, split_axis=0, concat_axis=0, tiled=True)


def spread(mine):
    return [mine] + [swap_dp(mine, rel) for rel in range(1, lax.axis_size(DP))]


def spread_halves(mine):
    half = mine.shape[0] // 2
    count = lax.axis_size(DP)
    bits = [1 << n for n in range(count.bit_length() - 1)]
    low, high = {0: mine[:half]}, {0: mine[half:]}
    for one, other in zip(bits, bits[::-1]):
        low.update({rel ^ one: swap_dp(piece, one) for rel, piece in list(low.items())})
        high.update({rel ^ other: swap_dp(piece, other) for rel, piece in list(high.items())})
    return [(low[rel], high[rel]) for rel in range(count)]


def stack_rows(pieces, start, size):
    cols = pieces[0].shape[2]
    return jnp.concatenate([p[:, start : start + size] for p in pieces], axis=0).reshape(-1, cols)


def reduce_dp(parts):
    total = parts[0].astype(F32)
    moved = [swap_dp(parts[rel], rel) for rel in range(1, len(parts))]
    for piece in moved:
        total = total + piece.astype(F32)
    return total.astype(BF)


def send_back(summed):
    return lax.all_to_all(summed, SEQ, split_axis=0, concat_axis=0, tiled=True)


def ffn_kernel(copies, rows, n_ref, u_ref, *refs):
    pair, down, (act_ref, dx_ref) = refs[:copies], refs[copies : 2 * copies], refs[2 * copies :]
    block = n_ref.shape[1] // copies
    cols = pair[0].shape[2]

    def gate_rows(m):
        return pair[m][:, :rows, :].reshape(block, cols)

    def up_rows(m):
        return pair[m][:, rows:, :].reshape(block, cols)

    gate = upward = grad = 0.0
    for m in range(copies):
        span = slice(m * block, (m + 1) * block)
        gate = gate + nn(n_ref[:, span], gate_rows(m))
        upward = upward + nn(n_ref[:, span], up_rows(m))
        grad = grad + nn(u_ref[:, span], down[m][...].reshape(block, cols))
    sig = jax.nn.sigmoid(gate)
    silu = gate * sig
    grad_gate = (grad * upward * sig * (1.0 + gate * (1.0 - sig))).astype(BF)
    grad_up = (grad * silu).astype(BF)
    act_ref[0] = grad_gate
    act_ref[1] = grad_up
    act_ref[2] = (silu * upward).astype(BF)
    for m in range(copies):
        part = nt(grad_gate, gate_rows(m)) + nt(grad_up, up_rows(m))
        dx_ref[:, m * block : (m + 1) * block] = part.astype(BF)


def whole(array):
    zero = (0,) * array.ndim
    return pl.BlockSpec(array.shape, lambda *i: zero, pipeline_mode=pl.Buffered(1))


def ffn_both(normed, upstream, pair, down, rows, bq):
    length, width = normed.shape
    cols = down[0].shape[2]
    row = pl.BlockSpec((bq, width), lambda i: (i, 0))
    return pl.pallas_call(
        functools.partial(ffn_kernel, len(pair), rows),
        grid=(length // bq,),
        in_specs=[row, row] + [whole(w) for w in pair + down],
        out_specs=[pl.BlockSpec((3, bq, cols), lambda i: (0, i, 0)), row],
        out_shape=[
            jax.ShapeDtypeStruct((3, length, cols), BF),
            jax.ShapeDtypeStruct((length, width), BF),
        ],
        cost_estimate=pl.CostEstimate(
            flops=10 * length * width * cols,
            bytes_accessed=6 * length * width + 6 * width * cols,
            transcendentals=length * cols,
        ),
        name="ffn",
    )(normed, upstream, *pair, *down)


def back_kernel(rows, x_ref, *refs):
    weights, out_ref = refs[:-1], refs[-1]
    cols = weights[0].shape[2]
    size = out_ref.shape[1] // len(weights)
    x = x_ref[...].reshape(out_ref.shape[0], cols)
    for n, weight in enumerate(weights):
        part = weight[:, :rows, :].reshape(size, cols)
        out_ref[:, n * size : (n + 1) * size] = nt(x, part).astype(BF)


def back_rows(x, kind, weights, rows, width, bq):
    _, length, cols = x.shape
    return pl.pallas_call(
        functools.partial(back_kernel, rows),
        grid=(length // bq,),
        in_specs=[pl.BlockSpec((1, bq, cols), lambda i: (kind, i, 0))] + [whole(w) for w in weights],
        out_specs=pl.BlockSpec((bq, width), lambda i: (i, 0)),
        out_shape=jax.ShapeDtypeStruct((length, width), BF),
        cost_estimate=pl.CostEstimate(
            flops=2 * length * width * cols,
            bytes_accessed=2 * length * width + 2 * width * cols,
            transcendentals=0,
        ),
        name="back",
    )(x, *weights)


def grad_kernel(n_ref, u_ref, act_ref, out_ref):
    kind = pl.program_id(0)
    groups, _, rows, cols = out_ref.shape

    def emit(left):
        out_ref[...] = nn(left[...].T, act_ref[0]).astype(BF).reshape(groups, 1, rows, cols)

    @pl.when(kind < 2)
    def _():
        emit(n_ref)

    @pl.when(kind == 2)
    def _():
        emit(u_ref)


def ffn_grads(normed, upstream, act, m, copies, groups):
    length, width = normed.shape
    block = width // copies
    rows = block // groups
    cols = act.shape[2]
    side = pl.BlockSpec((length, block), lambda k: (0, m), pipeline_mode=pl.Buffered(1))
    return pl.pallas_call(
        grad_kernel,
        grid=(3,),
        in_specs=[side, side, pl.BlockSpec((1, length, cols), lambda k: (k, 0, 0))],
        out_specs=pl.BlockSpec((groups, 1, rows, cols), lambda k: (0, k, 0, 0)),
        out_shape=jax.ShapeDtypeStruct((groups, 3, rows, cols), BF),
        cost_estimate=pl.CostEstimate(
            flops=6 * length * block * cols,
            bytes_accessed=4 * length * block + 6 * length * cols + 6 * block * cols,
            transcendentals=0,
        ),
        name="gw",
    )(normed, upstream, act)


def wide_kernel(parts, back_ref, *outs):
    rows = outs[0].shape[0]
    groups = back_ref.shape[0]
    for out, pieces in zip(outs, parts):
        for start, at, cols, base, step in pieces:
            for s in range(groups):
                value = back_ref[s, start : start + rows, at : at + cols]
                out[:, base + s * step : base + s * step + cols] = value.astype(F32)


def widen(back, rows, parts):
    groups = back.shape[0]
    shapes = [jax.ShapeDtypeStruct((rows, groups * sum(p[2] for p in pieces)), F32) for pieces in parts]
    return pl.pallas_call(
        functools.partial(wide_kernel, parts),
        out_shape=shapes,
        cost_estimate=pl.CostEstimate(flops=0, bytes_accessed=3 * back.size * 2, transcendentals=0),
        name="wide",
    )(back)


def unit_of(values):
    center = values - jnp.mean(values, axis=-1, keepdims=True)
    factor = lax.rsqrt(jnp.mean(center * center, axis=-1, keepdims=True) + EPSILON)
    return center * factor, factor


def norm_back(upstream, unit, factor, gain):
    scaled = upstream * gain
    return factor * (
        scaled
        - jnp.mean(scaled, axis=-1, keepdims=True)
        - unit * jnp.mean(scaled * unit, axis=-1, keepdims=True)
    )


def dot(left, right, dims):
    return lax.dot_general(left, right, (dims, ((), ())), preferred_element_type=F32)


NN = ((1,), (0,))
NT = ((1,), (1,))
TN = ((0,), (0,))


def own_rows(partial):
    return lax.psum_scatter(partial.astype(BF), SEQ, scatter_dimension=0, tiled=True).astype(F32)


def every(values):
    return lax.all_gather(values, SEQ, axis=0, tiled=True)


def chip_shift(values, k, groups):
    return lax.ppermute(values, SEQ, [(s, (s + 2 * k) % groups) for s in range(groups)])


def core_swap(values, groups):
    return lax.ppermute(values, SEQ, [(s, s ^ 1) for s in range(groups)])


def place_kernel(spot_ref, *refs):
    out_ref = refs[-1]
    for n, piece in enumerate(refs[:-1]):

        @pl.when(pl.program_id(0) == n)
        def _():
            out_ref[...] = piece[...]


def every_beside(values, me, groups):
    chips = groups // 2
    tokens, width = values.shape
    held = [values] + [chip_shift(values, k, groups) for k in range(1, chips)]
    other = [core_swap(piece, groups) for piece in held]
    steps = jnp.arange(groups, dtype=jnp.int32)
    who = jnp.where(steps < chips, me, me + 1 - 2 * (me % 2))
    spots = (who - 2 * (steps % chips) + groups) % groups
    return pl.pallas_call(
        place_kernel,
        grid_spec=pltpu.PrefetchScalarGridSpec(
            num_scalar_prefetch=1,
            grid=(groups,),
            in_specs=[whole(values)] * groups,
            out_specs=pl.BlockSpec((tokens, width), lambda n, spot: (spot[n], 0)),
        ),
        out_shape=jax.ShapeDtypeStruct((groups * tokens, width), values.dtype),
        cost_estimate=pl.CostEstimate(flops=0, bytes_accessed=4 * groups * tokens * width, transcendentals=0),
        name="place",
    )(spots.astype(jnp.int32), *held, *other)


def own_rows_beside(partial, me, groups, after):
    chips = groups // 2
    tokens = partial.shape[0] // groups
    blocks = partial.reshape(chips, 2, tokens, partial.shape[1])
    core = me % 2
    theirs = lax.dynamic_index_in_dim(blocks, 1 - core, 1, keepdims=False)
    ours = lax.dynamic_index_in_dim(blocks, core, 1, keepdims=False)
    moved = core_swap(theirs, groups)
    pair = (ours.astype(F32) + moved.astype(F32)).astype(BF)
    pair, _ = lax.optimization_barrier((pair, after))
    chip = me // 2
    moved = [
        chip_shift(lax.dynamic_index_in_dim(pair, (chip + k) % chips, 0, keepdims=False), k, groups)
        for k in range(1, chips)
    ]
    return [lax.dynamic_index_in_dim(pair, chip, 0, keepdims=False)] + moved


def layer(
    inputs,
    position,
    upstream,
    attn_gain,
    attn_shift,
    qkv_weight,
    qkv_bias,
    out_weight,
    ffn_gain,
    ffn_shift,
    gate_weight,
    up_weight,
    down_weight,
):
    tokens, width = inputs.shape
    groups = lax.axis_size(SEQ)
    copies = lax.axis_size(DP)
    me = lax.axis_index(SEQ)
    mine = lax.axis_index(DP)
    length = tokens * groups
    heads = HEADS // groups
    hc = heads * HD
    rows = qkv_weight.shape[0]
    nbias = qkv_bias.shape[0]
    bq = 256

    own = relate(inputs, mine, copies, 1)
    own_up = relate(upstream, mine, copies, 1)

    def by_group(weight, parts=1):
        cols = weight.shape[1] // (parts * groups)
        view = weight.reshape(rows, parts, groups, cols).transpose(2, 0, 1, 3)
        return view.reshape(groups, rows, parts * cols)

    small = jnp.concatenate(
        [
            attn_gain,
            attn_shift,
            ffn_gain,
            ffn_shift,
            qkv_bias,
            (position // 256).astype(BF),
            (position % 256).astype(BF),
        ]
    )
    extra = jnp.zeros((8, 3 * hc), BF).at[0, : small.shape[0]].set(small)
    view_qkv = jnp.concatenate(
        [by_group(qkv_weight, 3), jnp.broadcast_to(extra[None], (groups, 8, 3 * hc))], axis=1
    )
    taken, own = lax.optimization_barrier((take(view_qkv), own))
    x_all = every(own)
    pieces_qkv = [piece for pair in spread_halves(taken) for piece in pair]
    weight_out = stack_rows(spread(take(by_group(out_weight))), 0, rows)
    spot = taken[:, rows, 4 * rows + nbias : 4 * rows + nbias + 2 * tokens]
    positions = (
        spot[:, :tokens].astype(jnp.int32) * 256 + spot[:, tokens:].astype(jnp.int32)
    ).reshape(length)
    everyone = jnp.concatenate([p[:, rows, : 4 * rows + nbias] for p in pieces_qkv]).astype(F32)
    everyone = everyone.reshape(copies, groups, -1)
    gain_one, shift_one, gain_two, shift_two = [
        everyone[:, :, n * rows : (n + 1) * rows].reshape(1, width) for n in range(4)
    ]
    bias_full = relate(everyone[:, :, 4 * rows :].reshape(-1), mine, copies, 0)
    chosen = (jnp.arange(groups, dtype=jnp.int32) == me).astype(F32)
    bias_mine = jnp.sum(bias_full.reshape(3, groups, hc) * chosen[None, :, None], axis=1).reshape(1, -1)

    tables = rotary_rows(positions)
    lowest = jnp.arange(length, dtype=jnp.int32) - positions
    low8 = jnp.broadcast_to(lowest[None], (8, length))
    first = (jnp.min(lowest.reshape(length // bq, bq), axis=1) // bq).astype(jnp.int32)

    view_gu = jnp.concatenate([by_group(gate_weight), by_group(up_weight)], axis=1)
    view_down, x_all = lax.optimization_barrier((by_group(down_weight), x_all))
    taken_gu = take(view_gu)
    up_sent, unused = lax.optimization_barrier((own_up, taken_gu))
    up_all = every_beside(up_sent, me, groups)
    pieces_gu = spread(taken_gu)
    pieces_down = spread(take(view_down))

    normed_one, qkv, context, lse = attend_fwd(
        x_all, gain_one, shift_one, bias_mine, pieces_qkv, rows, tables, low8, first, heads, bq
    )
    flat = own.astype(F32)
    middle = flat + own_rows(dot(context, weight_out, NT))
    unit_two, factor_two = unit_of(middle)
    normed_two = (unit_two * gain_two + shift_two).astype(BF)
    normed_two = every(normed_two)
    act, dx = ffn_both(normed_two, up_all, pieces_gu, pieces_down, rows, bq)
    grad_normed_two = own_rows(dx)
    down_part = back_rows(act, 2, pieces_down, rows, width, bq)
    block = width // copies

    def by_owner(left, right):
        return [
            dot(left[:, m * block : (m + 1) * block], right, TN).astype(BF).reshape(groups, rows, -1)
            for m in range(copies)
        ]

    grads = [None] * copies
    for m in [*range(1, copies), 0]:
        grads[m] = ffn_grads(normed_two, up_all, act, m, copies, groups)
    sum_ffn = reduce_dp(grads).reshape(groups, 3 * rows, -1)
    sum_ffn = send_back(sum_ffn)

    grad_middle = own_up.astype(F32) + norm_back(grad_normed_two, unit_two, factor_two, gain_two)
    grad_mixed = grad_middle.astype(BF)
    grad_mixed = every(grad_mixed)
    down_sum = own_rows_beside(down_part, me, groups, grad_mixed)
    grad_context = dot(grad_mixed, weight_out, NN).astype(BF)
    grad_projected, bias_part = attend_bwd(qkv, context, lse, grad_context, tables, low8, first, heads, bq)
    dqkv = back_rows(grad_projected[None], 0, pieces_qkv, rows, width, bq)
    grad_normed_one = own_rows(dqkv)

    late, unused = lax.optimization_barrier((down_sum[0], bias_part))
    total = late.astype(F32)
    for piece in down_sum[1:]:
        total = total + piece.astype(F32)
    output = (middle + total).astype(BF)

    grad_qkv_weight = by_owner(normed_one, grad_projected)
    x_late, unused = lax.optimization_barrier((x_all, grad_qkv_weight[0]))
    unit_all, unused = unit_of(x_late.astype(F32))
    bias_part = jnp.sum(bias_part, axis=0).reshape(3, 1, hc) * chosen[None, :, None]
    bias_part = relate(bias_part.reshape(-1), mine, copies, 0).reshape(copies, groups, nbias)
    parts = [
        jnp.sum(dqkv.astype(F32) * unit_all, axis=0),
        jnp.sum(dqkv.astype(F32), axis=0),
        jnp.sum(grad_normed_two * unit_two, axis=0),
        jnp.sum(grad_normed_two, axis=0),
    ]
    parts = [p.reshape(copies, groups, 1, rows) for p in parts] + [bias_part[:, :, None]]
    parts = jnp.concatenate(parts, axis=3)
    parts = jnp.pad(parts, ((0, 0), (0, 0), (0, 0), (0, 8 * hc - parts.shape[3]))).astype(BF)
    parts = parts.reshape(copies, groups, 8, hc)

    sum_qkv = reduce_dp(grad_qkv_weight)
    grad_out_weight = by_owner(grad_mixed, context)
    sum_out = reduce_dp([jnp.concatenate([grad_out_weight[m], parts[m]], axis=1) for m in range(copies)])
    sum_attn = jnp.concatenate([jnp.pad(sum_qkv, ((0, 0), (0, 8), (0, 0))), sum_out], axis=2)
    sum_attn = send_back(sum_attn)
    total = jnp.sum(sum_attn[:, rows:, 3 * hc :].astype(F32), axis=0).reshape(-1)
    sums = [total[n * rows : (n + 1) * rows] for n in range(4)] + [total[4 * rows : 4 * rows + nbias]]
    wide_qkv, wide_out = widen(
        sum_attn,
        rows,
        (tuple((0, n * hc, hc, n * width, hc) for n in range(3)), ((0, 3 * hc, hc, 0, hc),)),
    )
    unit_one, factor_one = unit_of(flat)
    grad_input = grad_middle + norm_back(grad_normed_one, unit_one, factor_one, gain_one)

    cols = sum_ffn.shape[2]
    wide_gate, wide_up, wide_down = widen(
        sum_ffn, rows, tuple(((n * rows, 0, cols, 0, cols),) for n in range(3))
    )
    return (
        relate(output, mine, copies, 1)[None],
        relate(grad_input, mine, copies, 1)[None],
        sums[0],
        sums[1],
        wide_qkv,
        sums[4],
        wide_out,
        sums[2],
        sums[3],
        wide_gate,
        wide_up,
        wide_down,
    )


def local(
    residual_in,
    attn_gain,
    attn_shift,
    qkv_weight,
    qkv_bias,
    out_weight,
    ffn_gain,
    ffn_shift,
    gate_weight,
    up_weight,
    down_weight,
    positions,
    cotangent,
):
    return layer(
        residual_in[0],
        positions[0],
        cotangent[0],
        attn_gain,
        attn_shift,
        qkv_weight,
        qkv_bias,
        out_weight,
        ffn_gain,
        ffn_shift,
        gate_weight,
        up_weight,
        down_weight,
    )


def solution(mesh):
    both = (DP, SEQ)
    in_specs = (
        P(DP, SEQ, None),
        P(both),
        P(both),
        P(both, None),
        P(both),
        P(both, None),
        P(both),
        P(both),
        P(both, None),
        P(both, None),
        P(both, None),
        P(DP, SEQ),
        P(DP, SEQ, None),
    )
    out_specs = (
        P(DP, SEQ, None),
        P(DP, SEQ, None),
        P(both),
        P(both),
        P(both, None),
        P(both),
        P(both, None),
        P(both),
        P(both),
        P(both, None),
        P(both, None),
        P(both, None),
    )
    return jax.shard_map(local, mesh=mesh, in_specs=in_specs, out_specs=out_specs, check_vma=False)
```

```python
import functools

import jax
import jax.numpy as jnp
from jax import lax
from jax.experimental import pallas as pl
from jax.experimental.pallas import tpu as pltpu
from jax.sharding import PartitionSpec as P


HEADS = 32
HD = 64
ROT = 16
LANES = 128
EPSILON = 1e-05
ROPE_BASE = 10000.0
MASKED = -1e30
BF = jnp.bfloat16
F32 = jnp.float32

DP = "dp"
SEQ = "seq"


def rotary_rows(position):
    lane = jnp.arange(LANES, dtype=jnp.int32) % HD
    half = ROT // 2
    power = ROPE_BASE ** (-(lane % half).astype(F32) * (2.0 / ROT))
    freq = jnp.where(lane < ROT, power, 0.0)
    angle = position.astype(F32)[:, None] * freq[None, :]
    cosine = jnp.cos(angle); sine = jnp.sin(angle)
    first = jnp.where(lane < half, -sine, 0.0)
    second = jnp.where((lane >= half) & (lane < ROT), sine, 0.0)
    return cosine, first, second


def turn(x, cosine, first, second):
    return x * cosine + pltpu.roll(x, LANES - ROT // 2, 1) * first + pltpu.roll(x, ROT // 2, 1) * second


def head_mask(x, h):
    lane = lax.broadcasted_iota(jnp.int32, x.shape, 1)
    return jnp.where((lane >= h * HD) & (lane < (h + 1) * HD), x, jnp.zeros_like(x))


def nt(a, b):
    return lax.dot_general(a, b, (((1,), (1,)), ((), ())), preferred_element_type=F32)


def nn(a, b):
    return lax.dot_general(a, b, (((1,), (0,)), ((), ())), preferred_element_type=F32)


def block_bias(i, j, bq, low_row):
    key = j * bq + lax.broadcasted_iota(jnp.int32, (bq, bq), 0)
    query = i * bq + lax.broadcasted_iota(jnp.int32, (bq, bq), 1)
    return jnp.where((key <= query) & (key >= low_row), 0.0, MASKED)


def fwd_kernel(heads, bq, rows, first_ref, low_ref, cos_ref, s1_ref, s2_ref, x_ref, gain_ref, shift_ref, add_ref, *refs):
    weights = refs[:-7]
    norm_ref, qkv_ref, ctx_ref, lse_ref, k_s, vt_s, st_s = refs[-7:]
    i = pl.program_id(0)
    hc = heads * HD
    x = x_ref[...].astype(F32)
    center = x - jnp.mean(x, axis=-1, keepdims=True)
    factor = lax.rsqrt(jnp.mean(center * center, axis=-1, keepdims=True) + EPSILON)
    normed = (center * factor * gain_ref[...] + shift_ref[...]).astype(BF)
    norm_ref[...] = normed
    proj = add_ref[...]
    size = x_ref.shape[1] // len(weights)
    for n, weight in enumerate(weights):
        part = weight[:, :rows, :].reshape(size, 3 * hc)
        proj = proj + nn(normed[:, n * size:(n + 1) * size], part)
    c, s1, s2 = cos_ref[...], s1_ref[...], s2_ref[...]
    parts = []
    for base in (0, hc):
        for t in range(hc // LANES):
            x = proj[:, base + t * LANES: base + (t + 1) * LANES]
            parts.append(turn(x, c, s1, s2).astype(BF))
    n = hc // LANES
    q = jnp.concatenate(parts[:n], axis=1) if n > 1 else parts[0]
    k = jnp.concatenate(parts[n:], axis=1) if n > 1 else parts[n]
    v32 = proj[:, 2 * hc:]
    v = v32.astype(BF)
    qkv_ref[:, :hc] = q
    qkv_ref[:, hc:2 * hc] = k
    qkv_ref[:, 2 * hc:] = v
    rows = pl.ds(pl.multiple_of(i * bq, bq), bq)
    k_s[rows, :] = k
    vt_s[:, rows] = v32.T.astype(BF)
    low = low_ref[0:1, :]
    qm = [head_mask(q, h) for h in range(heads)]
    first = first_ref[i]

    def score_step(j, tops):
        kj = k_s[pl.ds(pl.multiple_of(j * bq, bq), bq), :]
        bias = block_bias(i, j, bq, low)
        out = []
        for h in range(heads):
            s = nt(kj, qm[h]) * 0.125 + bias
            st_s[h, pl.ds(pl.multiple_of(j * bq, bq), bq), :] = s
            out.append(jnp.maximum(tops[h], jnp.max(s.reshape(bq // 8, 8, bq), axis=0)))
        return tuple(out)

    tops = lax.fori_loop(first, i + 1, score_step,
                         tuple(jnp.full((8, bq), MASKED, F32) for _ in range(heads)))
    tops = [jnp.max(t, axis=0, keepdims=True) for t in tops]

    def value_step(j, state):
        new = []
        vt = vt_s[:, pl.ds(pl.multiple_of(j * bq, bq), bq)]
        for h in range(heads):
            tot, acc = state[h]
            p = jnp.exp(st_s[h, pl.ds(pl.multiple_of(j * bq, bq), bq), :] - tops[h])
            tot = tot + jnp.sum(p.reshape(bq // 8, 8, bq), axis=0)
            acc = acc + nn(vt[h * HD:(h + 1) * HD, :], p.astype(BF))
            new.append((tot, acc))
        return tuple(new)

    state = lax.fori_loop(first, i + 1, value_step,
                          tuple((jnp.zeros((8, bq), F32), jnp.zeros((HD, bq), F32)) for _ in range(heads)))
    outs = []
    lses = []
    for h in range(heads):
        tot, acc = state[h]
        tot = jnp.sum(tot, axis=0, keepdims=True)
        outs.append(acc / tot)
        lses.append(tops[h] + jnp.log(tot))
    ctx_ref[...] = jnp.concatenate(outs, axis=0).T.astype(BF)
    pad = [jnp.zeros((8 - heads, bq), F32)] if heads < 8 else []
    lse_ref[...] = jnp.concatenate(lses + pad, axis=0)


def attend_fwd(x, gain, shift, add, weights, rows, tables, low8, first, heads, bq):
    T, width = x.shape; hc = heads * HD
    row = lambda w: pl.BlockSpec((bq, w), lambda i, f: (i, 0))
    return pl.pallas_call(
        functools.partial(fwd_kernel, heads, bq, rows),
        grid_spec=pltpu.PrefetchScalarGridSpec(
            num_scalar_prefetch=1, grid=(T // bq,),
            in_specs=[pl.BlockSpec((8, bq), lambda i, f: (0, i)), row(LANES), row(LANES), row(LANES), row(width)]
            + [whole(w) for w in (gain, shift, add, *weights)],
            out_specs=[row(width), row(3 * hc), row(hc), pl.BlockSpec((8, bq), lambda i, f: (0, i))],
            scratch_shapes=[pltpu.VMEM((T, hc), BF), pltpu.VMEM((hc, T), BF), pltpu.VMEM((heads, T, bq), F32)]),
        out_shape=[jax.ShapeDtypeStruct((T, width), BF), jax.ShapeDtypeStruct((T, 3 * hc), BF),
                   jax.ShapeDtypeStruct((T, hc), BF), jax.ShapeDtypeStruct((8, T), F32)],
        cost_estimate=pl.CostEstimate(flops=4 * T * T * hc + 6 * T * width * hc, bytes_accessed=T * hc * 24 + 4 * T * width,
                                      transcendentals=T * T * heads // 2),
        name="af",
    )(first, low8, *tables, x, gain, shift, add, *weights)


def bwd_kernel(heads, bq, count, first_ref, low_ref, cos_ref, s1_ref, s2_ref, qkv_ref, ctx_ref, lse_ref, gc_ref,
               gp_ref, bias_ref, dk_s, dv_s, dq_s):
    step = pl.program_id(0)
    i = count - 1 - step
    hc = heads * HD
    rows = pl.ds(pl.multiple_of(i * bq, bq), bq)

    @pl.when(step == 0)
    def _():
        dk_s[...] = jnp.zeros_like(dk_s)
        dv_s[...] = jnp.zeros_like(dv_s)
        bias_ref[...] = jnp.zeros_like(bias_ref)

    low = low_ref[0:1, rows]
    q = qkv_ref[rows, :hc]
    g = gc_ref[rows, :]
    prod = (g.astype(F32) * ctx_ref[rows, :].astype(F32)).T
    deltas = [jnp.sum(prod[h * HD:(h + 1) * HD, :], axis=0, keepdims=True) for h in range(heads)]
    lses = [lse_ref[h:h + 1, rows] for h in range(heads)]
    qm = [head_mask(q, h) for h in range(heads)]
    gm = [head_mask(g, h) for h in range(heads)]
    dq_s[...] = jnp.zeros_like(dq_s)

    @pl.loop(first_ref[i], i + 1)
    def _(j):
        cols = pl.ds(pl.multiple_of(j * bq, bq), bq)
        kj = qkv_ref[cols, hc:2 * hc]
        vj = qkv_ref[cols, 2 * hc:]
        kt = kj.T
        bias = block_bias(i, j, bq, low)
        dk = dk_s[cols, :]
        dv = dv_s[cols, :]
        for h in range(heads):
            s = nt(kj, qm[h]) * 0.125 + bias
            p = jnp.exp(s - lses[h])
            dp = nt(vj, gm[h])
            ds = (p * (dp - deltas[h]) * 0.125).astype(BF)
            dv = dv + nn(p.astype(BF), gm[h])
            dk = dk + nn(ds, qm[h])
            dq_s[h * HD:(h + 1) * HD, :] += nn(kt[h * HD:(h + 1) * HD, :], ds)
        dk_s[cols, :] = dk
        dv_s[cols, :] = dv

    c, s1, s2 = cos_ref[rows, :], s1_ref[rows, :], s2_ref[rows, :]
    dq = dq_s[...].T
    dk = dk_s[rows, :]
    dv = dv_s[rows, :]

    def emit(x, base):
        gp_ref[:, base: base + x.shape[1]] = x.astype(BF)
        bias_ref[:, base: base + x.shape[1]] += jnp.sum(x.reshape(bq // 8, 8, x.shape[1]), axis=0)

    for src, base in ((dq, 0), (dk, hc)):
        for t in range(hc // LANES):
            emit(turn(src[:, t * LANES:(t + 1) * LANES], c, -s1, -s2), base + t * LANES)
    emit(dv, 2 * hc)


def attend_bwd(qkv, ctx, lse, gc, tables, low8, first, heads, bq):
    T = qkv.shape[0]; hc = heads * HD; count = T // bq
    full = lambda r, w: pl.BlockSpec((r, w), lambda i, f: (0, 0))
    return pl.pallas_call(
        functools.partial(bwd_kernel, heads, bq, count),
        grid_spec=pltpu.PrefetchScalarGridSpec(
            num_scalar_prefetch=1, grid=(count,),
            in_specs=[full(8, T), full(T, LANES), full(T, LANES), full(T, LANES), full(T, 3 * hc), full(T, hc), full(8, T), full(T, hc)],
            out_specs=[pl.BlockSpec((bq, 3 * hc), lambda i, f: (count - 1 - i, 0)), full(8, 3 * hc)],
            scratch_shapes=[pltpu.VMEM((T, hc), F32), pltpu.VMEM((T, hc), F32), pltpu.VMEM((hc, bq), F32)]),
        out_shape=[jax.ShapeDtypeStruct((T, 3 * hc), BF), jax.ShapeDtypeStruct((8, 3 * hc), F32)],
        cost_estimate=pl.CostEstimate(flops=5 * T * T * hc * 2, bytes_accessed=T * hc * 24, transcendentals=T * T * heads // 2),
        name="ab",
    )(first, low8, *tables, qkv, ctx, lse, gc)


def relate(values, mine, count, axis):
    size = values.shape[axis] // count
    bit = 1
    while bit < count:
        order = [m ^ bit for m in range(count)]
        swapped = jnp.concatenate(
            [lax.slice_in_dim(values, m * size, (m + 1) * size, axis=axis) for m in order], axis=axis
        )
        values = jnp.where((mine & bit) != 0, swapped, values)
        bit *= 2
    return values


def swap_dp(values, rel):
    return lax.ppermute(values, DP, [(d, d ^ rel) for d in range(lax.axis_size(DP))])


def take(view):
    return lax.all_to_all(view, SEQ, split_axis=0, concat_axis=0, tiled=True)


def spread(mine):
    return [mine] + [swap_dp(mine, rel) for rel in range(1, lax.axis_size(DP))]


def spread_halves(mine):
    half = mine.shape[0] // 2
    count = lax.axis_size(DP)
    bits = [1 << n for n in range(count.bit_length() - 1)]
    low, high = {0: mine[:half]}, {0: mine[half:]}
    for one, other in zip(bits, bits[::-1]):
        low.update({rel ^ one: swap_dp(piece, one) for rel, piece in list(low.items())})
        high.update({rel ^ other: swap_dp(piece, other) for rel, piece in list(high.items())})
    return [(low[rel], high[rel]) for rel in range(count)]


def stack_rows(pieces, start, size):
    cols = pieces[0].shape[2]
    return jnp.concatenate([p[:, start : start + size] for p in pieces], axis=0).reshape(-1, cols)


def reduce_dp(parts):
    total = parts[0].astype(F32)
    moved = [swap_dp(parts[rel], rel) for rel in range(1, len(parts))]
    for piece in moved:
        total = total + piece.astype(F32)
    return total.astype(BF)


def send_back(summed):
    return lax.all_to_all(summed, SEQ, split_axis=0, concat_axis=0, tiled=True)


def ffn_kernel(copies, rows, n_ref, u_ref, *refs):
    pair, down, (act_ref, dx_ref) = refs[:copies], refs[copies : 2 * copies], refs[2 * copies :]
    block = n_ref.shape[1] // copies
    cols = pair[0].shape[2]

    def gate_rows(m):
        return pair[m][:, :rows, :].reshape(block, cols)

    def up_rows(m):
        return pair[m][:, rows:, :].reshape(block, cols)

    gate = upward = grad = 0.0
    for m in range(copies):
        span = slice(m * block, (m + 1) * block)
        gate = gate + nn(n_ref[:, span], gate_rows(m))
        upward = upward + nn(n_ref[:, span], up_rows(m))
        grad = grad + nn(u_ref[:, span], down[m][...].reshape(block, cols))
    sig = jax.nn.sigmoid(gate)
    silu = gate * sig
    grad_gate = (grad * upward * sig * (1.0 + gate * (1.0 - sig))).astype(BF)
    grad_up = (grad * silu).astype(BF)
    act_ref[0] = grad_gate
    act_ref[1] = grad_up
    act_ref[2] = (silu * upward).astype(BF)
    for m in range(copies):
        part = nt(grad_gate, gate_rows(m)) + nt(grad_up, up_rows(m))
        dx_ref[:, m * block : (m + 1) * block] = part.astype(BF)


def whole(array):
    zero = (0,) * array.ndim
    return pl.BlockSpec(array.shape, lambda *i: zero, pipeline_mode=pl.Buffered(1))


def ffn_both(normed, upstream, pair, down, rows, bq):
    length, width = normed.shape
    cols = down[0].shape[2]
    row = pl.BlockSpec((bq, width), lambda i: (i, 0))
    return pl.pallas_call(
        functools.partial(ffn_kernel, len(pair), rows),
        grid=(length // bq,),
        in_specs=[row, row] + [whole(w) for w in pair + down],
        out_specs=[pl.BlockSpec((3, bq, cols), lambda i: (0, i, 0)), row],
        out_shape=[
            jax.ShapeDtypeStruct((3, length, cols), BF),
            jax.ShapeDtypeStruct((length, width), BF),
        ],
        cost_estimate=pl.CostEstimate(
            flops=10 * length * width * cols,
            bytes_accessed=6 * length * width + 6 * width * cols,
            transcendentals=length * cols,
        ),
        name="ffn",
    )(normed, upstream, *pair, *down)


def back_kernel(rows, x_ref, *refs):
    weights, out_ref = refs[:-1], refs[-1]
    cols = weights[0].shape[2]
    size = out_ref.shape[1] // len(weights)
    x = x_ref[...].reshape(out_ref.shape[0], cols)
    for n, weight in enumerate(weights):
        part = weight[:, :rows, :].reshape(size, cols)
        out_ref[:, n * size : (n + 1) * size] = nt(x, part).astype(BF)


def back_rows(x, kind, weights, rows, width, bq):
    _, length, cols = x.shape
    return pl.pallas_call(
        functools.partial(back_kernel, rows),
        grid=(length // bq,),
        in_specs=[pl.BlockSpec((1, bq, cols), lambda i: (kind, i, 0))] + [whole(w) for w in weights],
        out_specs=pl.BlockSpec((bq, width), lambda i: (i, 0)),
        out_shape=jax.ShapeDtypeStruct((length, width), BF),
        cost_estimate=pl.CostEstimate(
            flops=2 * length * width * cols,
            bytes_accessed=2 * length * width + 2 * width * cols,
            transcendentals=0,
        ),
        name="back",
    )(x, *weights)


def grad_kernel(n_ref, u_ref, act_ref, out_ref):
    kind = pl.program_id(0)
    groups, _, rows, cols = out_ref.shape

    def emit(left):
        out_ref[...] = nn(left[...].T, act_ref[0]).astype(BF).reshape(groups, 1, rows, cols)

    @pl.when(kind < 2)
    def _():
        emit(n_ref)

    @pl.when(kind == 2)
    def _():
        emit(u_ref)


def ffn_grads(normed, upstream, act, m, copies, groups):
    length, width = normed.shape
    block = width // copies
    rows = block // groups
    cols = act.shape[2]
    side = pl.BlockSpec((length, block), lambda k: (0, m), pipeline_mode=pl.Buffered(1))
    return pl.pallas_call(
        grad_kernel,
        grid=(3,),
        in_specs=[side, side, pl.BlockSpec((1, length, cols), lambda k: (k, 0, 0))],
        out_specs=pl.BlockSpec((groups, 1, rows, cols), lambda k: (0, k, 0, 0)),
        out_shape=jax.ShapeDtypeStruct((groups, 3, rows, cols), BF),
        cost_estimate=pl.CostEstimate(
            flops=6 * length * block * cols,
            bytes_accessed=4 * length * block + 6 * length * cols + 6 * block * cols,
            transcendentals=0,
        ),
        name="gw",
    )(normed, upstream, act)


def wide_kernel(parts, back_ref, *outs):
    rows = outs[0].shape[0]
    groups = back_ref.shape[0]
    for out, pieces in zip(outs, parts):
        for start, at, cols, base, step in pieces:
            for s in range(groups):
                value = back_ref[s, start : start + rows, at : at + cols]
                out[:, base + s * step : base + s * step + cols] = value.astype(F32)


def widen(back, rows, parts):
    groups = back.shape[0]
    shapes = [jax.ShapeDtypeStruct((rows, groups * sum(p[2] for p in pieces)), F32) for pieces in parts]
    return pl.pallas_call(
        functools.partial(wide_kernel, parts),
        out_shape=shapes,
        cost_estimate=pl.CostEstimate(flops=0, bytes_accessed=3 * back.size * 2, transcendentals=0),
        name="wide",
    )(back)


def unit_of(values):
    center = values - jnp.mean(values, axis=-1, keepdims=True)
    factor = lax.rsqrt(jnp.mean(center * center, axis=-1, keepdims=True) + EPSILON)
    return center * factor, factor


def norm_back(upstream, unit, factor, gain):
    scaled = upstream * gain
    return factor * (
        scaled
        - jnp.mean(scaled, axis=-1, keepdims=True)
        - unit * jnp.mean(scaled * unit, axis=-1, keepdims=True)
    )


def dot(left, right, dims):
    return lax.dot_general(left, right, (dims, ((), ())), preferred_element_type=F32)


NN = ((1,), (0,))
NT = ((1,), (1,))
TN = ((0,), (0,))


def own_rows(partial):
    return lax.psum_scatter(partial.astype(BF), SEQ, scatter_dimension=0, tiled=True).astype(F32)


def every(values):
    return lax.all_gather(values, SEQ, axis=0, tiled=True)


def chip_shift(values, k, groups):
    return lax.ppermute(values, SEQ, [(s, (s + 2 * k) % groups) for s in range(groups)])


def core_swap(values, groups):
    return lax.ppermute(values, SEQ, [(s, s ^ 1) for s in range(groups)])


def own_rows_beside(partial, me, groups, after):
    chips = groups // 2
    tokens = partial.shape[0] // groups
    blocks = partial.reshape(chips, 2, tokens, partial.shape[1])
    core = me % 2
    theirs = lax.dynamic_index_in_dim(blocks, 1 - core, 1, keepdims=False)
    ours = lax.dynamic_index_in_dim(blocks, core, 1, keepdims=False)
    moved = core_swap(theirs, groups)
    pair = (ours.astype(F32) + moved.astype(F32)).astype(BF)
    pair, _ = lax.optimization_barrier((pair, after))
    chip = me // 2
    moved = [
        chip_shift(lax.dynamic_index_in_dim(pair, (chip + k) % chips, 0, keepdims=False), k, groups)
        for k in range(1, chips)
    ]
    return [lax.dynamic_index_in_dim(pair, chip, 0, keepdims=False)] + moved


def layer(
    inputs,
    position,
    upstream,
    attn_gain,
    attn_shift,
    qkv_weight,
    qkv_bias,
    out_weight,
    ffn_gain,
    ffn_shift,
    gate_weight,
    up_weight,
    down_weight,
):
    tokens, width = inputs.shape
    groups = lax.axis_size(SEQ)
    copies = lax.axis_size(DP)
    me = lax.axis_index(SEQ)
    mine = lax.axis_index(DP)
    length = tokens * groups
    heads = HEADS // groups
    hc = heads * HD
    rows = qkv_weight.shape[0]
    nbias = qkv_bias.shape[0]
    bq = 256

    own = relate(inputs, mine, copies, 1)
    own_up = relate(upstream, mine, copies, 1)
    up_all = every(own_up)

    def by_group(weight, parts=1):
        cols = weight.shape[1] // (parts * groups)
        view = weight.reshape(rows, parts, groups, cols).transpose(2, 0, 1, 3)
        return view.reshape(groups, rows, parts * cols)

    small = jnp.concatenate(
        [
            attn_gain,
            attn_shift,
            ffn_gain,
            ffn_shift,
            qkv_bias,
            (position // 256).astype(BF),
            (position % 256).astype(BF),
        ]
    )
    extra = jnp.zeros((8, 3 * hc), BF).at[0, : small.shape[0]].set(small)
    view_qkv = jnp.concatenate(
        [by_group(qkv_weight, 3), jnp.broadcast_to(extra[None], (groups, 8, 3 * hc))], axis=1
    )
    taken, own = lax.optimization_barrier((take(view_qkv), own))
    x_all = every(own)
    pieces_qkv = [piece for pair in spread_halves(taken) for piece in pair]
    weight_out = stack_rows(spread(take(by_group(out_weight))), 0, rows)
    spot = taken[:, rows, 4 * rows + nbias : 4 * rows + nbias + 2 * tokens]
    positions = (
        spot[:, :tokens].astype(jnp.int32) * 256 + spot[:, tokens:].astype(jnp.int32)
    ).reshape(length)
    everyone = jnp.concatenate([p[:, rows, : 4 * rows + nbias] for p in pieces_qkv]).astype(F32)
    everyone = everyone.reshape(copies, groups, -1)
    gain_one, shift_one, gain_two, shift_two = [
        everyone[:, :, n * rows : (n + 1) * rows].reshape(1, width) for n in range(4)
    ]
    bias_full = relate(everyone[:, :, 4 * rows :].reshape(-1), mine, copies, 0)
    chosen = (jnp.arange(groups, dtype=jnp.int32) == me).astype(F32)
    bias_mine = jnp.sum(bias_full.reshape(3, groups, hc) * chosen[None, :, None], axis=1).reshape(1, -1)

    tables = rotary_rows(positions)
    lowest = jnp.arange(length, dtype=jnp.int32) - positions
    low8 = jnp.broadcast_to(lowest[None], (8, length))
    first = (jnp.min(lowest.reshape(length // bq, bq), axis=1) // bq).astype(jnp.int32)

    view_gu = jnp.concatenate([by_group(gate_weight), by_group(up_weight)], axis=1)
    view_gu, view_down, x_all = lax.optimization_barrier((view_gu, by_group(down_weight), x_all))
    pieces_gu = spread(take(view_gu))
    pieces_down = spread(take(view_down))

    normed_one, qkv, context, lse = attend_fwd(
        x_all, gain_one, shift_one, bias_mine, pieces_qkv, rows, tables, low8, first, heads, bq
    )
    flat = own.astype(F32)
    middle = flat + own_rows(dot(context, weight_out, NT))
    unit_two, factor_two = unit_of(middle)
    normed_two = (unit_two * gain_two + shift_two).astype(BF)
    normed_two = every(normed_two)
    act, dx = ffn_both(normed_two, up_all, pieces_gu, pieces_down, rows, bq)
    grad_normed_two = own_rows(dx)
    down_part = back_rows(act, 2, pieces_down, rows, width, bq)
    block = width // copies

    def by_owner(left, right):
        return [
            dot(left[:, m * block : (m + 1) * block], right, TN).astype(BF).reshape(groups, rows, -1)
            for m in range(copies)
        ]

    grads = [None] * copies
    for m in [*range(1, copies), 0]:
        grads[m] = ffn_grads(normed_two, up_all, act, m, copies, groups)
    sum_ffn = reduce_dp(grads).reshape(groups, 3 * rows, -1)
    sum_ffn = send_back(sum_ffn)

    grad_middle = own_up.astype(F32) + norm_back(grad_normed_two, unit_two, factor_two, gain_two)
    grad_mixed = grad_middle.astype(BF)
    grad_mixed = every(grad_mixed)
    down_sum = own_rows_beside(down_part, me, groups, grad_mixed)
    grad_context = dot(grad_mixed, weight_out, NN).astype(BF)
    grad_projected, bias_part = attend_bwd(qkv, context, lse, grad_context, tables, low8, first, heads, bq)
    dqkv = back_rows(grad_projected[None], 0, pieces_qkv, rows, width, bq)
    grad_normed_one = own_rows(dqkv)

    late, unused = lax.optimization_barrier((down_sum[0], bias_part))
    total = late.astype(F32)
    for piece in down_sum[1:]:
        total = total + piece.astype(F32)
    output = (middle + total).astype(BF)

    grad_qkv_weight = by_owner(normed_one, grad_projected)
    x_late, unused = lax.optimization_barrier((x_all, grad_qkv_weight[0]))
    unit_all, unused = unit_of(x_late.astype(F32))
    bias_part = jnp.sum(bias_part, axis=0).reshape(3, 1, hc) * chosen[None, :, None]
    bias_part = relate(bias_part.reshape(-1), mine, copies, 0).reshape(copies, groups, nbias)
    parts = [
        jnp.sum(dqkv.astype(F32) * unit_all, axis=0),
        jnp.sum(dqkv.astype(F32), axis=0),
        jnp.sum(grad_normed_two * unit_two, axis=0),
        jnp.sum(grad_normed_two, axis=0),
    ]
    parts = [p.reshape(copies, groups, 1, rows) for p in parts] + [bias_part[:, :, None]]
    parts = jnp.concatenate(parts, axis=3)
    parts = jnp.pad(parts, ((0, 0), (0, 0), (0, 0), (0, 8 * hc - parts.shape[3]))).astype(BF)
    parts = parts.reshape(copies, groups, 8, hc)

    sum_qkv = reduce_dp(grad_qkv_weight)
    grad_out_weight = by_owner(grad_mixed, context)
    sum_out = reduce_dp([jnp.concatenate([grad_out_weight[m], parts[m]], axis=1) for m in range(copies)])
    sum_attn = jnp.concatenate([jnp.pad(sum_qkv, ((0, 0), (0, 8), (0, 0))), sum_out], axis=2)
    sum_attn = send_back(sum_attn)
    total = jnp.sum(sum_attn[:, rows:, 3 * hc :].astype(F32), axis=0).reshape(-1)
    sums = [total[n * rows : (n + 1) * rows] for n in range(4)] + [total[4 * rows : 4 * rows + nbias]]
    wide_qkv, wide_out = widen(
        sum_attn,
        rows,
        (tuple((0, n * hc, hc, n * width, hc) for n in range(3)), ((0, 3 * hc, hc, 0, hc),)),
    )
    unit_one, factor_one = unit_of(flat)
    grad_input = grad_middle + norm_back(grad_normed_one, unit_one, factor_one, gain_one)

    cols = sum_ffn.shape[2]
    wide_gate, wide_up, wide_down = widen(
        sum_ffn, rows, tuple(((n * rows, 0, cols, 0, cols),) for n in range(3))
    )
    return (
        relate(output, mine, copies, 1)[None],
        relate(grad_input, mine, copies, 1)[None],
        sums[0],
        sums[1],
        wide_qkv,
        sums[4],
        wide_out,
        sums[2],
        sums[3],
        wide_gate,
        wide_up,
        wide_down,
    )


def local(
    residual_in,
    attn_gain,
    attn_shift,
    qkv_weight,
    qkv_bias,
    out_weight,
    ffn_gain,
    ffn_shift,
    gate_weight,
    up_weight,
    down_weight,
    positions,
    cotangent,
):
    return layer(
        residual_in[0],
        positions[0],
        cotangent[0],
        attn_gain,
        attn_shift,
        qkv_weight,
        qkv_bias,
        out_weight,
        ffn_gain,
        ffn_shift,
        gate_weight,
        up_weight,
        down_weight,
    )


def solution(mesh):
    both = (DP, SEQ)
    in_specs = (
        P(DP, SEQ, None),
        P(both),
        P(both),
        P(both, None),
        P(both),
        P(both, None),
        P(both),
        P(both),
        P(both, None),
        P(both, None),
        P(both, None),
        P(DP, SEQ),
        P(DP, SEQ, None),
    )
    out_specs = (
        P(DP, SEQ, None),
        P(DP, SEQ, None),
        P(both),
        P(both),
        P(both, None),
        P(both),
        P(both, None),
        P(both),
        P(both),
        P(both, None),
        P(both, None),
        P(both, None),
    )
    return jax.shard_map(local, mesh=mesh, in_specs=in_specs, out_specs=out_specs, check_vma=False)
```
